32 devices in a mesh: pole: 4 (over x, core), grid: 8 (over z, y).
Axes of the slice: x: 2, y: 2, z: 4, core: 2. Of those that a mesh axis runs over, the one named last changes fastest.
Arguments:
- anc_inv: bfloat16 [4, 1536, 1536], P('pole', 'grid'), may hold values from -6 to 6
- factor_cols: bfloat16 [4, 8, 2, 256, 256], P('pole', 'grid'), may hold values from -0.25 to 0.25
- diag_inv: bfloat16 [4, 8, 256, 256], P('pole', 'grid'), may hold values from -6 to 6
- intersection: bfloat16 [8, 256, 256], P('grid'), may hold values from -0.0234375 to 0.0234375
- pole_w: float32 [4], P('pole'), may hold values from 0.5 to 2
- pole_z: float32 [4], P('pole'), may hold values from -2 to -0.5
- ancestors: int32 [8, 2], P('grid'), may hold values from 0 to 5, as said below
- counts: int32 [8], P('grid'), may hold values from 1 to 2
- hpattern: int32 [8, 2], P('grid'), may hold values 0 or 1
- siesta_of: int32 [2048], P('grid'), may hold values from 0 to 2047, as said below
- supernode_of: int32 [2048], P('grid'), may hold values from 0 to 2047, as said below
Outputs:
- density: bfloat16 [2048, 768], P('grid', 'pole')
- energy: bfloat16 [2048, 768], P('grid', 'pole')
- electrons: float32 [], replicated
The draws below stay inside these ranges and needn't reach their ends.
Inputs may be any that keep to these rules, and one draw needn't show every extreme that they name: `ancestors`: the 2 entries of a row are distinct. `siesta_of`: A permutation; supernode K's 256 orbitals go to each block-column owner (index // 256) at most 32 times, and exactly 32 times to some owner. `supernode_of`: the inverse permutation of siesta_of.
All inputs are finite; a program needn't handle non-finite values. No bound on the sum of `hpattern` on one device may be relied on, other than what follows from the above.
Results may differ from the reference program's by a relative error of at most 0.001.
Values may be sent and summed in bfloat16 or wider, within the bound.
No kernel may reach another device: no remote copies, remote signals or barrier semaphores. Data moves between devices by JAX's collectives and lax.ppermute only.
A program may use at most 64 MiB of HBM per device.

```python
import jax
import jax.numpy as jnp
from jax import lax

W = 256
NA = 6
M = 2
POLES = 4
NCOL = 8
NORB = 2048


def siesta_table(key):
    key_source, key_owner = jax.random.split(jax.random.fold_in(key, 7), 2)
    source_dev = jnp.arange(NCOL, dtype=jnp.int32)[:, None]
    local_pos = jnp.arange(W, dtype=jnp.int32)[None, :]
    owner_dev = (source_dev + local_pos * NCOL // W) % NCOL
    source_perm = jax.vmap(lambda sub_key: jax.random.permutation(sub_key, W))(jax.random.split(key_source, NCOL)).astype(jnp.int32)
    owner_perm = jax.vmap(lambda sub_key: jax.random.permutation(sub_key, W))(jax.random.split(key_owner, NCOL)).astype(jnp.int32)
    local_full = jnp.broadcast_to(local_pos, (NCOL, W))
    target = owner_dev * W + owner_perm[owner_dev, local_full]
    column = source_dev * W + source_perm
    return jnp.zeros((NCOL * W,), jnp.int32).at[column.reshape(-1)].set(target.reshape(-1).astype(jnp.int32))


def draw_siesta_of(key, part):
    return siesta_table(key)


def draw_supernode_of(key, part):
    mapping = siesta_table(key)
    return jnp.zeros((NCOL * W,), jnp.int32).at[mapping].set(jnp.arange(NCOL * W, dtype=jnp.int32))


def draw_ancestors(key, part):
    row_keys = jax.random.split(jax.random.fold_in(key, 3), NCOL)
    return jax.vmap(lambda sub_key: jax.random.permutation(sub_key, NA)[:M])(row_keys).astype(jnp.int32)


def touch_ends(values, rng, smallest, high):
    longest = values.shape.index(max(values.shape))
    spots = []
    for shift in (0, 1):
        where = [jax.random.randint(jax.random.fold_in(rng, axis), (), 0, length) for axis, length in enumerate(values.shape)]
        where[longest] = (where[longest] + shift) % values.shape[longest]
        spots.append(tuple(where))
    return values.at[spots[0]].set(smallest).at[spots[1]].set(high)


def shard_levels(own_key, dims, shards, smallest, high):
    loudness, own = 1.0, jax.random.fold_in(own_key, 6)
    for dim, blocks in shards:
        draws = jnp.exp(jax.random.uniform(jax.random.fold_in(own, dim), (blocks,), jnp.float32, smallest / len(shards), high / len(shards)))
        loudness = loudness * jnp.repeat(draws, dims[dim] // blocks).reshape([-1 if axis == dim else 1 for axis in range(len(dims))])
    return loudness


def centred(key, extent, width, most, cuts=(), kind=jnp.bfloat16):
    array = width * jax.random.normal(key, extent, jnp.float32)
    if cuts:
        array = array * shard_levels(key, extent, cuts, -0.22, 0.18)
    return jnp.clip(array, -most, most).astype(kind)


def setup_inputs(seed: int = 0) -> dict:
    streams_of = jax.random.split(jax.random.key(seed), 12)
    anc_inv = centred(streams_of[0], (POLES, NA * W, NA * W), 1.0, 6.0, ((0, 4), (1, 8)))
    factor_cols = centred(streams_of[1], (POLES, NCOL, M, W, W), (M * W) ** -0.5, 0.25, ((0, 4), (1, 8)))
    diag_inv = centred(streams_of[2], (POLES, NCOL, W, W), 1.0, 6.0, ((0, 4), (1, 8)))
    intersection = centred(streams_of[3], (NCOL, W, W), (W * W) ** -0.5, 0.0234375, ((0, 8),))
    pole_w = jnp.clip(0.5 + 1.5 * jax.random.uniform(streams_of[4], (POLES,), jnp.float32) ** shard_levels(streams_of[4], (POLES,), ((0, 4),), -0.2, 0.2), 0.5, 2.0)
    pole_z = jnp.clip(-2.0 + 1.5 * jax.random.uniform(streams_of[5], (POLES,), jnp.float32) ** shard_levels(streams_of[5], (POLES,), ((0, 4),), -0.2, 0.2), -2.0, -0.5)
    ancestors = draw_ancestors(jax.random.fold_in(streams_of[11], 71), 0)
    counts = touch_ends(jax.random.randint(streams_of[7], (NCOL,), 1, M + 1), jax.random.fold_in(streams_of[7], 1), 1, M).astype(jnp.int32)
    hpattern = touch_ends((jax.random.randint(streams_of[8], (NCOL, M), 0, 3) < 2).astype(jnp.int32), jax.random.fold_in(streams_of[8], 1), 0, 1)
    siesta_of = draw_siesta_of(jax.random.fold_in(streams_of[11], 71), 0)
    supernode_of = draw_supernode_of(jax.random.fold_in(streams_of[11], 71), 0)
    return {"anc_inv": anc_inv, "factor_cols": factor_cols, "diag_inv": diag_inv, "intersection": intersection, "pole_w": pole_w, "pole_z": pole_z, "ancestors": ancestors, "counts": counts, "hpattern": hpattern, "siesta_of": siesta_of, "supernode_of": supernode_of}


def one_pole(anc_pole, factor_pole, diaginv_pole, ancestors, counts, hpattern, intersection):
    anc_blocks = anc_pole.reshape(NA, W, NA, W)

    def one_column(anc_ids, count_one, hmask, factor_one, diaginv_one, intersection_one):
        rows_sel = jnp.take(anc_blocks, anc_ids, axis=0)
        sub_block = jnp.take(rows_sel, anc_ids, axis=2).reshape(M * W, M * W)
        live_mask = (jnp.arange(M) < count_one).astype(jnp.bfloat16)
        lower_cols = (factor_one * live_mask[:, None, None]).reshape(M * W, W)
        off_inv = -jnp.dot(sub_block, lower_cols, preferred_element_type=jnp.float32)
        diag_block = diaginv_one.astype(jnp.float32) - jnp.dot(lower_cols.astype(jnp.float32).T, off_inv, precision=lax.Precision.HIGHEST, preferred_element_type=jnp.float32)
        masked = off_inv.reshape(M, W, W) * hmask.astype(jnp.float32)[:, None, None]
        stacked = jnp.concatenate([diag_block[None], masked], axis=0)
        cols_rows = stacked.transpose(2, 0, 1).reshape(W, (M + 1) * W)
        return cols_rows, jnp.sum(diag_block * intersection_one.astype(jnp.float32))

    return jax.vmap(one_column)(ancestors, counts, hpattern, factor_pole, diaginv_pole, intersection)


def reference(anc_inv, factor_cols, diag_inv, intersection, pole_w, pole_z, ancestors, counts, hpattern, siesta_of, supernode_of):
    dens_sum = jnp.zeros((NCOL, W, (M + 1) * W), jnp.float32)
    energy_sum = jnp.zeros((NCOL, W, (M + 1) * W), jnp.float32)
    electrons = jnp.zeros((), jnp.float32)
    for pole_num in range(POLES):
        cols_rows, traces = one_pole(anc_inv[pole_num], factor_cols[pole_num], diag_inv[pole_num], ancestors, counts, hpattern, intersection)
        dens_sum = dens_sum + pole_w[pole_num] * cols_rows
        energy_sum = energy_sum + pole_z[pole_num] * cols_rows
        electrons = electrons + pole_w[pole_num] * jnp.sum(traces)
    dens_flat = dens_sum.reshape(NORB, (M + 1) * W)
    energy_flat = energy_sum.reshape(NORB, (M + 1) * W)
    density = jnp.take(dens_flat, supernode_of, axis=0).astype(jnp.bfloat16)
    energy = jnp.take(energy_flat, supernode_of, axis=0).astype(jnp.bfloat16)
    return (density, energy, electrons)
```

```python
import functools

import jax
import jax.numpy as jnp
from jax import lax
from jax.experimental import pallas as pl
from jax.experimental.pallas import tpu as pltpu
from jax.sharding import PartitionSpec as P

VMEM = pltpu.VMEM
SMEM = pltpu.SMEM
LANES = 128
SUB = 8


def vspec():
    return pl.BlockSpec(memory_space=VMEM)


def sspec():
    return pl.BlockSpec(memory_space=SMEM)


def select_kernel(width, rows, blk_count, table_ref, spread_ref, out_ref):
    for dest in range(out_ref.shape[0]):
        for row_blk in range(blk_count):
            row_at = pl.multiple_of(table_ref[dest, row_blk] * rows, rows)
            for col_blk in range(blk_count):
                col_at = pl.multiple_of(table_ref[dest, col_blk] * width, width)
                out_ref[
                    dest,
                    row_blk * rows : (row_blk + 1) * rows,
                    col_blk * width : (col_blk + 1) * width,
                ] = spread_ref[pl.ds(row_at, rows), pl.ds(col_at, width)]


def columns_kernel(
    shares,
    chunk,
    counts_ref,
    hpattern_ref,
    weight_ref,
    energy_ref,
    rows_ref,
    factor_ref,
    diag_ref,
    inter_ref,
    out_ref,
    off_ref,
):
    blk_count, width, _ = factor_ref.shape
    parts = [
        factor_ref[m] * (m < counts_ref[0]).astype(jnp.float32).astype(jnp.bfloat16)
        for m in range(blk_count)
    ]
    lower = jnp.concatenate(parts, axis=0)
    product = jnp.dot(rows_ref[...], lower, preferred_element_type=jnp.float32)
    per_blk = width // shares
    for m in range(blk_count):
        scale = hpattern_ref[0, m].astype(jnp.float32)
        for j in range(shares):
            for c in range(per_blk // SUB):
                at = (j * blk_count + m) * per_blk + c * SUB
                piece = -product[at : at + SUB]
                row = m * width + (c * shares + j) * SUB
                off_ref[row : row + SUB, :] = piece
                place = width + row
                out_ref[place // chunk, place % chunk : place % chunk + SUB, :] = piece * scale
    off = off_ref[...]
    high = off.astype(jnp.bfloat16)
    rest = off - high.astype(jnp.float32)
    mid = rest.astype(jnp.bfloat16)
    low = (rest - mid.astype(jnp.float32)).astype(jnp.bfloat16)
    contract = functools.partial(
        lax.dot_general,
        dimension_numbers=(((0,), (0,)), ((), ())),
        preferred_element_type=jnp.float32,
    )
    product_sum = contract(lower, low) + contract(lower, mid) + contract(lower, high)
    diag_block = diag_ref[...].astype(jnp.float32) - product_sum
    at = 0
    while at < width:
        size = min(chunk - at % chunk, width - at)
        out_ref[at // chunk, at % chunk : at % chunk + size, :] = diag_block[at : at + size]
        at += size
    count = weight_ref[0] * jnp.sum(diag_block * inter_ref[...].astype(jnp.float32))
    row_id = lax.broadcasted_iota(jnp.int32, (SUB, width), 0)
    extra = jnp.where(row_id == 0, weight_ref[0], jnp.where(row_id == 1, energy_ref[0], count))
    for q in range(out_ref.shape[0]):
        out_ref[q, chunk : chunk + SUB, :] = extra


def place_kernel(slot_cap, dests, slot_ref, stack_ref, out_ref):
    poles, rows, width = stack_ref.shape
    chunk = rows - SUB
    dens = jnp.zeros((chunk, width), jnp.float32)
    energy = jnp.zeros((chunk, width), jnp.float32)
    count = jnp.zeros((1, width), jnp.float32)
    for p in range(poles):
        term = stack_ref[p, :chunk, :]
        dens = dens + stack_ref[p, chunk : chunk + 1, :] * term
        energy = energy + stack_ref[p, chunk + 1 : chunk + 2, :] * term
        count = count + stack_ref[p, chunk + 2 : chunk + 3, :]
    both = jnp.concatenate([dens, energy], axis=0).astype(jnp.bfloat16)
    total, lanes = out_ref.shape
    slots = total // dests
    one_hot = (lax.broadcasted_iota(jnp.int32, (total, width), 0) == slot_ref[...]).astype(
        jnp.bfloat16
    )
    placed = lax.dot_general(
        one_hot, both, (((1,), (1,)), ((), ())), preferred_element_type=jnp.float32
    )
    own = count[:, 0:1]
    high = own.astype(jnp.bfloat16).astype(jnp.float32)
    rest = own - high
    mid = rest.astype(jnp.bfloat16).astype(jnp.float32)
    lane = lax.broadcasted_iota(jnp.int32, (1, lanes), 1)
    pieces = jnp.where(lane == 0, high, jnp.where(lane == 1, mid, rest - mid))
    pieces = jnp.where(lane < 3, pieces, 0.0)
    row = lax.broadcasted_iota(jnp.int32, (total, 1), 0)
    marked = functools.reduce(
        jnp.logical_or, [row == g * slots + slot_cap for g in range(dests)]
    )
    out_ref[...] = jnp.where(marked, pieces, placed).astype(jnp.bfloat16)


def pickup_kernel(slot_cap, dests, slot_ref, recv_ref, dens_ref, energy_ref, count_ref):
    total, lanes = recv_ref.shape
    slots = total // dests
    chunk = lanes // 2
    width = slot_ref.shape[1]
    recv = recv_ref[...]
    one_hot = (lax.broadcasted_iota(jnp.int32, (total, width), 0) == slot_ref[...]).astype(
        jnp.bfloat16
    )
    out = lax.dot_general(
        recv, one_hot, (((0,), (0,)), ((), ())), preferred_element_type=jnp.float32
    ).astype(jnp.bfloat16)
    dens_ref[...] = out[:chunk]
    energy_ref[...] = out[chunk:]
    row = lax.broadcasted_iota(jnp.int32, (total, 1), 0)
    marked = functools.reduce(
        jnp.logical_or, [row == g * slots + slot_cap for g in range(dests)]
    )
    pieces = jnp.where(marked, recv[:, :LANES].astype(jnp.float32), 0.0)
    count_ref[0, 0] = jnp.sum(pieces)


def ranks(own, order):
    same = own[:, None] == own[None, :]
    earlier = order[None, :] < order[:, None]
    return jnp.sum((same & earlier).astype(jnp.int32), axis=1)


def body(
    anc_inv,
    factor_cols,
    diag_inv,
    intersection,
    pole_w,
    pole_z,
    ancestors,
    counts,
    hpattern,
    siesta_of,
    supernode_of,
):
    width = diag_inv.shape[-1]
    local_rows, anc_rows = anc_inv.shape[1:]
    blk_count = ancestors.shape[1]
    grid_count = lax.axis_size("grid")
    pole_count = lax.axis_size("pole")
    chunk = (blk_count + 1) * width // pole_count
    slot_cap = (width + grid_count - 1) // grid_count
    slots = slot_cap + (SUB if slot_cap % SUB == 0 else 1)

    dest_owner = siesta_of // width
    send_slot = dest_owner * slots + ranks(dest_owner, jnp.arange(width))
    source_dev = supernode_of // width
    recv_slot = source_dev * slots + ranks(source_dev, supernode_of)

    spread = grid_count * SUB
    if local_rows % spread == 0 and width % spread == 0:
        shares = grid_count
        mine = anc_inv[0].reshape(local_rows // spread, grid_count, SUB, anc_rows)
        mine = mine.transpose(1, 0, 2, 3).reshape(grid_count, local_rows // grid_count, anc_rows)
        table = jnp.broadcast_to(
            jnp.pad(ancestors, ((0, 0), (0, LANES - blk_count))).astype(jnp.bfloat16)[None],
            (grid_count, local_rows // grid_count, LANES),
        )
        sent = jnp.concatenate([mine, table], axis=2)
        held = lax.all_to_all(sent, "grid", split_axis=0, concat_axis=0, tiled=True)
        all_anc = held[:, 0, anc_rows : anc_rows + blk_count].astype(jnp.int32)
        rows = width // grid_count
        chosen = pl.pallas_call(
            functools.partial(select_kernel, width, rows, blk_count),
            out_shape=jax.ShapeDtypeStruct(
                (grid_count, blk_count * rows, blk_count * width), jnp.bfloat16
            ),
            in_specs=[sspec(), vspec()],
            out_specs=vspec(),
            name="select",
        )(all_anc, held.reshape(local_rows, anc_rows + LANES))
        sub_block = lax.all_to_all(chosen, "grid", split_axis=0, concat_axis=0, tiled=True)
    else:
        shares = 1
        gathered = lax.all_gather(anc_inv[0], "grid", axis=0, tiled=True)
        blocks = gathered.reshape(anc_rows // width, width, anc_rows // width, width)
        sub_block = jnp.take(jnp.take(blocks, ancestors[0], axis=0), ancestors[0], axis=2)
    sub_block = sub_block.reshape(blk_count * width, blk_count * width)

    stack = pl.pallas_call(
        functools.partial(columns_kernel, shares, chunk),
        out_shape=jax.ShapeDtypeStruct((pole_count, chunk + SUB, width), jnp.float32),
        in_specs=[sspec()] * 4 + [vspec()] * 4,
        out_specs=vspec(),
        scratch_shapes=[VMEM((blk_count * width, width), jnp.float32)],
        name="columns",
    )(
        counts,
        hpattern,
        pole_w,
        pole_z,
        sub_block,
        factor_cols[0, 0],
        diag_inv[0, 0],
        intersection[0],
    )
    stack = lax.all_to_all(stack, "pole", split_axis=0, concat_axis=0, tiled=True)

    total = grid_count * slots
    placed = pl.pallas_call(
        functools.partial(place_kernel, slot_cap, grid_count),
        out_shape=jax.ShapeDtypeStruct((total, 2 * chunk), jnp.bfloat16),
        in_specs=[vspec(), vspec()],
        out_specs=vspec(),
        name="place",
    )(send_slot[None], stack)
    arrived = lax.all_to_all(
        placed.reshape(grid_count, slots, 2 * chunk),
        "grid",
        split_axis=0,
        concat_axis=0,
        tiled=True,
    )
    density, energy, electrons = pl.pallas_call(
        functools.partial(pickup_kernel, slot_cap, grid_count),
        out_shape=(
            jax.ShapeDtypeStruct((chunk, width), jnp.bfloat16),
            jax.ShapeDtypeStruct((chunk, width), jnp.bfloat16),
            jax.ShapeDtypeStruct((1, 1), jnp.float32),
        ),
        in_specs=[vspec(), vspec()],
        out_specs=(vspec(), vspec(), sspec()),
        name="pickup",
    )(recv_slot[None], arrived.reshape(total, 2 * chunk))
    return (density.T, energy.T, electrons[0, 0])


def solution(mesh):
    placed = (
        P("pole", "grid", None),
        P("pole", "grid", None, None, None),
        P("pole", "grid", None, None),
        P("grid", None, None),
        P("pole"),
        P("pole"),
        P("grid", None),
        P("grid"),
        P("grid", None),
        P("grid"),
        P("grid"),
    )
    return jax.shard_map(
        body,
        mesh=mesh,
        in_specs=placed,
        out_specs=(P("grid", "pole"), P("grid", "pole"), P()),
        check_vma=False,
    )
```

```python
import functools

import jax
import jax.numpy as jnp
from jax import lax
from jax.experimental import pallas as pl
from jax.experimental.pallas import tpu as pltpu
from jax.sharding import PartitionSpec as P

VMEM = pltpu.VMEM
SMEM = pltpu.SMEM
LANES = 128
SUB = 8


def invmem(x):
    return pltpu.with_memory_space_constraint(x, VMEM)


def vspec():
    return pl.BlockSpec(memory_space=VMEM)


def sspec():
    return pl.BlockSpec(memory_space=SMEM)


def select_kernel(width, rows, blk_count, table_ref, spread_ref, out_ref):
    for dest in range(out_ref.shape[0]):
        for row_blk in range(blk_count):
            row_at = pl.multiple_of(table_ref[dest, row_blk] * rows, rows)
            for col_blk in range(blk_count):
                col_at = pl.multiple_of(table_ref[dest, col_blk] * width, width)
                out_ref[
                    dest,
                    row_blk * rows : (row_blk + 1) * rows,
                    col_blk * width : (col_blk + 1) * width,
                ] = spread_ref[pl.ds(row_at, rows), pl.ds(col_at, width)]


def columns_kernel(
    shares,
    chunk,
    counts_ref,
    hpattern_ref,
    weight_ref,
    energy_ref,
    rows_ref,
    factor_ref,
    diag_ref,
    inter_ref,
    out_ref,
    off_ref,
):
    blk_count, width, _ = factor_ref.shape
    parts = [
        factor_ref[m] * (m < counts_ref[0]).astype(jnp.float32).astype(jnp.bfloat16)
        for m in range(blk_count)
    ]
    lower = jnp.concatenate(parts, axis=0)
    product = jnp.dot(rows_ref[...], lower, preferred_element_type=jnp.float32)
    per_blk = width // shares
    for m in range(blk_count):
        scale = hpattern_ref[0, m].astype(jnp.float32)
        for j in range(shares):
            for c in range(per_blk // SUB):
                at = (j * blk_count + m) * per_blk + c * SUB
                piece = -product[at : at + SUB]
                row = m * width + (c * shares + j) * SUB
                off_ref[row : row + SUB, :] = piece
                place = width + row
                out_ref[place // chunk, place % chunk : place % chunk + SUB, :] = piece * scale
    off = off_ref[...]
    high = off.astype(jnp.bfloat16)
    rest = off - high.astype(jnp.float32)
    mid = rest.astype(jnp.bfloat16)
    low = (rest - mid.astype(jnp.float32)).astype(jnp.bfloat16)
    contract = functools.partial(
        lax.dot_general,
        dimension_numbers=(((0,), (0,)), ((), ())),
        preferred_element_type=jnp.float32,
    )
    product_sum = contract(lower, low) + contract(lower, mid) + contract(lower, high)
    diag_block = diag_ref[...].astype(jnp.float32) - product_sum
    at = 0
    while at < width:
        size = min(chunk - at % chunk, width - at)
        out_ref[at // chunk, at % chunk : at % chunk + size, :] = diag_block[at : at + size]
        at += size
    count = weight_ref[0] * jnp.sum(diag_block * inter_ref[...].astype(jnp.float32))
    row_id = lax.broadcasted_iota(jnp.int32, (SUB, width), 0)
    extra = jnp.where(row_id == 0, weight_ref[0], jnp.where(row_id == 1, energy_ref[0], count))
    for q in range(out_ref.shape[0]):
        out_ref[q, chunk : chunk + SUB, :] = extra


def place_kernel(slot_cap, dests, slot_ref, stack_ref, out_ref):
    poles, rows, width = stack_ref.shape
    chunk = rows - SUB
    dens = jnp.zeros((chunk, width), jnp.float32)
    energy = jnp.zeros((chunk, width), jnp.float32)
    count = jnp.zeros((1, width), jnp.float32)
    for p in range(poles):
        term = stack_ref[p, :chunk, :]
        dens = dens + stack_ref[p, chunk : chunk + 1, :] * term
        energy = energy + stack_ref[p, chunk + 1 : chunk + 2, :] * term
        count = count + stack_ref[p, chunk + 2 : chunk + 3, :]
    both = jnp.concatenate([dens, energy], axis=0).astype(jnp.bfloat16)
    total, lanes = out_ref.shape
    slots = total // dests
    one_hot = (lax.broadcasted_iota(jnp.int32, (total, width), 0) == slot_ref[...]).astype(
        jnp.bfloat16
    )
    placed = lax.dot_general(
        one_hot, both, (((1,), (1,)), ((), ())), preferred_element_type=jnp.float32
    )
    own = count[:, 0:1]
    high = own.astype(jnp.bfloat16).astype(jnp.float32)
    rest = own - high
    mid = rest.astype(jnp.bfloat16).astype(jnp.float32)
    lane = lax.broadcasted_iota(jnp.int32, (1, lanes), 1)
    pieces = jnp.where(lane == 0, high, jnp.where(lane == 1, mid, rest - mid))
    pieces = jnp.where(lane < 3, pieces, 0.0)
    row = lax.broadcasted_iota(jnp.int32, (total, 1), 0)
    marked = functools.reduce(
        jnp.logical_or, [row == g * slots + slot_cap for g in range(dests)]
    )
    out_ref[...] = jnp.where(marked, pieces, placed).astype(jnp.bfloat16)


def pickup_kernel(slot_cap, dests, slot_ref, recv_ref, dens_ref, energy_ref, count_ref):
    total, lanes = recv_ref.shape
    slots = total // dests
    chunk = lanes // 2
    width = slot_ref.shape[1]
    recv = recv_ref[...]
    one_hot = (lax.broadcasted_iota(jnp.int32, (total, width), 0) == slot_ref[...]).astype(
        jnp.bfloat16
    )
    out = lax.dot_general(
        recv, one_hot, (((0,), (0,)), ((), ())), preferred_element_type=jnp.float32
    ).astype(jnp.bfloat16)
    dens_ref[...] = out[:chunk]
    energy_ref[...] = out[chunk:]
    row = lax.broadcasted_iota(jnp.int32, (total, 1), 0)
    marked = functools.reduce(
        jnp.logical_or, [row == g * slots + slot_cap for g in range(dests)]
    )
    pieces = jnp.where(marked, recv[:, :LANES].astype(jnp.float32), 0.0)
    count_ref[0, 0] = jnp.sum(pieces)


def ranks(own, order):
    same = own[:, None] == own[None, :]
    earlier = order[None, :] < order[:, None]
    return jnp.sum((same & earlier).astype(jnp.int32), axis=1)


def body(
    anc_inv,
    factor_cols,
    diag_inv,
    intersection,
    pole_w,
    pole_z,
    ancestors,
    counts,
    hpattern,
    siesta_of,
    supernode_of,
):
    width = diag_inv.shape[-1]
    local_rows, anc_rows = anc_inv.shape[1:]
    blk_count = ancestors.shape[1]
    grid_count = lax.axis_size("grid")
    pole_count = lax.axis_size("pole")
    chunk = (blk_count + 1) * width // pole_count
    slot_cap = (width + grid_count - 1) // grid_count
    slots = slot_cap + (SUB if slot_cap % SUB == 0 else 1)

    dest_owner = siesta_of // width
    send_slot = dest_owner * slots + ranks(dest_owner, jnp.arange(width))
    source_dev = supernode_of // width
    recv_slot = source_dev * slots + ranks(source_dev, supernode_of)

    spread = grid_count * SUB
    if local_rows % spread == 0 and width % spread == 0:
        shares = grid_count
        mine = anc_inv[0].reshape(local_rows // spread, grid_count, SUB, anc_rows)
        mine = mine.transpose(1, 0, 2, 3).reshape(grid_count, local_rows // grid_count, anc_rows)
        table = jnp.broadcast_to(
            jnp.pad(ancestors, ((0, 0), (0, LANES - blk_count))).astype(jnp.bfloat16)[None],
            (grid_count, local_rows // grid_count, LANES),
        )
        sent = jnp.concatenate([mine, table], axis=2)
        held = lax.all_to_all(sent, "grid", split_axis=0, concat_axis=0, tiled=True)
        all_anc = held[:, 0, anc_rows : anc_rows + blk_count].astype(jnp.int32)
        rows = width // grid_count
        chosen = pl.pallas_call(
            functools.partial(select_kernel, width, rows, blk_count),
            out_shape=jax.ShapeDtypeStruct(
                (grid_count, blk_count * rows, blk_count * width), jnp.bfloat16
            ),
            in_specs=[sspec(), vspec()],
            out_specs=vspec(),
            name="select",
        )(all_anc, invmem(held.reshape(local_rows, anc_rows + LANES)))
        sub_block = lax.all_to_all(chosen, "grid", split_axis=0, concat_axis=0, tiled=True)
    else:
        shares = 1
        gathered = lax.all_gather(anc_inv[0], "grid", axis=0, tiled=True)
        blocks = gathered.reshape(anc_rows // width, width, anc_rows // width, width)
        sub_block = jnp.take(jnp.take(blocks, ancestors[0], axis=0), ancestors[0], axis=2)
    sub_block = sub_block.reshape(blk_count * width, blk_count * width)

    stack = pl.pallas_call(
        functools.partial(columns_kernel, shares, chunk),
        out_shape=jax.ShapeDtypeStruct((pole_count, chunk + SUB, width), jnp.float32),
        in_specs=[sspec()] * 4 + [vspec()] * 4,
        out_specs=vspec(),
        scratch_shapes=[VMEM((blk_count * width, width), jnp.float32)],
        name="columns",
    )(
        counts,
        hpattern,
        pole_w,
        pole_z,
        invmem(sub_block),
        factor_cols[0, 0],
        diag_inv[0, 0],
        intersection[0],
    )
    stack = lax.all_to_all(stack, "pole", split_axis=0, concat_axis=0, tiled=True)

    total = grid_count * slots
    placed = pl.pallas_call(
        functools.partial(place_kernel, slot_cap, grid_count),
        out_shape=jax.ShapeDtypeStruct((total, 2 * chunk), jnp.bfloat16),
        in_specs=[vspec(), vspec()],
        out_specs=vspec(),
        name="place",
    )(send_slot[None], invmem(stack))
    arrived = lax.all_to_all(
        placed.reshape(grid_count, slots, 2 * chunk),
        "grid",
        split_axis=0,
        concat_axis=0,
        tiled=True,
    )
    density, energy, electrons = pl.pallas_call(
        functools.partial(pickup_kernel, slot_cap, grid_count),
        out_shape=(
            jax.ShapeDtypeStruct((chunk, width), jnp.bfloat16),
            jax.ShapeDtypeStruct((chunk, width), jnp.bfloat16),
            jax.ShapeDtypeStruct((1, 1), jnp.float32),
        ),
        in_specs=[vspec(), vspec()],
        out_specs=(vspec(), vspec(), sspec()),
        name="pickup",
    )(recv_slot[None], invmem(arrived.reshape(total, 2 * chunk)))
    return (density.T, energy.T, electrons[0, 0])


def solution(mesh):
    placed = (
        P("pole", "grid", None),
        P("pole", "grid", None, None, None),
        P("pole", "grid", None, None),
        P("grid", None, None),
        P("pole"),
        P("pole"),
        P("grid", None),
        P("grid"),
        P("grid", None),
        P("grid"),
        P("grid"),
    )
    return jax.shard_map(
        body,
        mesh=mesh,
        in_specs=placed,
        out_specs=(P("grid", "pole"), P("grid", "pole"), P()),
        check_vma=False,
    )
```

```python
import functools

import jax
import jax.numpy as jnp
from jax import lax
from jax.experimental import pallas as pl
from jax.experimental.pallas import tpu as pltpu
from jax.sharding import PartitionSpec as P

VMEM = pltpu.VMEM
SMEM = pltpu.SMEM
LANES = 128
SUB = 8
TINY = 1e-30
FINE = 64.0
STEPS = 32760.0


def invmem(x):
    return pltpu.with_memory_space_constraint(x, VMEM)


def vspec():
    return pl.BlockSpec(memory_space=VMEM)


def sspec():
    return pl.BlockSpec(memory_space=SMEM)


def select_kernel(width, rows, blk_count, table_ref, spread_ref, out_ref):
    for dest in range(out_ref.shape[0]):
        for row_blk in range(blk_count):
            row_at = pl.multiple_of(table_ref[dest, row_blk] * rows, rows)
            for col_blk in range(blk_count):
                col_at = pl.multiple_of(table_ref[dest, col_blk] * width, width)
                out_ref[
                    dest,
                    row_blk * rows : (row_blk + 1) * rows,
                    col_blk * width : (col_blk + 1) * width,
                ] = spread_ref[pl.ds(row_at, rows), pl.ds(col_at, width)]


def columns_kernel(
    shares,
    chunk,
    counts_ref,
    hpattern_ref,
    weight_ref,
    energy_ref,
    rows_ref,
    factor_ref,
    diag_ref,
    inter_ref,
    out_ref,
    off_ref,
):
    blk_count, width, _ = factor_ref.shape
    parts = [
        factor_ref[m] * (m < counts_ref[0]).astype(jnp.float32).astype(jnp.bfloat16)
        for m in range(blk_count)
    ]
    lower = jnp.concatenate(parts, axis=0)
    product = jnp.dot(rows_ref[...], lower, preferred_element_type=jnp.float32)
    per_blk = width // shares
    for m in range(blk_count):
        scale = hpattern_ref[0, m].astype(jnp.float32)
        for j in range(shares):
            for c in range(per_blk // SUB):
                at = (j * blk_count + m) * per_blk + c * SUB
                piece = -product[at : at + SUB]
                row = m * width + (c * shares + j) * SUB
                off_ref[row : row + SUB, :] = piece
                place = width + row
                out_ref[place // chunk, place % chunk : place % chunk + SUB, :] = piece * scale
    off = off_ref[...]
    high = off.astype(jnp.bfloat16)
    rest = off - high.astype(jnp.float32)
    mid = rest.astype(jnp.bfloat16)
    low = (rest - mid.astype(jnp.float32)).astype(jnp.bfloat16)
    contract = functools.partial(
        lax.dot_general,
        dimension_numbers=(((0,), (0,)), ((), ())),
        preferred_element_type=jnp.float32,
    )
    product_sum = contract(lower, low) + contract(lower, mid) + contract(lower, high)
    diag_block = diag_ref[...].astype(jnp.float32) - product_sum
    at = 0
    while at < width:
        size = min(chunk - at % chunk, width - at)
        out_ref[at // chunk, at % chunk : at % chunk + size, :] = diag_block[at : at + size]
        at += size
    count = weight_ref[0] * jnp.sum(diag_block * inter_ref[...].astype(jnp.float32))
    row_id = lax.broadcasted_iota(jnp.int32, (SUB, width), 0)
    extra = jnp.where(row_id == 0, weight_ref[0], jnp.where(row_id == 1, energy_ref[0], count))
    for q in range(out_ref.shape[0]):
        out_ref[q, chunk : chunk + SUB, :] = extra


def place_kernel(slot_cap, dests, slot_ref, stack_ref, out_ref):
    poles, rows, width = stack_ref.shape
    chunk = rows - SUB
    dens = jnp.zeros((chunk, width), jnp.float32)
    energy = jnp.zeros((chunk, width), jnp.float32)
    count = jnp.zeros((1, width), jnp.float32)
    for p in range(poles):
        term = stack_ref[p, :chunk, :]
        dens = dens + stack_ref[p, chunk : chunk + 1, :] * term
        energy = energy + stack_ref[p, chunk + 1 : chunk + 2, :] * term
        count = count + stack_ref[p, chunk + 2 : chunk + 3, :]
    both = jnp.concatenate([dens, energy], axis=0).astype(jnp.bfloat16)
    total, lanes = out_ref.shape
    slots = total // dests
    one_hot = (lax.broadcasted_iota(jnp.int32, (total, width), 0) == slot_ref[...]).astype(
        jnp.bfloat16
    )
    placed = lax.dot_general(
        one_hot, both, (((1,), (1,)), ((), ())), preferred_element_type=jnp.float32
    )
    own = count[:, 0:1]
    high = own.astype(jnp.bfloat16).astype(jnp.float32)
    rest = own - high
    mid = rest.astype(jnp.bfloat16).astype(jnp.float32)
    lane = lax.broadcasted_iota(jnp.int32, (1, lanes), 1)
    pieces = jnp.where(lane == 0, high, jnp.where(lane == 1, mid, rest - mid))
    pieces = jnp.where(lane < 3, pieces, 0.0)
    row = lax.broadcasted_iota(jnp.int32, (total, 1), 0)
    marked = functools.reduce(
        jnp.logical_or, [row == g * slots + slot_cap for g in range(dests)]
    )
    out_ref[...] = jnp.where(marked, pieces, placed).astype(jnp.bfloat16)


def pickup_kernel(slot_cap, dests, slot_ref, recv_ref, dens_ref, energy_ref, count_ref):
    total, lanes = recv_ref.shape
    slots = total // dests
    chunk = lanes // 2
    width = slot_ref.shape[1]
    recv = recv_ref[...]
    one_hot = (lax.broadcasted_iota(jnp.int32, (total, width), 0) == slot_ref[...]).astype(
        jnp.bfloat16
    )
    out = lax.dot_general(
        recv, one_hot, (((0,), (0,)), ((), ())), preferred_element_type=jnp.float32
    ).astype(jnp.bfloat16)
    dens_ref[...] = out[:chunk]
    energy_ref[...] = out[chunk:]
    row = lax.broadcasted_iota(jnp.int32, (total, 1), 0)
    marked = functools.reduce(
        jnp.logical_or, [row == g * slots + slot_cap for g in range(dests)]
    )
    pieces = jnp.where(marked, recv[:, :LANES].astype(jnp.float32), 0.0)
    count_ref[0, 0] = jnp.sum(pieces)


def order_kernel(
    counts_ref, slot_ref, factor_ref, diag_ref, inter_ref, lower_ref, turned_ref, diag_out, inter_out
):
    blk_count, width, _ = factor_ref.shape
    one_hot = (lax.broadcasted_iota(jnp.int32, (width, width), 0) == slot_ref[...]).astype(
        jnp.bfloat16
    )

    def turn(matrix):
        return lax.dot_general(
            one_hot, matrix, (((1,), (1,)), ((), ())), preferred_element_type=jnp.float32
        ).astype(jnp.bfloat16)

    for m in range(blk_count):
        live = (m < counts_ref[0]).astype(jnp.float32).astype(jnp.bfloat16)
        block = factor_ref[m] * live
        lower_ref[m * width : (m + 1) * width, :] = block
        turned_ref[:, m * width : (m + 1) * width] = turn(block)
    diag_out[...] = turn(diag_ref[...])
    inter_out[...] = turn(inter_ref[...])


def halved_sum(values):
    while values.shape[0] > SUB:
        half = values.shape[0] // 2
        values = values[:half] + values[half:]
    while values.shape[1] > LANES:
        half = values.shape[1] // 2
        values = values[:, :half] + values[:, half:]
    return jnp.sum(values)


def whole(value):
    return value.astype(jnp.int32).astype(jnp.int16)


def fold_half(tile, right):
    rows = tile.shape[0] // 2
    lane = lax.broadcasted_iota(jnp.int32, (rows, LANES), 1)
    top, bottom = tile[:rows], tile[rows:]
    if right:
        return jnp.where(lane < LANES // 2, pltpu.roll(top, LANES // 2, 1), bottom)
    return jnp.where(lane < LANES // 2, top, pltpu.roll(bottom, LANES // 2, 1))


def encode_kernel(
    shares,
    chunk,
    hpattern_ref,
    weight_ref,
    energy_ref,
    rows_ref,
    lower_ref,
    turned_ref,
    diag_ref,
    inter_ref,
    out_ref,
    sorted_ref,
):
    blk_count = hpattern_ref.shape[1]
    width = lower_ref.shape[1]
    per_blk = width // shares
    for m in range(blk_count):
        for j in range(shares):
            at = (j * blk_count + m) * per_blk
            piece = rows_ref[at : at + per_blk, :].astype(jnp.float32)
            for c in range(per_blk // SUB):
                row = m * width + (c * shares + j) * SUB
                sorted_ref[row : row + SUB, :] = piece[c * SUB : (c + 1) * SUB]
    off = -lax.dot_general(
        turned_ref[...],
        sorted_ref[...].astype(jnp.bfloat16),
        (((1,), (1,)), ((), ())),
        preferred_element_type=jnp.float32,
    )
    high = off.astype(jnp.bfloat16)
    rest = off - high.astype(jnp.float32)
    mid = rest.astype(jnp.bfloat16)
    low = (rest - mid.astype(jnp.float32)).astype(jnp.bfloat16)
    lower = lower_ref[...]
    diag = diag_ref[...].astype(jnp.float32) - (
        jnp.dot(low, lower, preferred_element_type=jnp.float32)
        + jnp.dot(mid, lower, preferred_element_type=jnp.float32)
        + jnp.dot(high, lower, preferred_element_type=jnp.float32)
    )
    count = weight_ref[0] * halved_sum(diag * inter_ref[...].astype(jnp.float32))
    parts = [diag] + [
        off[:, m * width : (m + 1) * width] * hpattern_ref[0, m].astype(jnp.float32)
        for m in range(blk_count)
    ]
    values = jnp.concatenate(parts, axis=1)
    largest = jnp.max(jnp.abs(values), axis=0, keepdims=True)
    level = jnp.ceil(jnp.log2(jnp.maximum(largest, TINY)) * FINE)
    codes = jnp.floor(values * (jnp.exp2(level * (-1.0 / FINE)) * STEPS) + 0.5)

    row_id = lax.broadcasted_iota(jnp.int32, (SUB, LANES), 0)
    lane_id = lax.broadcasted_iota(jnp.int32, (SUB, LANES), 1)
    full_count = jnp.full((SUB, LANES), count)
    power = jnp.ceil(jnp.log2(jnp.maximum(jnp.abs(full_count), TINY)))
    scaled = full_count * jnp.exp2(-power) * 2.0**14
    scaled_high = jnp.floor(scaled)
    extra = jnp.where(
        lane_id == 0,
        power,
        jnp.where(lane_id == 1, scaled_high, jnp.floor((scaled - scaled_high) * 2.0**15)),
    )
    for at, scalar in ((2, weight_ref[0]), (4, energy_ref[0])):
        grown = jnp.full((SUB, LANES), scalar) * 2.0**13
        grown_high = jnp.floor(grown)
        extra = jnp.where(row_id == at, grown_high, extra)
        extra = jnp.where(row_id == at + 1, (grown - grown_high) * 2.0**15, extra)

    dests, _, _ = out_ref.shape
    pole_count = values.shape[1] // chunk
    owners = dests // pole_count
    cap = width // owners
    half = cap // 2
    for q in range(pole_count):
        right = q % 2 == 1
        full_at = (q * chunk + LANES - 1) // LANES * LANES
        half_at = full_at - LANES if right else full_at + LANES
        level_half = level[:, half_at : half_at + LANES]
        lane = lax.broadcasted_iota(jnp.int32, (1, LANES), 1)
        other = pltpu.roll(jnp.broadcast_to(level_half, (SUB, LANES)), LANES // 2, 1)[:1]
        level_half = jnp.where((lane < LANES // 2) == (not right), level_half, other)
        tail = jnp.where(
            row_id == 0,
            level[:, full_at : full_at + LANES],
            jnp.where(row_id == 1, level_half, extra),
        )
        tail = whole(tail)
        for g in range(owners):
            rows = slice(g * cap, (g + 1) * cap)
            d = q * owners + g
            out_ref[d, :cap, :] = whole(codes[rows, full_at : full_at + LANES])
            out_ref[d, cap : cap + half, :] = whole(
                fold_half(codes[rows, half_at : half_at + LANES], right)
            )
            out_ref[d, cap + half :, :] = tail


def decode_kernel(
    owners, cap, odd_ref, slot_ref, recv_ref, dens_ref, energy_ref, count_ref, full_ref, half_ref
):
    dests, rows, _ = recv_ref.shape
    poles = dests // owners
    half = cap // 2
    width = slot_ref.shape[1]
    count = jnp.zeros((1, 1), jnp.float32)
    lost = jnp.zeros((1, 1), jnp.float32)
    for g in range(owners):
        sums = [0.0, 0.0, 0.0, 0.0]
        for p in range(poles):
            piece = recv_ref[p * owners + g].astype(jnp.int32).astype(jnp.float32)
            extra = piece[cap + half :]
            scale = jnp.exp2(extra[:2] * (1.0 / FINE)) * (1.0 / STEPS)
            weight = extra[2:3] * 2.0**-13 + extra[3:4] * 2.0**-28
            energy = extra[4:5] * 2.0**-13 + extra[5:6] * 2.0**-28
            full = piece[:cap] * scale[:1]
            rest = piece[cap : cap + half] * scale[1:2]
            for at, term in enumerate(
                (weight * full, energy * full, weight * rest, energy * rest)
            ):
                sums[at] = sums[at] + term
            own = extra[6:7]
            own = (own[:, 1:2] * 2.0**-14 + own[:, 2:3] * 2.0**-29) * jnp.exp2(own[:, 0:1])
            grown = count + own
            part = grown - count
            lost = lost + ((count - (grown - part)) + (own - part))
            count = grown
        full_ref[g * cap : (g + 1) * cap, :LANES] = sums[0].astype(jnp.bfloat16)
        full_ref[g * cap : (g + 1) * cap, LANES:] = sums[1].astype(jnp.bfloat16)
        half_ref[g * half : (g + 1) * half, :LANES] = sums[2].astype(jnp.bfloat16)
        half_ref[g * half : (g + 1) * half, LANES:] = sums[3].astype(jnp.bfloat16)
    count_ref[0, 0] = jnp.sum(count + lost)

    slot = slot_ref[...]
    pick = (lax.broadcasted_iota(jnp.int32, (owners * cap, width), 0) == slot).astype(jnp.bfloat16)
    row = lax.broadcasted_iota(jnp.int32, (owners * half, width), 0)
    owner = slot // cap
    within = slot - owner * cap
    place = owner * half + within
    left = (row == jnp.where(within < half, place, -1)).astype(jnp.bfloat16)
    right = (row == jnp.where(within >= half, place - half, -1)).astype(jnp.bfloat16)

    def take(held, chosen):
        return lax.dot_general(
            held, chosen, (((0,), (0,)), ((), ())), preferred_element_type=jnp.float32
        )

    full = take(full_ref[...], pick).astype(jnp.bfloat16)
    by_left = take(half_ref[...], left)
    by_right = take(half_ref[...], right)
    mid = LANES // 2
    full_at = pl.multiple_of(odd_ref[0] * mid, mid)
    half_at = pl.multiple_of((1 - odd_ref[0]) * LANES, mid)
    for at, ref in ((0, dens_ref), (LANES, energy_ref)):
        ref[pl.ds(full_at, LANES), :] = full[at : at + LANES]
        joined = by_left[at : at + mid] + by_right[at + mid : at + LANES]
        ref[pl.ds(half_at, mid), :] = joined.astype(jnp.bfloat16)


def ranks(own, order):
    same = own[:, None] == own[None, :]
    earlier = order[None, :] < order[:, None]
    return jnp.sum((same & earlier).astype(jnp.int32), axis=1)


def body(
    anc_inv,
    factor_cols,
    diag_inv,
    intersection,
    pole_w,
    pole_z,
    ancestors,
    counts,
    hpattern,
    siesta_of,
    supernode_of,
):
    width = diag_inv.shape[-1]
    local_rows, anc_rows = anc_inv.shape[1:]
    blk_count = ancestors.shape[1]
    grid_count = lax.axis_size("grid")
    pole_count = lax.axis_size("pole")
    chunk = (blk_count + 1) * width // pole_count
    slot_cap = (width + grid_count - 1) // grid_count
    direct = (
        slot_cap * grid_count == width and slot_cap % 32 == 0 and chunk == LANES * 3 // 2
    )
    slots = slot_cap + (0 if direct else SUB if slot_cap % SUB == 0 else 1)

    dest_owner = siesta_of // width
    send_slot = dest_owner * slots + ranks(dest_owner, jnp.arange(width))
    source_dev = supernode_of // width
    recv_slot = source_dev * slots + ranks(source_dev, supernode_of)

    spread = grid_count * SUB
    if local_rows % spread == 0 and width % spread == 0:
        shares = grid_count
        mine = anc_inv[0].reshape(local_rows // spread, grid_count, SUB, anc_rows)
        mine = mine.transpose(1, 0, 2, 3).reshape(grid_count, local_rows // grid_count, anc_rows)
        table = jnp.broadcast_to(
            jnp.pad(ancestors, ((0, 0), (0, LANES - blk_count))).astype(jnp.bfloat16)[None],
            (grid_count, local_rows // grid_count, LANES),
        )
        sent = jnp.concatenate([mine, table], axis=2)
        held = lax.all_to_all(sent, "grid", split_axis=0, concat_axis=0, tiled=True)
        all_anc = held[:, 0, anc_rows : anc_rows + blk_count].astype(jnp.int32)
        rows = width // grid_count
        chosen = pl.pallas_call(
            functools.partial(select_kernel, width, rows, blk_count),
            out_shape=jax.ShapeDtypeStruct(
                (grid_count, blk_count * rows, blk_count * width), jnp.bfloat16
            ),
            in_specs=[sspec(), vspec()],
            out_specs=vspec(),
            name="select",
        )(all_anc, invmem(held.reshape(local_rows, anc_rows + LANES)))
        sub_block = lax.all_to_all(chosen, "grid", split_axis=0, concat_axis=0, tiled=True)
    else:
        shares = 1
        gathered = lax.all_gather(anc_inv[0], "grid", axis=0, tiled=True)
        blocks = gathered.reshape(anc_rows // width, width, anc_rows // width, width)
        sub_block = jnp.take(jnp.take(blocks, ancestors[0], axis=0), ancestors[0], axis=2)
    sub_block = sub_block.reshape(blk_count * width, blk_count * width)

    if direct:
        factor, diag, inter = factor_cols[0, 0], diag_inv[0, 0], intersection[0]
        square = jax.ShapeDtypeStruct((width, width), jnp.bfloat16)
        lower, turned, diag, inter = pl.pallas_call(
            order_kernel,
            out_shape=(
                jax.ShapeDtypeStruct((blk_count * width, width), jnp.bfloat16),
                jax.ShapeDtypeStruct((width, blk_count * width), jnp.bfloat16),
                square,
                square,
            ),
            in_specs=[sspec()] + [vspec()] * 4,
            out_specs=(vspec(),) * 4,
            name="order",
        )(counts, send_slot[None], factor, diag, inter)
        rows = slot_cap * 3 // 2 + SUB
        coded = pl.pallas_call(
            functools.partial(encode_kernel, shares, chunk),
            out_shape=jax.ShapeDtypeStruct((pole_count * grid_count, rows, LANES), jnp.int16),
            in_specs=[sspec()] * 3 + [vspec()] * 5,
            out_specs=vspec(),
            scratch_shapes=[VMEM((blk_count * width, blk_count * width), jnp.float32)],
            name="encode",
        )(hpattern, pole_w, pole_z, invmem(sub_block), *map(invmem, (lower, turned, diag, inter)))
        arrived = lax.all_to_all(
            coded, ("pole", "grid"), split_axis=0, concat_axis=0, tiled=True
        )
        odd = (lax.axis_index("pole") & 1).astype(jnp.int32)[None]
        half = jax.ShapeDtypeStruct((chunk, width), jnp.bfloat16)
        density, energy, electrons = pl.pallas_call(
            functools.partial(decode_kernel, grid_count, slot_cap),
            out_shape=(half, half, jax.ShapeDtypeStruct((1, 1), jnp.float32)),
            in_specs=[sspec(), vspec(), vspec()],
            out_specs=(vspec(), vspec(), sspec()),
            scratch_shapes=[
                VMEM((width, 2 * LANES), jnp.bfloat16),
                VMEM((width // 2, 2 * LANES), jnp.bfloat16),
            ],
            name="decode",
        )(odd, recv_slot[None], invmem(arrived))
        return (density.T, energy.T, electrons[0, 0])

    stack = pl.pallas_call(
        functools.partial(columns_kernel, shares, chunk),
        out_shape=jax.ShapeDtypeStruct((pole_count, chunk + SUB, width), jnp.float32),
        in_specs=[sspec()] * 4 + [vspec()] * 4,
        out_specs=vspec(),
        scratch_shapes=[VMEM((blk_count * width, width), jnp.float32)],
        name="columns",
    )(
        counts,
        hpattern,
        pole_w,
        pole_z,
        invmem(sub_block),
        factor_cols[0, 0],
        diag_inv[0, 0],
        intersection[0],
    )
    stack = lax.all_to_all(stack, "pole", split_axis=0, concat_axis=0, tiled=True)

    total = grid_count * slots
    placed = pl.pallas_call(
        functools.partial(place_kernel, slot_cap, grid_count),
        out_shape=jax.ShapeDtypeStruct((total, 2 * chunk), jnp.bfloat16),
        in_specs=[vspec(), vspec()],
        out_specs=vspec(),
        name="place",
    )(send_slot[None], invmem(stack))
    arrived = lax.all_to_all(
        placed.reshape(grid_count, slots, 2 * chunk),
        "grid",
        split_axis=0,
        concat_axis=0,
        tiled=True,
    )
    density, energy, electrons = pl.pallas_call(
        functools.partial(pickup_kernel, slot_cap, grid_count),
        out_shape=(
            jax.ShapeDtypeStruct((chunk, width), jnp.bfloat16),
            jax.ShapeDtypeStruct((chunk, width), jnp.bfloat16),
            jax.ShapeDtypeStruct((1, 1), jnp.float32),
        ),
        in_specs=[vspec(), vspec()],
        out_specs=(vspec(), vspec(), sspec()),
        name="pickup",
    )(recv_slot[None], invmem(arrived.reshape(total, 2 * chunk)))
    return (density.T, energy.T, electrons[0, 0])


def solution(mesh):
    placed = (
        P("pole", "grid", None),
        P("pole", "grid", None, None, None),
        P("pole", "grid", None, None),
        P("grid", None, None),
        P("pole"),
        P("pole"),
        P("grid", None),
        P("grid"),
        P("grid", None),
        P("grid"),
        P("grid"),
    )
    return jax.shard_map(
        body,
        mesh=mesh,
        in_specs=placed,
        out_specs=(P("grid", "pole"), P("grid", "pole"), P()),
        check_vma=False,
    )
```

```python
import functools

import jax
import jax.numpy as jnp
from jax import lax
from jax.experimental import pallas as pl
from jax.experimental.pallas import tpu as pltpu
from jax.sharding import PartitionSpec as P

VMEM = pltpu.VMEM
SMEM = pltpu.SMEM
LANES = 128
SUB = 8
TINY = 1e-30
FINE = 64.0
STEPS = 32760.0


def invmem(x):
    return pltpu.with_memory_space_constraint(x, VMEM)


def vspec():
    return pl.BlockSpec(memory_space=VMEM)


def hspec():
    return pl.BlockSpec(memory_space=pltpu.HBM)


def sspec():
    return pl.BlockSpec(memory_space=SMEM)


def pack_kernel(table_ref, rows_ref, out_ref, sems):
    stretches, _, _, width = rows_ref.shape
    copies = [
        pltpu.make_async_copy(
            rows_ref.at[c], out_ref.at[:, c * SUB : (c + 1) * SUB, :width], sems.at[c]
        )
        for c in range(stretches)
    ]
    for copy in copies:
        copy.start()
    shares, rows, lanes = out_ref.shape
    lane = lax.broadcasted_iota(jnp.int32, (rows, lanes - width), 1)
    table = jnp.zeros((rows, lanes - width), jnp.float32)
    for m in range(table_ref.shape[1]):
        table = jnp.where(lane == m, table_ref[0, m].astype(jnp.float32), table)
    table = table.astype(jnp.bfloat16)
    for j in range(shares):
        out_ref[j, :, width:] = table
    for copy in copies:
        copy.wait()


def select_kernel(width, blk_count, held_ref, out_ref, sems):
    dests, picked, _ = out_ref.shape
    rows = picked // blk_count
    local = held_ref.shape[0] // dests
    tail = held_ref.shape[1] - LANES
    lane = lax.broadcasted_iota(jnp.int32, (1, LANES), 1)
    copies = []
    for dest in range(dests):
        entry = held_ref[dest * local : (dest + 1) * local, tail:].astype(jnp.float32)[:1]
        table = [
            jnp.sum(jnp.where(lane == m, entry, 0.0)).astype(jnp.int32) for m in range(blk_count)
        ]
        for m in range(blk_count):
            row_at = pl.multiple_of(table[m] * rows, rows)
            for n in range(blk_count):
                col_at = pl.multiple_of(table[n] * width, width)
                copy = pltpu.make_async_copy(
                    held_ref.at[pl.ds(row_at, rows), pl.ds(col_at, width)],
                    out_ref.at[dest, m * rows : (m + 1) * rows, n * width : (n + 1) * width],
                    sems.at[dest, m, n],
                )
                copy.start()
                copies.append(copy)
    for copy in copies:
        copy.wait()


def columns_kernel(
    shares,
    chunk,
    counts_ref,
    hpattern_ref,
    weight_ref,
    energy_ref,
    rows_ref,
    factor_ref,
    diag_ref,
    inter_ref,
    out_ref,
    off_ref,
):
    blk_count, width, _ = factor_ref.shape
    parts = [
        factor_ref[m] * (m < counts_ref[0]).astype(jnp.float32).astype(jnp.bfloat16)
        for m in range(blk_count)
    ]
    lower = jnp.concatenate(parts, axis=0)
    product = jnp.dot(rows_ref[...], lower, preferred_element_type=jnp.float32)
    per_blk = width // shares
    for m in range(blk_count):
        scale = hpattern_ref[0, m].astype(jnp.float32)
        for j in range(shares):
            for c in range(per_blk // SUB):
                at = (j * blk_count + m) * per_blk + c * SUB
                piece = -product[at : at + SUB]
                row = m * width + (c * shares + j) * SUB
                off_ref[row : row + SUB, :] = piece
                place = width + row
                out_ref[place // chunk, place % chunk : place % chunk + SUB, :] = piece * scale
    off = off_ref[...]
    high = off.astype(jnp.bfloat16)
    rest = off - high.astype(jnp.float32)
    mid = rest.astype(jnp.bfloat16)
    low = (rest - mid.astype(jnp.float32)).astype(jnp.bfloat16)
    contract = functools.partial(
        lax.dot_general,
        dimension_numbers=(((0,), (0,)), ((), ())),
        preferred_element_type=jnp.float32,
    )
    product_sum = contract(lower, low) + contract(lower, mid) + contract(lower, high)
    diag_block = diag_ref[...].astype(jnp.float32) - product_sum
    at = 0
    while at < width:
        size = min(chunk - at % chunk, width - at)
        out_ref[at // chunk, at % chunk : at % chunk + size, :] = diag_block[at : at + size]
        at += size
    count = weight_ref[0] * jnp.sum(diag_block * inter_ref[...].astype(jnp.float32))
    row_id = lax.broadcasted_iota(jnp.int32, (SUB, width), 0)
    extra = jnp.where(row_id == 0, weight_ref[0], jnp.where(row_id == 1, energy_ref[0], count))
    for q in range(out_ref.shape[0]):
        out_ref[q, chunk : chunk + SUB, :] = extra


def place_kernel(slot_cap, dests, slot_ref, stack_ref, out_ref):
    poles, rows, width = stack_ref.shape
    chunk = rows - SUB
    dens = jnp.zeros((chunk, width), jnp.float32)
    energy = jnp.zeros((chunk, width), jnp.float32)
    count = jnp.zeros((1, width), jnp.float32)
    for p in range(poles):
        term = stack_ref[p, :chunk, :]
        dens = dens + stack_ref[p, chunk : chunk + 1, :] * term
        energy = energy + stack_ref[p, chunk + 1 : chunk + 2, :] * term
        count = count + stack_ref[p, chunk + 2 : chunk + 3, :]
    both = jnp.concatenate([dens, energy], axis=0).astype(jnp.bfloat16)
    total, lanes = out_ref.shape
    slots = total // dests
    one_hot = (lax.broadcasted_iota(jnp.int32, (total, width), 0) == slot_ref[...]).astype(
        jnp.bfloat16
    )
    placed = lax.dot_general(
        one_hot, both, (((1,), (1,)), ((), ())), preferred_element_type=jnp.float32
    )
    own = count[:, 0:1]
    high = own.astype(jnp.bfloat16).astype(jnp.float32)
    rest = own - high
    mid = rest.astype(jnp.bfloat16).astype(jnp.float32)
    lane = lax.broadcasted_iota(jnp.int32, (1, lanes), 1)
    pieces = jnp.where(lane == 0, high, jnp.where(lane == 1, mid, rest - mid))
    pieces = jnp.where(lane < 3, pieces, 0.0)
    row = lax.broadcasted_iota(jnp.int32, (total, 1), 0)
    marked = functools.reduce(
        jnp.logical_or, [row == g * slots + slot_cap for g in range(dests)]
    )
    out_ref[...] = jnp.where(marked, pieces, placed).astype(jnp.bfloat16)


def pickup_kernel(slot_cap, dests, slot_ref, recv_ref, dens_ref, energy_ref, count_ref):
    total, lanes = recv_ref.shape
    slots = total // dests
    chunk = lanes // 2
    width = slot_ref.shape[1]
    recv = recv_ref[...]
    one_hot = (lax.broadcasted_iota(jnp.int32, (total, width), 0) == slot_ref[...]).astype(
        jnp.bfloat16
    )
    out = lax.dot_general(
        recv, one_hot, (((0,), (0,)), ((), ())), preferred_element_type=jnp.float32
    ).astype(jnp.bfloat16)
    dens_ref[...] = out[:chunk]
    energy_ref[...] = out[chunk:]
    row = lax.broadcasted_iota(jnp.int32, (total, 1), 0)
    marked = functools.reduce(
        jnp.logical_or, [row == g * slots + slot_cap for g in range(dests)]
    )
    pieces = jnp.where(marked, recv[:, :LANES].astype(jnp.float32), 0.0)
    count_ref[0, 0] = jnp.sum(pieces)


def order_kernel(
    counts_ref, slot_ref, factor_ref, diag_ref, inter_ref, lower_ref, turned_ref, diag_out, inter_out
):
    blk_count, width, _ = factor_ref.shape
    one_hot = (lax.broadcasted_iota(jnp.int32, (width, width), 0) == slot_ref[...]).astype(
        jnp.bfloat16
    )

    def turn(matrix):
        return lax.dot_general(
            one_hot, matrix, (((1,), (1,)), ((), ())), preferred_element_type=jnp.float32
        ).astype(jnp.bfloat16)

    for m in range(blk_count):
        live = (m < counts_ref[0]).astype(jnp.float32).astype(jnp.bfloat16)
        block = factor_ref[m] * live
        lower_ref[m * width : (m + 1) * width, :] = block
        turned_ref[:, m * width : (m + 1) * width] = turn(block)
    diag_out[...] = turn(diag_ref[...])
    inter_out[...] = turn(inter_ref[...])


def halved_sum(values):
    while values.shape[0] > SUB:
        half = values.shape[0] // 2
        values = values[:half] + values[half:]
    while values.shape[1] > LANES:
        half = values.shape[1] // 2
        values = values[:, :half] + values[:, half:]
    return jnp.sum(values)


def whole(value):
    return value.astype(jnp.int32).astype(jnp.int16)


def fold_half(tile, right):
    rows = tile.shape[0] // 2
    lane = lax.broadcasted_iota(jnp.int32, (rows, LANES), 1)
    top, bottom = tile[:rows], tile[rows:]
    if right:
        return jnp.where(lane < LANES // 2, pltpu.roll(top, LANES // 2, 1), bottom)
    return jnp.where(lane < LANES // 2, top, pltpu.roll(bottom, LANES // 2, 1))


def encode_kernel(
    shares,
    chunk,
    hpattern_ref,
    weight_ref,
    energy_ref,
    rows_ref,
    lower_ref,
    turned_ref,
    diag_ref,
    inter_ref,
    out_ref,
    sorted_ref,
):
    blk_count = hpattern_ref.shape[1]
    width = lower_ref.shape[1]
    per_blk = width // shares
    for m in range(blk_count):
        for j in range(shares):
            at = (j * blk_count + m) * per_blk
            piece = rows_ref[at : at + per_blk, :].astype(jnp.float32)
            for c in range(per_blk // SUB):
                row = m * width + (c * shares + j) * SUB
                sorted_ref[row : row + SUB, :] = piece[c * SUB : (c + 1) * SUB]
    off = -lax.dot_general(
        turned_ref[...],
        sorted_ref[...].astype(jnp.bfloat16),
        (((1,), (1,)), ((), ())),
        preferred_element_type=jnp.float32,
    )
    high = off.astype(jnp.bfloat16)
    rest = off - high.astype(jnp.float32)
    mid = rest.astype(jnp.bfloat16)
    low = (rest - mid.astype(jnp.float32)).astype(jnp.bfloat16)
    lower = lower_ref[...]
    diag = diag_ref[...].astype(jnp.float32) - (
        jnp.dot(low, lower, preferred_element_type=jnp.float32)
        + jnp.dot(mid, lower, preferred_element_type=jnp.float32)
        + jnp.dot(high, lower, preferred_element_type=jnp.float32)
    )
    count = weight_ref[0] * halved_sum(diag * inter_ref[...].astype(jnp.float32))
    parts = [diag] + [
        off[:, m * width : (m + 1) * width] * hpattern_ref[0, m].astype(jnp.float32)
        for m in range(blk_count)
    ]
    values = jnp.concatenate(parts, axis=1)
    largest = jnp.max(jnp.abs(values), axis=0, keepdims=True)
    level = jnp.ceil(jnp.log2(jnp.maximum(largest, TINY)) * FINE)
    codes = jnp.floor(values * (jnp.exp2(level * (-1.0 / FINE)) * STEPS) + 0.5)

    row_id = lax.broadcasted_iota(jnp.int32, (SUB, LANES), 0)
    lane_id = lax.broadcasted_iota(jnp.int32, (SUB, LANES), 1)
    full_count = jnp.full((SUB, LANES), count)
    power = jnp.ceil(jnp.log2(jnp.maximum(jnp.abs(full_count), TINY)))
    scaled = full_count * jnp.exp2(-power) * 2.0**14
    scaled_high = jnp.floor(scaled)
    extra = jnp.where(
        lane_id == 0,
        power,
        jnp.where(lane_id == 1, scaled_high, jnp.floor((scaled - scaled_high) * 2.0**15)),
    )
    for at, scalar in ((2, weight_ref[0]), (4, energy_ref[0])):
        grown = jnp.full((SUB, LANES), scalar) * 2.0**13
        grown_high = jnp.floor(grown)
        extra = jnp.where(row_id == at, grown_high, extra)
        extra = jnp.where(row_id == at + 1, (grown - grown_high) * 2.0**15, extra)

    dests, _, _ = out_ref.shape
    pole_count = values.shape[1] // chunk
    owners = dests // pole_count
    cap = width // owners
    half = cap // 2
    for q in range(pole_count):
        right = q % 2 == 1
        full_at = (q * chunk + LANES - 1) // LANES * LANES
        half_at = full_at - LANES if right else full_at + LANES
        level_half = level[:, half_at : half_at + LANES]
        lane = lax.broadcasted_iota(jnp.int32, (1, LANES), 1)
        other = pltpu.roll(jnp.broadcast_to(level_half, (SUB, LANES)), LANES // 2, 1)[:1]
        level_half = jnp.where((lane < LANES // 2) == (not right), level_half, other)
        tail = jnp.where(
            row_id == 0,
            level[:, full_at : full_at + LANES],
            jnp.where(row_id == 1, level_half, extra),
        )
        tail = whole(tail)
        for g in range(owners):
            rows = slice(g * cap, (g + 1) * cap)
            d = q * owners + g
            out_ref[d, :cap, :] = whole(codes[rows, full_at : full_at + LANES])
            out_ref[d, cap : cap + half, :] = whole(
                fold_half(codes[rows, half_at : half_at + LANES], right)
            )
            out_ref[d, cap + half :, :] = tail


def decode_kernel(
    owners, cap, odd_ref, slot_ref, recv_ref, dens_ref, energy_ref, count_ref, full_ref, half_ref
):
    dests, rows, _ = recv_ref.shape
    poles = dests // owners
    half = cap // 2
    width = slot_ref.shape[1]
    count = jnp.zeros((1, 1), jnp.float32)
    lost = jnp.zeros((1, 1), jnp.float32)
    for g in range(owners):
        sums = [0.0, 0.0, 0.0, 0.0]
        for p in range(poles):
            piece = recv_ref[p * owners + g].astype(jnp.int32).astype(jnp.float32)
            extra = piece[cap + half :]
            scale = jnp.exp2(extra[:2] * (1.0 / FINE)) * (1.0 / STEPS)
            weight = extra[2:3] * 2.0**-13 + extra[3:4] * 2.0**-28
            energy = extra[4:5] * 2.0**-13 + extra[5:6] * 2.0**-28
            full = piece[:cap] * scale[:1]
            rest = piece[cap : cap + half] * scale[1:2]
            for at, term in enumerate(
                (weight * full, energy * full, weight * rest, energy * rest)
            ):
                sums[at] = sums[at] + term
            own = extra[6:7]
            own = (own[:, 1:2] * 2.0**-14 + own[:, 2:3] * 2.0**-29) * jnp.exp2(own[:, 0:1])
            grown = count + own
            part = grown - count
            lost = lost + ((count - (grown - part)) + (own - part))
            count = grown
        full_ref[g * cap : (g + 1) * cap, :LANES] = sums[0].astype(jnp.bfloat16)
        full_ref[g * cap : (g + 1) * cap, LANES:] = sums[1].astype(jnp.bfloat16)
        half_ref[g * half : (g + 1) * half, :LANES] = sums[2].astype(jnp.bfloat16)
        half_ref[g * half : (g + 1) * half, LANES:] = sums[3].astype(jnp.bfloat16)
    count_ref[0, 0] = jnp.sum(count + lost)

    slot = slot_ref[...]
    pick = (lax.broadcasted_iota(jnp.int32, (owners * cap, width), 0) == slot).astype(jnp.bfloat16)
    row = lax.broadcasted_iota(jnp.int32, (owners * half, width), 0)
    owner = slot // cap
    within = slot - owner * cap
    place = owner * half + within
    left = (row == jnp.where(within < half, place, -1)).astype(jnp.bfloat16)
    right = (row == jnp.where(within >= half, place - half, -1)).astype(jnp.bfloat16)

    def take(held, chosen):
        return lax.dot_general(
            held, chosen, (((0,), (0,)), ((), ())), preferred_element_type=jnp.float32
        )

    full = take(full_ref[...], pick).astype(jnp.bfloat16)
    by_left = take(half_ref[...], left)
    by_right = take(half_ref[...], right)
    mid = LANES // 2
    full_at = pl.multiple_of(odd_ref[0] * mid, mid)
    half_at = pl.multiple_of((1 - odd_ref[0]) * LANES, mid)
    for at, ref in ((0, dens_ref), (LANES, energy_ref)):
        ref[pl.ds(full_at, LANES), :] = full[at : at + LANES]
        joined = by_left[at : at + mid] + by_right[at + mid : at + LANES]
        ref[pl.ds(half_at, mid), :] = joined.astype(jnp.bfloat16)


def ranks(own, order):
    same = own[:, None] == own[None, :]
    earlier = order[None, :] < order[:, None]
    return jnp.sum((same & earlier).astype(jnp.int32), axis=1)


def body(
    anc_inv,
    factor_cols,
    diag_inv,
    intersection,
    pole_w,
    pole_z,
    ancestors,
    counts,
    hpattern,
    siesta_of,
    supernode_of,
):
    width = diag_inv.shape[-1]
    local_rows, anc_rows = anc_inv.shape[1:]
    blk_count = ancestors.shape[1]
    grid_count = lax.axis_size("grid")
    pole_count = lax.axis_size("pole")
    chunk = (blk_count + 1) * width // pole_count
    slot_cap = (width + grid_count - 1) // grid_count
    direct = (
        slot_cap * grid_count == width and slot_cap % 32 == 0 and chunk == LANES * 3 // 2
    )
    slots = slot_cap + (0 if direct else SUB if slot_cap % SUB == 0 else 1)

    dest_owner = siesta_of // width
    send_slot = dest_owner * slots + ranks(dest_owner, jnp.arange(width))
    source_dev = supernode_of // width
    recv_slot = source_dev * slots + ranks(source_dev, supernode_of)

    spread = grid_count * SUB
    if local_rows % spread == 0 and width % spread == 0:
        shares = grid_count
        stretches = local_rows // spread
        sent = pl.pallas_call(
            pack_kernel,
            out_shape=VMEM(
                (grid_count, local_rows // grid_count, anc_rows + LANES), jnp.bfloat16
            ),
            in_specs=[sspec(), hspec()],
            scratch_shapes=[pltpu.SemaphoreType.DMA((stretches,))],
            name="pack",
        )(ancestors, anc_inv[0].reshape(stretches, grid_count, SUB, anc_rows))
        held = lax.all_to_all(sent, "grid", split_axis=0, concat_axis=0, tiled=True)
        rows = width // grid_count
        chosen = pl.pallas_call(
            functools.partial(select_kernel, width, blk_count),
            out_shape=jax.ShapeDtypeStruct(
                (grid_count, blk_count * rows, blk_count * width), jnp.bfloat16
            ),
            in_specs=[vspec()],
            out_specs=hspec(),
            scratch_shapes=[pltpu.SemaphoreType.DMA((grid_count, blk_count, blk_count))],
            name="select",
        )(invmem(held.reshape(local_rows, anc_rows + LANES)))
        sub_block = lax.all_to_all(chosen, "grid", split_axis=0, concat_axis=0, tiled=True)
    else:
        shares = 1
        gathered = lax.all_gather(anc_inv[0], "grid", axis=0, tiled=True)
        blocks = gathered.reshape(anc_rows // width, width, anc_rows // width, width)
        sub_block = jnp.take(jnp.take(blocks, ancestors[0], axis=0), ancestors[0], axis=2)
    sub_block = sub_block.reshape(blk_count * width, blk_count * width)

    if direct:
        factor, diag, inter = factor_cols[0, 0], diag_inv[0, 0], intersection[0]
        square = jax.ShapeDtypeStruct((width, width), jnp.bfloat16)
        lower, turned, diag, inter = pl.pallas_call(
            order_kernel,
            out_shape=(
                VMEM((blk_count * width, width), jnp.bfloat16),
                VMEM((width, blk_count * width), jnp.bfloat16),
                VMEM((width, width), jnp.bfloat16),
                VMEM((width, width), jnp.bfloat16),
            ),
            in_specs=[sspec()] + [vspec()] * 4,
            name="order",
        )(counts, send_slot[None], factor, diag, inter)
        rows = slot_cap * 3 // 2 + SUB
        coded = pl.pallas_call(
            functools.partial(encode_kernel, shares, chunk),
            out_shape=jax.ShapeDtypeStruct((pole_count * grid_count, rows, LANES), jnp.int16),
            in_specs=[sspec()] * 3 + [vspec()] * 5,
            out_specs=vspec(),
            scratch_shapes=[VMEM((blk_count * width, blk_count * width), jnp.float32)],
            name="encode",
        )(hpattern, pole_w, pole_z, invmem(sub_block), *map(invmem, (lower, turned, diag, inter)))
        arrived = lax.all_to_all(
            coded, ("pole", "grid"), split_axis=0, concat_axis=0, tiled=True
        )
        odd = (lax.axis_index("pole") & 1).astype(jnp.int32)[None]
        half = jax.ShapeDtypeStruct((chunk, width), jnp.bfloat16)
        density, energy, electrons = pl.pallas_call(
            functools.partial(decode_kernel, grid_count, slot_cap),
            out_shape=(half, half, jax.ShapeDtypeStruct((1, 1), jnp.float32)),
            in_specs=[sspec(), vspec(), vspec()],
            out_specs=(vspec(), vspec(), sspec()),
            scratch_shapes=[
                VMEM((width, 2 * LANES), jnp.bfloat16),
                VMEM((width // 2, 2 * LANES), jnp.bfloat16),
            ],
            name="decode",
        )(odd, recv_slot[None], invmem(arrived))
        return (density.T, energy.T, electrons[0, 0])

    stack = pl.pallas_call(
        functools.partial(columns_kernel, shares, chunk),
        out_shape=jax.ShapeDtypeStruct((pole_count, chunk + SUB, width), jnp.float32),
        in_specs=[sspec()] * 4 + [vspec()] * 4,
        out_specs=vspec(),
        scratch_shapes=[VMEM((blk_count * width, width), jnp.float32)],
        name="columns",
    )(
        counts,
        hpattern,
        pole_w,
        pole_z,
        invmem(sub_block),
        factor_cols[0, 0],
        diag_inv[0, 0],
        intersection[0],
    )
    stack = lax.all_to_all(stack, "pole", split_axis=0, concat_axis=0, tiled=True)

    total = grid_count * slots
    placed = pl.pallas_call(
        functools.partial(place_kernel, slot_cap, grid_count),
        out_shape=jax.ShapeDtypeStruct((total, 2 * chunk), jnp.bfloat16),
        in_specs=[vspec(), vspec()],
        out_specs=vspec(),
        name="place",
    )(send_slot[None], invmem(stack))
    arrived = lax.all_to_all(
        placed.reshape(grid_count, slots, 2 * chunk),
        "grid",
        split_axis=0,
        concat_axis=0,
        tiled=True,
    )
    density, energy, electrons = pl.pallas_call(
        functools.partial(pickup_kernel, slot_cap, grid_count),
        out_shape=(
            jax.ShapeDtypeStruct((chunk, width), jnp.bfloat16),
            jax.ShapeDtypeStruct((chunk, width), jnp.bfloat16),
            jax.ShapeDtypeStruct((1, 1), jnp.float32),
        ),
        in_specs=[vspec(), vspec()],
        out_specs=(vspec(), vspec(), sspec()),
        name="pickup",
    )(recv_slot[None], invmem(arrived.reshape(total, 2 * chunk)))
    return (density.T, energy.T, electrons[0, 0])


def solution(mesh):
    placed = (
        P("pole", "grid", None),
        P("pole", "grid", None, None, None),
        P("pole", "grid", None, None),
        P("grid", None, None),
        P("pole"),
        P("pole"),
        P("grid", None),
        P("grid"),
        P("grid", None),
        P("grid"),
        P("grid"),
    )
    return jax.shard_map(
        body,
        mesh=mesh,
        in_specs=placed,
        out_specs=(P("grid", "pole"), P("grid", "pole"), P()),
        check_vma=False,
    )
```

```python
import functools

import jax
import jax.numpy as jnp
from jax import lax
from jax.experimental import pallas as pl
from jax.experimental.pallas import tpu as pltpu
from jax.sharding import PartitionSpec as P

VMEM = pltpu.VMEM
SMEM = pltpu.SMEM
LANES = 128
SUB = 8
TINY = 1e-30
FINE = 64.0
STEPS = 32760.0


def invmem(x):
    return pltpu.with_memory_space_constraint(x, VMEM)


def vspec():
    return pl.BlockSpec(memory_space=VMEM)


def hspec():
    return pl.BlockSpec(memory_space=pltpu.HBM)


def sspec():
    return pl.BlockSpec(memory_space=SMEM)


def pack_kernel(table_hbm, rows_ref, out_ref, table_ref, sems):
    stretches, _, _, width = rows_ref.shape
    copies = [
        pltpu.make_async_copy(
            rows_ref.at[c], out_ref.at[:, c * SUB : (c + 1) * SUB, :width], sems.at[c]
        )
        for c in range(stretches)
    ]
    for copy in copies:
        copy.start()
    pltpu.sync_copy(table_hbm, table_ref)
    shares, rows, lanes = out_ref.shape
    lane = lax.broadcasted_iota(jnp.int32, (rows, lanes - width), 1)
    table = jnp.zeros((rows, lanes - width), jnp.float32)
    for m in range(table_ref.shape[1]):
        table = jnp.where(lane == m, table_ref[0, m].astype(jnp.float32), table)
    table = table.astype(jnp.bfloat16)
    for j in range(shares):
        out_ref[j, :, width:] = table
    for copy in copies:
        copy.wait()


def select_kernel(width, blk_count, held_ref, out_ref, sems):
    dests, picked, _ = out_ref.shape
    rows = picked // blk_count
    local = held_ref.shape[0] // dests
    tail = held_ref.shape[1] - LANES
    lane = lax.broadcasted_iota(jnp.int32, (1, LANES), 1)
    copies = []
    for dest in range(dests):
        entry = held_ref[dest * local : (dest + 1) * local, tail:].astype(jnp.float32)[:1]
        table = [
            jnp.sum(jnp.where(lane == m, entry, 0.0)).astype(jnp.int32) for m in range(blk_count)
        ]
        for m in range(blk_count):
            row_at = pl.multiple_of(table[m] * rows, rows)
            for n in range(blk_count):
                col_at = pl.multiple_of(table[n] * width, width)
                copy = pltpu.make_async_copy(
                    held_ref.at[pl.ds(row_at, rows), pl.ds(col_at, width)],
                    out_ref.at[dest, m * rows : (m + 1) * rows, n * width : (n + 1) * width],
                    sems.at[dest, m, n],
                )
                copy.start()
                copies.append(copy)
    for copy in copies:
        copy.wait()


def columns_kernel(
    shares,
    chunk,
    counts_ref,
    hpattern_ref,
    weight_ref,
    energy_ref,
    rows_ref,
    factor_ref,
    diag_ref,
    inter_ref,
    out_ref,
    off_ref,
):
    blk_count, width, _ = factor_ref.shape
    parts = [
        factor_ref[m] * (m < counts_ref[0]).astype(jnp.float32).astype(jnp.bfloat16)
        for m in range(blk_count)
    ]
    lower = jnp.concatenate(parts, axis=0)
    product = jnp.dot(rows_ref[...], lower, preferred_element_type=jnp.float32)
    per_blk = width // shares
    for m in range(blk_count):
        scale = hpattern_ref[0, m].astype(jnp.float32)
        for j in range(shares):
            for c in range(per_blk // SUB):
                at = (j * blk_count + m) * per_blk + c * SUB
                piece = -product[at : at + SUB]
                row = m * width + (c * shares + j) * SUB
                off_ref[row : row + SUB, :] = piece
                place = width + row
                out_ref[place // chunk, place % chunk : place % chunk + SUB, :] = piece * scale
    off = off_ref[...]
    high = off.astype(jnp.bfloat16)
    rest = off - high.astype(jnp.float32)
    mid = rest.astype(jnp.bfloat16)
    low = (rest - mid.astype(jnp.float32)).astype(jnp.bfloat16)
    contract = functools.partial(
        lax.dot_general,
        dimension_numbers=(((0,), (0,)), ((), ())),
        preferred_element_type=jnp.float32,
    )
    product_sum = contract(lower, low) + contract(lower, mid) + contract(lower, high)
    diag_block = diag_ref[...].astype(jnp.float32) - product_sum
    at = 0
    while at < width:
        size = min(chunk - at % chunk, width - at)
        out_ref[at // chunk, at % chunk : at % chunk + size, :] = diag_block[at : at + size]
        at += size
    count = weight_ref[0] * jnp.sum(diag_block * inter_ref[...].astype(jnp.float32))
    row_id = lax.broadcasted_iota(jnp.int32, (SUB, width), 0)
    extra = jnp.where(row_id == 0, weight_ref[0], jnp.where(row_id == 1, energy_ref[0], count))
    for q in range(out_ref.shape[0]):
        out_ref[q, chunk : chunk + SUB, :] = extra


def place_kernel(slot_cap, dests, slot_ref, stack_ref, out_ref):
    poles, rows, width = stack_ref.shape
    chunk = rows - SUB
    dens = jnp.zeros((chunk, width), jnp.float32)
    energy = jnp.zeros((chunk, width), jnp.float32)
    count = jnp.zeros((1, width), jnp.float32)
    for p in range(poles):
        term = stack_ref[p, :chunk, :]
        dens = dens + stack_ref[p, chunk : chunk + 1, :] * term
        energy = energy + stack_ref[p, chunk + 1 : chunk + 2, :] * term
        count = count + stack_ref[p, chunk + 2 : chunk + 3, :]
    both = jnp.concatenate([dens, energy], axis=0).astype(jnp.bfloat16)
    total, lanes = out_ref.shape
    slots = total // dests
    one_hot = (lax.broadcasted_iota(jnp.int32, (total, width), 0) == slot_ref[...]).astype(
        jnp.bfloat16
    )
    placed = lax.dot_general(
        one_hot, both, (((1,), (1,)), ((), ())), preferred_element_type=jnp.float32
    )
    own = count[:, 0:1]
    high = own.astype(jnp.bfloat16).astype(jnp.float32)
    rest = own - high
    mid = rest.astype(jnp.bfloat16).astype(jnp.float32)
    lane = lax.broadcasted_iota(jnp.int32, (1, lanes), 1)
    pieces = jnp.where(lane == 0, high, jnp.where(lane == 1, mid, rest - mid))
    pieces = jnp.where(lane < 3, pieces, 0.0)
    row = lax.broadcasted_iota(jnp.int32, (total, 1), 0)
    marked = functools.reduce(
        jnp.logical_or, [row == g * slots + slot_cap for g in range(dests)]
    )
    out_ref[...] = jnp.where(marked, pieces, placed).astype(jnp.bfloat16)


def pickup_kernel(slot_cap, dests, slot_ref, recv_ref, dens_ref, energy_ref, count_ref):
    total, lanes = recv_ref.shape
    slots = total // dests
    chunk = lanes // 2
    width = slot_ref.shape[1]
    recv = recv_ref[...]
    one_hot = (lax.broadcasted_iota(jnp.int32, (total, width), 0) == slot_ref[...]).astype(
        jnp.bfloat16
    )
    out = lax.dot_general(
        recv, one_hot, (((0,), (0,)), ((), ())), preferred_element_type=jnp.float32
    ).astype(jnp.bfloat16)
    dens_ref[...] = out[:chunk]
    energy_ref[...] = out[chunk:]
    row = lax.broadcasted_iota(jnp.int32, (total, 1), 0)
    marked = functools.reduce(
        jnp.logical_or, [row == g * slots + slot_cap for g in range(dests)]
    )
    pieces = jnp.where(marked, recv[:, :LANES].astype(jnp.float32), 0.0)
    count_ref[0, 0] = jnp.sum(pieces)


def order_kernel(
    counts_ref,
    hpattern_ref,
    weight_ref,
    energy_ref,
    odd_ref,
    send_ref,
    recv_ref,
    factor_ref,
    diag_ref,
    inter_ref,
    lower_ref,
    turned_ref,
    diag_out,
    inter_out,
    info_ref,
    slots_ref,
):
    blk_count, width, _ = factor_ref.shape
    one_hot = (lax.broadcasted_iota(jnp.int32, (width, width), 0) == send_ref[...]).astype(
        jnp.bfloat16
    )

    def turn(matrix):
        return lax.dot_general(
            one_hot, matrix, (((1,), (1,)), ((), ())), preferred_element_type=jnp.float32
        ).astype(jnp.bfloat16)

    for m in range(blk_count):
        live = (m < counts_ref[0]).astype(jnp.float32).astype(jnp.bfloat16)
        block = factor_ref[m] * live
        lower_ref[m * width : (m + 1) * width, :] = block
        turned_ref[:, m * width : (m + 1) * width] = turn(block)
    diag_out[...] = turn(diag_ref[...])
    inter_out[...] = turn(inter_ref[...])

    rows, lanes = info_ref.shape
    row_id = lax.broadcasted_iota(jnp.int32, (rows, lanes), 0)
    block = lax.broadcasted_iota(jnp.int32, (rows, lanes), 1) // width
    info = jnp.ones((rows, lanes), jnp.float32)
    for m in range(blk_count):
        info = jnp.where(block == m + 1, hpattern_ref[0, m].astype(jnp.float32), info)
    info = jnp.where(row_id == 1, weight_ref[0], info)
    for at, scalar in ((2, weight_ref[0]), (4, energy_ref[0])):
        grown = jnp.full((rows, lanes), scalar) * 2.0**13
        grown_high = jnp.floor(grown)
        info = jnp.where(row_id == at, grown_high, info)
        info = jnp.where(row_id == at + 1, (grown - grown_high) * 2.0**15, info)
    info_ref[...] = info
    row_id = lax.broadcasted_iota(jnp.int32, (SUB, width), 0)
    slots_ref[...] = jnp.where(row_id == 0, recv_ref[...], odd_ref[0])


def halved_sum(values):
    while values.shape[0] > SUB:
        half = values.shape[0] // 2
        values = values[:half] + values[half:]
    while values.shape[1] > LANES:
        half = values.shape[1] // 2
        values = values[:, :half] + values[:, half:]
    return jnp.sum(values)


def whole(value):
    return value.astype(jnp.int32).astype(jnp.int16)


def fold_half(tile, right):
    rows = tile.shape[0] // 2
    lane = lax.broadcasted_iota(jnp.int32, (rows, LANES), 1)
    top, bottom = tile[:rows], tile[rows:]
    if right:
        return jnp.where(lane < LANES // 2, pltpu.roll(top, LANES // 2, 1), bottom)
    return jnp.where(lane < LANES // 2, top, pltpu.roll(bottom, LANES // 2, 1))


def encode_kernel(
    shares,
    chunk,
    rows_ref,
    lower_ref,
    turned_ref,
    diag_ref,
    inter_ref,
    info_ref,
    out_ref,
    sorted_ref,
):
    depth, width = lower_ref.shape
    blk_count = depth // width
    per_blk = width // shares
    for m in range(blk_count):
        for j in range(shares):
            at = (j * blk_count + m) * per_blk
            piece = rows_ref[at : at + per_blk, :].astype(jnp.float32)
            for c in range(per_blk // SUB):
                row = m * width + (c * shares + j) * SUB
                sorted_ref[row : row + SUB, :] = piece[c * SUB : (c + 1) * SUB]
    off = -lax.dot_general(
        turned_ref[...],
        sorted_ref[...].astype(jnp.bfloat16),
        (((1,), (1,)), ((), ())),
        preferred_element_type=jnp.float32,
    )
    high = off.astype(jnp.bfloat16)
    rest = off - high.astype(jnp.float32)
    mid = rest.astype(jnp.bfloat16)
    low = (rest - mid.astype(jnp.float32)).astype(jnp.bfloat16)
    lower = lower_ref[...]
    diag = diag_ref[...].astype(jnp.float32) - (
        jnp.dot(low, lower, preferred_element_type=jnp.float32)
        + jnp.dot(mid, lower, preferred_element_type=jnp.float32)
        + jnp.dot(high, lower, preferred_element_type=jnp.float32)
    )
    count = halved_sum(diag * inter_ref[...].astype(jnp.float32))
    values = jnp.concatenate([diag, off * info_ref[:1, width:]], axis=1)
    largest = jnp.max(jnp.abs(values), axis=0, keepdims=True)
    level = jnp.ceil(jnp.log2(jnp.maximum(largest, TINY)) * FINE)
    codes = jnp.floor(values * (jnp.exp2(level * (-1.0 / FINE)) * STEPS) + 0.5)

    row_id = lax.broadcasted_iota(jnp.int32, (SUB, LANES), 0)
    lane_id = lax.broadcasted_iota(jnp.int32, (SUB, LANES), 1)
    full_count = info_ref[1:2, :LANES] * jnp.full((SUB, LANES), count)
    power = jnp.ceil(jnp.log2(jnp.maximum(jnp.abs(full_count), TINY)))
    scaled = full_count * jnp.exp2(-power) * 2.0**14
    scaled_high = jnp.floor(scaled)
    extra = jnp.where(
        lane_id == 0,
        power,
        jnp.where(lane_id == 1, scaled_high, jnp.floor((scaled - scaled_high) * 2.0**15)),
    )
    extra = jnp.where(row_id < 6, info_ref[:, :LANES], extra)

    dests, _, _ = out_ref.shape
    pole_count = values.shape[1] // chunk
    owners = dests // pole_count
    cap = width // owners
    half = cap // 2
    for q in range(pole_count):
        right = q % 2 == 1
        full_at = (q * chunk + LANES - 1) // LANES * LANES
        half_at = full_at - LANES if right else full_at + LANES
        level_half = level[:, half_at : half_at + LANES]
        lane = lax.broadcasted_iota(jnp.int32, (1, LANES), 1)
        other = pltpu.roll(jnp.broadcast_to(level_half, (SUB, LANES)), LANES // 2, 1)[:1]
        level_half = jnp.where((lane < LANES // 2) == (not right), level_half, other)
        tail = jnp.where(
            row_id == 0,
            level[:, full_at : full_at + LANES],
            jnp.where(row_id == 1, level_half, extra),
        )
        tail = whole(tail)
        for g in range(owners):
            rows = slice(g * cap, (g + 1) * cap)
            d = q * owners + g
            out_ref[d, :cap, :] = whole(codes[rows, full_at : full_at + LANES])
            out_ref[d, cap : cap + half, :] = whole(
                fold_half(codes[rows, half_at : half_at + LANES], right)
            )
            out_ref[d, cap + half :, :] = tail


def decode_kernel(
    owners, cap, slots_ref, recv_ref, dens_ref, energy_ref, count_ref, full_ref, half_ref
):
    dests, rows, _ = recv_ref.shape
    poles = dests // owners
    half = cap // 2
    width = slots_ref.shape[1]
    count = jnp.zeros((1, 1), jnp.float32)
    lost = jnp.zeros((1, 1), jnp.float32)
    for g in range(owners):
        sums = [0.0, 0.0, 0.0, 0.0]
        for p in range(poles):
            piece = recv_ref[p * owners + g].astype(jnp.int32).astype(jnp.float32)
            extra = piece[cap + half :]
            scale = jnp.exp2(extra[:2] * (1.0 / FINE)) * (1.0 / STEPS)
            weight = extra[2:3] * 2.0**-13 + extra[3:4] * 2.0**-28
            energy = extra[4:5] * 2.0**-13 + extra[5:6] * 2.0**-28
            full = piece[:cap] * scale[:1]
            rest = piece[cap : cap + half] * scale[1:2]
            for at, term in enumerate(
                (weight * full, energy * full, weight * rest, energy * rest)
            ):
                sums[at] = sums[at] + term
            own = extra[6:7]
            own = (own[:, 1:2] * 2.0**-14 + own[:, 2:3] * 2.0**-29) * jnp.exp2(own[:, 0:1])
            grown = count + own
            part = grown - count
            lost = lost + ((count - (grown - part)) + (own - part))
            count = grown
        full_ref[g * cap : (g + 1) * cap, :LANES] = sums[0].astype(jnp.bfloat16)
        full_ref[g * cap : (g + 1) * cap, LANES:] = sums[1].astype(jnp.bfloat16)
        half_ref[g * half : (g + 1) * half, :LANES] = sums[2].astype(jnp.bfloat16)
        half_ref[g * half : (g + 1) * half, LANES:] = sums[3].astype(jnp.bfloat16)
    count_ref[0, 0] = jnp.sum(count + lost)

    slot = slots_ref[:1, :]
    pick = (lax.broadcasted_iota(jnp.int32, (owners * cap, width), 0) == slot).astype(jnp.bfloat16)
    row = lax.broadcasted_iota(jnp.int32, (owners * half, width), 0)
    owner = slot // cap
    within = slot - owner * cap
    place = owner * half + within
    left = (row == jnp.where(within < half, place, -1)).astype(jnp.bfloat16)
    right = (row == jnp.where(within >= half, place - half, -1)).astype(jnp.bfloat16)

    def take(held, chosen):
        return lax.dot_general(
            held, chosen, (((0,), (0,)), ((), ())), preferred_element_type=jnp.float32
        )

    full = take(full_ref[...], pick)
    by_left = take(half_ref[...], left)
    by_right = take(half_ref[...], right)
    mid = LANES // 2
    odd = jnp.broadcast_to(slots_ref[1:2, :], (LANES + mid, width)) == 1
    for at, ref in ((0, dens_ref), (LANES, energy_ref)):
        wide = full[at : at + LANES]
        slim = by_left[at : at + mid] + by_right[at + mid : at + LANES]
        ref[...] = jnp.where(
            odd, jnp.concatenate([slim, wide], axis=0), jnp.concatenate([wide, slim], axis=0)
        ).astype(jnp.bfloat16)


def ranks(own, order):
    same = own[:, None] == own[None, :]
    earlier = order[None, :] < order[:, None]
    return jnp.sum((same & earlier).astype(jnp.int32), axis=1)


def body(
    anc_inv,
    factor_cols,
    diag_inv,
    intersection,
    pole_w,
    pole_z,
    ancestors,
    counts,
    hpattern,
    siesta_of,
    supernode_of,
):
    width = diag_inv.shape[-1]
    local_rows, anc_rows = anc_inv.shape[1:]
    blk_count = ancestors.shape[1]
    grid_count = lax.axis_size("grid")
    pole_count = lax.axis_size("pole")
    chunk = (blk_count + 1) * width // pole_count
    slot_cap = (width + grid_count - 1) // grid_count
    direct = (
        slot_cap * grid_count == width and slot_cap % 32 == 0 and chunk == LANES * 3 // 2
    )
    slots = slot_cap + (0 if direct else SUB if slot_cap % SUB == 0 else 1)

    dest_owner = siesta_of // width
    send_slot = dest_owner * slots + ranks(dest_owner, jnp.arange(width))
    source_dev = supernode_of // width
    recv_slot = source_dev * slots + ranks(source_dev, supernode_of)

    spread = grid_count * SUB
    if local_rows % spread == 0 and width % spread == 0:
        shares = grid_count
        stretches = local_rows // spread
        sent = pl.pallas_call(
            pack_kernel,
            out_shape=VMEM(
                (grid_count, local_rows // grid_count, anc_rows + LANES), jnp.bfloat16
            ),
            in_specs=[hspec(), hspec()],
            scratch_shapes=[
                SMEM(ancestors.shape, jnp.int32),
                pltpu.SemaphoreType.DMA((stretches,)),
            ],
            name="pack",
        )(ancestors, anc_inv[0].reshape(stretches, grid_count, SUB, anc_rows))
        held = lax.all_to_all(sent, "grid", split_axis=0, concat_axis=0, tiled=True)
        rows = width // grid_count
        chosen = pl.pallas_call(
            functools.partial(select_kernel, width, blk_count),
            out_shape=jax.ShapeDtypeStruct(
                (grid_count, blk_count * rows, blk_count * width), jnp.bfloat16
            ),
            in_specs=[vspec()],
            out_specs=hspec(),
            scratch_shapes=[pltpu.SemaphoreType.DMA((grid_count, blk_count, blk_count))],
            name="select",
        )(invmem(held.reshape(local_rows, anc_rows + LANES)))
        sub_block = lax.all_to_all(chosen, "grid", split_axis=0, concat_axis=0, tiled=True)
    else:
        shares = 1
        gathered = lax.all_gather(anc_inv[0], "grid", axis=0, tiled=True)
        blocks = gathered.reshape(anc_rows // width, width, anc_rows // width, width)
        sub_block = jnp.take(jnp.take(blocks, ancestors[0], axis=0), ancestors[0], axis=2)
    sub_block = sub_block.reshape(blk_count * width, blk_count * width)

    if direct:
        odd = (lax.axis_index("pole") & 1).astype(jnp.int32)[None]
        lower, turned, diag, inter, info, pickup_slots = pl.pallas_call(
            order_kernel,
            out_shape=(
                VMEM((blk_count * width, width), jnp.bfloat16),
                VMEM((width, blk_count * width), jnp.bfloat16),
                VMEM((width, width), jnp.bfloat16),
                VMEM((width, width), jnp.bfloat16),
                VMEM((SUB, (blk_count + 1) * width), jnp.float32),
                VMEM((SUB, width), jnp.int32),
            ),
            in_specs=[sspec()] * 5 + [vspec()] * 5,
            name="order",
        )(
            counts,
            hpattern,
            pole_w,
            pole_z,
            odd,
            send_slot[None],
            recv_slot[None],
            factor_cols[0, 0],
            diag_inv[0, 0],
            intersection[0],
        )
        rows = slot_cap * 3 // 2 + SUB
        coded = pl.pallas_call(
            functools.partial(encode_kernel, shares, chunk),
            out_shape=VMEM((pole_count * grid_count, rows, LANES), jnp.int16),
            in_specs=[vspec()] * 6,
            scratch_shapes=[VMEM((blk_count * width, blk_count * width), jnp.float32)],
            name="encode",
        )(*map(invmem, (sub_block, lower, turned, diag, inter, info)))
        arrived = lax.all_to_all(
            coded, ("pole", "grid"), split_axis=0, concat_axis=0, tiled=True
        )
        half = jax.ShapeDtypeStruct((chunk, width), jnp.bfloat16)
        density, energy, electrons = pl.pallas_call(
            functools.partial(decode_kernel, grid_count, slot_cap),
            out_shape=(half, half, jax.ShapeDtypeStruct((1, 1), jnp.float32)),
            in_specs=[vspec(), vspec()],
            out_specs=(vspec(), vspec(), sspec()),
            scratch_shapes=[
                VMEM((width, 2 * LANES), jnp.bfloat16),
                VMEM((width // 2, 2 * LANES), jnp.bfloat16),
            ],
            name="decode",
        )(invmem(pickup_slots), invmem(arrived))
        return (density.T, energy.T, electrons[0, 0])

    stack = pl.pallas_call(
        functools.partial(columns_kernel, shares, chunk),
        out_shape=jax.ShapeDtypeStruct((pole_count, chunk + SUB, width), jnp.float32),
        in_specs=[sspec()] * 4 + [vspec()] * 4,
        out_specs=vspec(),
        scratch_shapes=[VMEM((blk_count * width, width), jnp.float32)],
        name="columns",
    )(
        counts,
        hpattern,
        pole_w,
        pole_z,
        invmem(sub_block),
        factor_cols[0, 0],
        diag_inv[0, 0],
        intersection[0],
    )
    stack = lax.all_to_all(stack, "pole", split_axis=0, concat_axis=0, tiled=True)

    total = grid_count * slots
    placed = pl.pallas_call(
        functools.partial(place_kernel, slot_cap, grid_count),
        out_shape=jax.ShapeDtypeStruct((total, 2 * chunk), jnp.bfloat16),
        in_specs=[vspec(), vspec()],
        out_specs=vspec(),
        name="place",
    )(send_slot[None], invmem(stack))
    arrived = lax.all_to_all(
        placed.reshape(grid_count, slots, 2 * chunk),
        "grid",
        split_axis=0,
        concat_axis=0,
        tiled=True,
    )
    density, energy, electrons = pl.pallas_call(
        functools.partial(pickup_kernel, slot_cap, grid_count),
        out_shape=(
            jax.ShapeDtypeStruct((chunk, width), jnp.bfloat16),
            jax.ShapeDtypeStruct((chunk, width), jnp.bfloat16),
            jax.ShapeDtypeStruct((1, 1), jnp.float32),
        ),
        in_specs=[vspec(), vspec()],
        out_specs=(vspec(), vspec(), sspec()),
        name="pickup",
    )(recv_slot[None], invmem(arrived.reshape(total, 2 * chunk)))
    return (density.T, energy.T, electrons[0, 0])


def solution(mesh):
    placed = (
        P("pole", "grid", None),
        P("pole", "grid", None, None, None),
        P("pole", "grid", None, None),
        P("grid", None, None),
        P("pole"),
        P("pole"),
        P("grid", None),
        P("grid"),
        P("grid", None),
        P("grid"),
        P("grid"),
    )
    return jax.shard_map(
        body,
        mesh=mesh,
        in_specs=placed,
        out_specs=(P("grid", "pole"), P("grid", "pole"), P()),
        check_vma=False,
    )
```

```python
import functools

import jax
import jax.numpy as jnp
from jax import lax
from jax.experimental import pallas as pl
from jax.experimental.pallas import tpu as pltpu
from jax.sharding import PartitionSpec as P

VMEM = pltpu.VMEM
SMEM = pltpu.SMEM
LANES = 128
SUB = 8
TINY = 1e-30
FINE = 64.0
STEPS = 32760.0


def invmem(x):
    return pltpu.with_memory_space_constraint(x, VMEM)


def vspec():
    return pl.BlockSpec(memory_space=VMEM)


def hspec():
    return pl.BlockSpec(memory_space=pltpu.HBM)


def sspec():
    return pl.BlockSpec(memory_space=SMEM)


def pack_kernel(table_hbm, rows_ref, out_ref, table_ref, sems):
    stretches, _, _, width = rows_ref.shape
    copies = [
        pltpu.make_async_copy(
            rows_ref.at[c], out_ref.at[:, c * SUB : (c + 1) * SUB, :width], sems.at[c]
        )
        for c in range(stretches)
    ]
    for copy in copies:
        copy.start()
    pltpu.sync_copy(table_hbm, table_ref)
    shares, rows, lanes = out_ref.shape
    lane = lax.broadcasted_iota(jnp.int32, (rows, lanes - width), 1)
    table = jnp.zeros((rows, lanes - width), jnp.float32)
    for m in range(table_ref.shape[1]):
        table = jnp.where(lane == m, table_ref[0, m].astype(jnp.float32), table)
    table = table.astype(jnp.bfloat16)
    for j in range(shares):
        out_ref[j, :, width:] = table
    for copy in copies:
        copy.wait()


def select_kernel(width, blk_count, ring, held_ref, out_ref, sems):
    dests, picked, _ = out_ref.shape
    rows = picked // blk_count
    local = held_ref.shape[0] // dests
    tail = held_ref.shape[1] - LANES
    lane = lax.broadcasted_iota(jnp.int32, (1, LANES), 1)
    copies = []
    for dest, owner in enumerate(ring):
        entry = held_ref[owner * local : (owner + 1) * local, tail:].astype(jnp.float32)[:1]
        table = [
            jnp.sum(jnp.where(lane == m, entry, 0.0)).astype(jnp.int32) for m in range(blk_count)
        ]
        for m in range(blk_count):
            row_at = pl.multiple_of(table[m] * rows, rows)
            for n in range(blk_count):
                col_at = pl.multiple_of(table[n] * width, width)
                copy = pltpu.make_async_copy(
                    held_ref.at[pl.ds(row_at, rows), pl.ds(col_at, width)],
                    out_ref.at[dest, m * rows : (m + 1) * rows, n * width : (n + 1) * width],
                    sems.at[dest, m, n],
                )
                copy.start()
                copies.append(copy)
    for copy in copies:
        copy.wait()


def columns_kernel(
    ring,
    chunk,
    counts_ref,
    hpattern_ref,
    weight_ref,
    energy_ref,
    rows_ref,
    factor_ref,
    diag_ref,
    inter_ref,
    out_ref,
    off_ref,
):
    blk_count, width, _ = factor_ref.shape
    parts = [
        factor_ref[m] * (m < counts_ref[0]).astype(jnp.float32).astype(jnp.bfloat16)
        for m in range(blk_count)
    ]
    lower = jnp.concatenate(parts, axis=0)
    product = jnp.dot(rows_ref[...], lower, preferred_element_type=jnp.float32)
    shares = len(ring)
    per_blk = width // shares
    for m in range(blk_count):
        scale = hpattern_ref[0, m].astype(jnp.float32)
        for at_share, j in enumerate(ring):
            for c in range(per_blk // SUB):
                at = (at_share * blk_count + m) * per_blk + c * SUB
                piece = -product[at : at + SUB]
                row = m * width + (c * shares + j) * SUB
                off_ref[row : row + SUB, :] = piece
                place = width + row
                out_ref[place // chunk, place % chunk : place % chunk + SUB, :] = piece * scale
    off = off_ref[...]
    high = off.astype(jnp.bfloat16)
    rest = off - high.astype(jnp.float32)
    mid = rest.astype(jnp.bfloat16)
    low = (rest - mid.astype(jnp.float32)).astype(jnp.bfloat16)
    contract = functools.partial(
        lax.dot_general,
        dimension_numbers=(((0,), (0,)), ((), ())),
        preferred_element_type=jnp.float32,
    )
    product_sum = contract(lower, low) + contract(lower, mid) + contract(lower, high)
    diag_block = diag_ref[...].astype(jnp.float32) - product_sum
    at = 0
    while at < width:
        size = min(chunk - at % chunk, width - at)
        out_ref[at // chunk, at % chunk : at % chunk + size, :] = diag_block[at : at + size]
        at += size
    count = weight_ref[0] * jnp.sum(diag_block * inter_ref[...].astype(jnp.float32))
    row_id = lax.broadcasted_iota(jnp.int32, (SUB, width), 0)
    extra = jnp.where(row_id == 0, weight_ref[0], jnp.where(row_id == 1, energy_ref[0], count))
    for q in range(out_ref.shape[0]):
        out_ref[q, chunk : chunk + SUB, :] = extra


def place_kernel(slot_cap, dests, slot_ref, stack_ref, out_ref):
    poles, rows, width = stack_ref.shape
    chunk = rows - SUB
    dens = jnp.zeros((chunk, width), jnp.float32)
    energy = jnp.zeros((chunk, width), jnp.float32)
    count = jnp.zeros((1, width), jnp.float32)
    for p in range(poles):
        term = stack_ref[p, :chunk, :]
        dens = dens + stack_ref[p, chunk : chunk + 1, :] * term
        energy = energy + stack_ref[p, chunk + 1 : chunk + 2, :] * term
        count = count + stack_ref[p, chunk + 2 : chunk + 3, :]
    both = jnp.concatenate([dens, energy], axis=0).astype(jnp.bfloat16)
    total, lanes = out_ref.shape
    slots = total // dests
    one_hot = (lax.broadcasted_iota(jnp.int32, (total, width), 0) == slot_ref[...]).astype(
        jnp.bfloat16
    )
    placed = lax.dot_general(
        one_hot, both, (((1,), (1,)), ((), ())), preferred_element_type=jnp.float32
    )
    own = count[:, 0:1]
    high = own.astype(jnp.bfloat16).astype(jnp.float32)
    rest = own - high
    mid = rest.astype(jnp.bfloat16).astype(jnp.float32)
    lane = lax.broadcasted_iota(jnp.int32, (1, lanes), 1)
    pieces = jnp.where(lane == 0, high, jnp.where(lane == 1, mid, rest - mid))
    pieces = jnp.where(lane < 3, pieces, 0.0)
    row = lax.broadcasted_iota(jnp.int32, (total, 1), 0)
    marked = functools.reduce(
        jnp.logical_or, [row == g * slots + slot_cap for g in range(dests)]
    )
    out_ref[...] = jnp.where(marked, pieces, placed).astype(jnp.bfloat16)


def pickup_kernel(slot_cap, dests, slot_ref, recv_ref, dens_ref, energy_ref, count_ref):
    total, lanes = recv_ref.shape
    slots = total // dests
    chunk = lanes // 2
    width = slot_ref.shape[1]
    recv = recv_ref[...]
    one_hot = (lax.broadcasted_iota(jnp.int32, (total, width), 0) == slot_ref[...]).astype(
        jnp.bfloat16
    )
    out = lax.dot_general(
        recv, one_hot, (((0,), (0,)), ((), ())), preferred_element_type=jnp.float32
    ).astype(jnp.bfloat16)
    dens_ref[...] = out[:chunk]
    energy_ref[...] = out[chunk:]
    row = lax.broadcasted_iota(jnp.int32, (total, 1), 0)
    marked = functools.reduce(
        jnp.logical_or, [row == g * slots + slot_cap for g in range(dests)]
    )
    pieces = jnp.where(marked, recv[:, :LANES].astype(jnp.float32), 0.0)
    count_ref[0, 0] = jnp.sum(pieces)


def order_kernel(
    counts_ref,
    hpattern_ref,
    weight_ref,
    energy_ref,
    odd_ref,
    send_ref,
    recv_ref,
    factor_ref,
    diag_ref,
    inter_ref,
    lower_ref,
    turned_ref,
    diag_out,
    inter_out,
    info_ref,
    slots_ref,
):
    blk_count, width, _ = factor_ref.shape
    one_hot = (lax.broadcasted_iota(jnp.int32, (width, width), 0) == send_ref[...]).astype(
        jnp.bfloat16
    )

    def turn(matrix):
        return lax.dot_general(
            one_hot, matrix, (((1,), (1,)), ((), ())), preferred_element_type=jnp.float32
        ).astype(jnp.bfloat16)

    for m in range(blk_count):
        live = (m < counts_ref[0]).astype(jnp.float32).astype(jnp.bfloat16)
        block = factor_ref[m] * live
        lower_ref[m * width : (m + 1) * width, :] = block
        turned_ref[:, m * width : (m + 1) * width] = turn(block)
    diag_out[...] = turn(diag_ref[...])
    inter_out[...] = turn(inter_ref[...])

    rows, lanes = info_ref.shape
    row_id = lax.broadcasted_iota(jnp.int32, (rows, lanes), 0)
    block = lax.broadcasted_iota(jnp.int32, (rows, lanes), 1) // width
    info = jnp.ones((rows, lanes), jnp.float32)
    for m in range(blk_count):
        info = jnp.where(block == m + 1, hpattern_ref[0, m].astype(jnp.float32), info)
    info = jnp.where(row_id == 1, weight_ref[0], info)
    for at, scalar in ((2, weight_ref[0]), (4, energy_ref[0])):
        grown = jnp.full((rows, lanes), scalar) * 2.0**13
        grown_high = jnp.floor(grown)
        info = jnp.where(row_id == at, grown_high, info)
        info = jnp.where(row_id == at + 1, (grown - grown_high) * 2.0**15, info)
    info_ref[...] = info
    row_id = lax.broadcasted_iota(jnp.int32, (SUB, width), 0)
    slots_ref[...] = jnp.where(row_id == 0, recv_ref[...], odd_ref[0])


def halved_sum(values):
    while values.shape[0] > SUB:
        half = values.shape[0] // 2
        values = values[:half] + values[half:]
    while values.shape[1] > LANES:
        half = values.shape[1] // 2
        values = values[:, :half] + values[:, half:]
    return jnp.sum(values)


def whole(value):
    return value.astype(jnp.int32).astype(jnp.int16)


def fold_half(tile, right):
    rows = tile.shape[0] // 2
    lane = lax.broadcasted_iota(jnp.int32, (rows, LANES), 1)
    top, bottom = tile[:rows], tile[rows:]
    if right:
        return jnp.where(lane < LANES // 2, pltpu.roll(top, LANES // 2, 1), bottom)
    return jnp.where(lane < LANES // 2, top, pltpu.roll(bottom, LANES // 2, 1))


def encode_kernel(
    ring,
    chunk,
    rows_ref,
    lower_ref,
    turned_ref,
    diag_ref,
    inter_ref,
    info_ref,
    out_ref,
    sorted_ref,
):
    depth, width = lower_ref.shape
    blk_count = depth // width
    shares = len(ring)
    per_blk = width // shares
    for m in range(blk_count):
        for place, j in enumerate(ring):
            at = (place * blk_count + m) * per_blk
            piece = rows_ref[at : at + per_blk, :].astype(jnp.float32)
            for c in range(per_blk // SUB):
                row = m * width + (c * shares + j) * SUB
                sorted_ref[row : row + SUB, :] = piece[c * SUB : (c + 1) * SUB]
    off = -lax.dot_general(
        turned_ref[...],
        sorted_ref[...].astype(jnp.bfloat16),
        (((1,), (1,)), ((), ())),
        preferred_element_type=jnp.float32,
    )
    high = off.astype(jnp.bfloat16)
    rest = off - high.astype(jnp.float32)
    mid = rest.astype(jnp.bfloat16)
    low = (rest - mid.astype(jnp.float32)).astype(jnp.bfloat16)
    lower = lower_ref[...]
    diag = diag_ref[...].astype(jnp.float32) - (
        jnp.dot(low, lower, preferred_element_type=jnp.float32)
        + jnp.dot(mid, lower, preferred_element_type=jnp.float32)
        + jnp.dot(high, lower, preferred_element_type=jnp.float32)
    )
    count = halved_sum(diag * inter_ref[...].astype(jnp.float32))
    values = jnp.concatenate([diag, off * info_ref[:1, width:]], axis=1)
    largest = jnp.max(jnp.abs(values), axis=0, keepdims=True)
    level = jnp.ceil(jnp.log2(jnp.maximum(largest, TINY)) * FINE)
    codes = jnp.floor(values * (jnp.exp2(level * (-1.0 / FINE)) * STEPS) + 0.5)

    row_id = lax.broadcasted_iota(jnp.int32, (SUB, LANES), 0)
    lane_id = lax.broadcasted_iota(jnp.int32, (SUB, LANES), 1)
    full_count = info_ref[1:2, :LANES] * jnp.full((SUB, LANES), count)
    power = jnp.ceil(jnp.log2(jnp.maximum(jnp.abs(full_count), TINY)))
    scaled = full_count * jnp.exp2(-power) * 2.0**14
    scaled_high = jnp.floor(scaled)
    extra = jnp.where(
        lane_id == 0,
        power,
        jnp.where(lane_id == 1, scaled_high, jnp.floor((scaled - scaled_high) * 2.0**15)),
    )
    extra = jnp.where(row_id < 6, info_ref[:, :LANES], extra)

    dests, _, _ = out_ref.shape
    pole_count = values.shape[1] // chunk
    owners = dests // pole_count
    cap = width // owners
    half = cap // 2
    for q in range(pole_count):
        right = q % 2 == 1
        full_at = (q * chunk + LANES - 1) // LANES * LANES
        half_at = full_at - LANES if right else full_at + LANES
        level_half = level[:, half_at : half_at + LANES]
        lane = lax.broadcasted_iota(jnp.int32, (1, LANES), 1)
        other = pltpu.roll(jnp.broadcast_to(level_half, (SUB, LANES)), LANES // 2, 1)[:1]
        level_half = jnp.where((lane < LANES // 2) == (not right), level_half, other)
        tail = jnp.where(
            row_id == 0,
            level[:, full_at : full_at + LANES],
            jnp.where(row_id == 1, level_half, extra),
        )
        tail = whole(tail)
        for g in range(owners):
            rows = slice(g * cap, (g + 1) * cap)
            d = q * owners + g
            out_ref[d, :cap, :] = whole(codes[rows, full_at : full_at + LANES])
            out_ref[d, cap : cap + half, :] = whole(
                fold_half(codes[rows, half_at : half_at + LANES], right)
            )
            out_ref[d, cap + half :, :] = tail


def decode_kernel(
    owners, cap, slots_ref, recv_ref, dens_ref, energy_ref, count_ref, full_ref, half_ref
):
    dests, rows, _ = recv_ref.shape
    poles = dests // owners
    half = cap // 2
    width = slots_ref.shape[1]
    count = jnp.zeros((1, 1), jnp.float32)
    lost = jnp.zeros((1, 1), jnp.float32)
    for g in range(owners):
        sums = [0.0, 0.0, 0.0, 0.0]
        for p in range(poles):
            piece = recv_ref[p * owners + g].astype(jnp.int32).astype(jnp.float32)
            extra = piece[cap + half :]
            scale = jnp.exp2(extra[:2] * (1.0 / FINE)) * (1.0 / STEPS)
            weight = extra[2:3] * 2.0**-13 + extra[3:4] * 2.0**-28
            energy = extra[4:5] * 2.0**-13 + extra[5:6] * 2.0**-28
            full = piece[:cap] * scale[:1]
            rest = piece[cap : cap + half] * scale[1:2]
            for at, term in enumerate(
                (weight * full, energy * full, weight * rest, energy * rest)
            ):
                sums[at] = sums[at] + term
            own = extra[6:7]
            own = (own[:, 1:2] * 2.0**-14 + own[:, 2:3] * 2.0**-29) * jnp.exp2(own[:, 0:1])
            grown = count + own
            part = grown - count
            lost = lost + ((count - (grown - part)) + (own - part))
            count = grown
        full_ref[g * cap : (g + 1) * cap, :LANES] = sums[0].astype(jnp.bfloat16)
        full_ref[g * cap : (g + 1) * cap, LANES:] = sums[1].astype(jnp.bfloat16)
        half_ref[g * half : (g + 1) * half, :LANES] = sums[2].astype(jnp.bfloat16)
        half_ref[g * half : (g + 1) * half, LANES:] = sums[3].astype(jnp.bfloat16)
    count_ref[0, 0] = jnp.sum(count + lost)

    slot = slots_ref[:1, :]
    pick = (lax.broadcasted_iota(jnp.int32, (owners * cap, width), 0) == slot).astype(jnp.bfloat16)
    row = lax.broadcasted_iota(jnp.int32, (owners * half, width), 0)
    owner = slot // cap
    within = slot - owner * cap
    place = owner * half + within
    left = (row == jnp.where(within < half, place, -1)).astype(jnp.bfloat16)
    right = (row == jnp.where(within >= half, place - half, -1)).astype(jnp.bfloat16)

    def take(held, chosen):
        return lax.dot_general(
            held, chosen, (((0,), (0,)), ((), ())), preferred_element_type=jnp.float32
        )

    full = take(full_ref[...], pick)
    by_left = take(half_ref[...], left)
    by_right = take(half_ref[...], right)
    mid = LANES // 2
    odd = jnp.broadcast_to(slots_ref[1:2, :], (LANES + mid, width)) == 1
    for at, ref in ((0, dens_ref), (LANES, energy_ref)):
        wide = full[at : at + LANES]
        slim = by_left[at : at + mid] + by_right[at + mid : at + LANES]
        ref[...] = jnp.where(
            odd, jnp.concatenate([slim, wide], axis=0), jnp.concatenate([wide, slim], axis=0)
        ).astype(jnp.bfloat16)


def ring_order(count):
    return list(range(0, count, 2)) + list(range(1, count, 2))[::-1]


def ranks(own, order):
    same = own[:, None] == own[None, :]
    earlier = order[None, :] < order[:, None]
    return jnp.sum((same & earlier).astype(jnp.int32), axis=1)


def body(
    anc_inv,
    factor_cols,
    diag_inv,
    intersection,
    pole_w,
    pole_z,
    ancestors,
    counts,
    hpattern,
    siesta_of,
    supernode_of,
):
    width = diag_inv.shape[-1]
    local_rows, anc_rows = anc_inv.shape[1:]
    blk_count = ancestors.shape[1]
    grid_count = lax.axis_size("grid")
    pole_count = lax.axis_size("pole")
    chunk = (blk_count + 1) * width // pole_count
    slot_cap = (width + grid_count - 1) // grid_count
    direct = (
        slot_cap * grid_count == width and slot_cap % 32 == 0 and chunk == LANES * 3 // 2
    )
    slots = slot_cap + (0 if direct else SUB if slot_cap % SUB == 0 else 1)

    dest_owner = siesta_of // width
    send_slot = dest_owner * slots + ranks(dest_owner, jnp.arange(width))
    source_dev = supernode_of // width
    recv_slot = source_dev * slots + ranks(source_dev, supernode_of)

    spread = grid_count * SUB
    if local_rows % spread == 0 and width % spread == 0:
        ring = ring_order(grid_count)
        stretches = local_rows // spread
        sent = pl.pallas_call(
            pack_kernel,
            out_shape=VMEM(
                (grid_count, local_rows // grid_count, anc_rows + LANES), jnp.bfloat16
            ),
            in_specs=[hspec(), hspec()],
            scratch_shapes=[
                SMEM(ancestors.shape, jnp.int32),
                pltpu.SemaphoreType.DMA((stretches,)),
            ],
            name="pack",
        )(ancestors, anc_inv[0].reshape(stretches, grid_count, SUB, anc_rows))
        held = lax.all_to_all(sent, "grid", split_axis=0, concat_axis=0, tiled=True)
        rows = width // grid_count
        chosen = pl.pallas_call(
            functools.partial(select_kernel, width, blk_count, ring),
            out_shape=jax.ShapeDtypeStruct(
                (grid_count, blk_count * rows, blk_count * width), jnp.bfloat16
            ),
            in_specs=[vspec()],
            out_specs=hspec(),
            scratch_shapes=[pltpu.SemaphoreType.DMA((grid_count, blk_count, blk_count))],
            name="select",
        )(invmem(held.reshape(local_rows, anc_rows + LANES)))
        sub_block = lax.all_to_all(
            chosen, "grid", split_axis=0, concat_axis=0, axis_index_groups=[ring], tiled=True
        )
    else:
        ring = [0]
        gathered = lax.all_gather(anc_inv[0], "grid", axis=0, tiled=True)
        blocks = gathered.reshape(anc_rows // width, width, anc_rows // width, width)
        sub_block = jnp.take(jnp.take(blocks, ancestors[0], axis=0), ancestors[0], axis=2)
    sub_block = sub_block.reshape(blk_count * width, blk_count * width)

    if direct:
        odd = (lax.axis_index("pole") & 1).astype(jnp.int32)[None]
        lower, turned, diag, inter, info, pickup_slots = pl.pallas_call(
            order_kernel,
            out_shape=(
                VMEM((blk_count * width, width), jnp.bfloat16),
                VMEM((width, blk_count * width), jnp.bfloat16),
                VMEM((width, width), jnp.bfloat16),
                VMEM((width, width), jnp.bfloat16),
                VMEM((SUB, (blk_count + 1) * width), jnp.float32),
                VMEM((SUB, width), jnp.int32),
            ),
            in_specs=[sspec()] * 5 + [vspec()] * 5,
            name="order",
        )(
            counts,
            hpattern,
            pole_w,
            pole_z,
            odd,
            send_slot[None],
            recv_slot[None],
            factor_cols[0, 0],
            diag_inv[0, 0],
            intersection[0],
        )
        rows = slot_cap * 3 // 2 + SUB
        coded = pl.pallas_call(
            functools.partial(encode_kernel, ring, chunk),
            out_shape=VMEM((pole_count * grid_count, rows, LANES), jnp.int16),
            in_specs=[vspec()] * 6,
            scratch_shapes=[VMEM((blk_count * width, blk_count * width), jnp.float32)],
            name="encode",
        )(*map(invmem, (sub_block, lower, turned, diag, inter, info)))
        arrived = lax.all_to_all(
            coded, ("pole", "grid"), split_axis=0, concat_axis=0, tiled=True
        )
        half = jax.ShapeDtypeStruct((chunk, width), jnp.bfloat16)
        density, energy, electrons = pl.pallas_call(
            functools.partial(decode_kernel, grid_count, slot_cap),
            out_shape=(half, half, jax.ShapeDtypeStruct((1, 1), jnp.float32)),
            in_specs=[vspec(), vspec()],
            out_specs=(vspec(), vspec(), sspec()),
            scratch_shapes=[
                VMEM((width, 2 * LANES), jnp.bfloat16),
                VMEM((width // 2, 2 * LANES), jnp.bfloat16),
            ],
            name="decode",
        )(invmem(pickup_slots), invmem(arrived))
        return (density.T, energy.T, electrons[0, 0])

    stack = pl.pallas_call(
        functools.partial(columns_kernel, ring, chunk),
        out_shape=jax.ShapeDtypeStruct((pole_count, chunk + SUB, width), jnp.float32),
        in_specs=[sspec()] * 4 + [vspec()] * 4,
        out_specs=vspec(),
        scratch_shapes=[VMEM((blk_count * width, width), jnp.float32)],
        name="columns",
    )(
        counts,
        hpattern,
        pole_w,
        pole_z,
        invmem(sub_block),
        factor_cols[0, 0],
        diag_inv[0, 0],
        intersection[0],
    )
    stack = lax.all_to_all(stack, "pole", split_axis=0, concat_axis=0, tiled=True)

    total = grid_count * slots
    placed = pl.pallas_call(
        functools.partial(place_kernel, slot_cap, grid_count),
        out_shape=jax.ShapeDtypeStruct((total, 2 * chunk), jnp.bfloat16),
        in_specs=[vspec(), vspec()],
        out_specs=vspec(),
        name="place",
    )(send_slot[None], invmem(stack))
    arrived = lax.all_to_all(
        placed.reshape(grid_count, slots, 2 * chunk),
        "grid",
        split_axis=0,
        concat_axis=0,
        tiled=True,
    )
    density, energy, electrons = pl.pallas_call(
        functools.partial(pickup_kernel, slot_cap, grid_count),
        out_shape=(
            jax.ShapeDtypeStruct((chunk, width), jnp.bfloat16),
            jax.ShapeDtypeStruct((chunk, width), jnp.bfloat16),
            jax.ShapeDtypeStruct((1, 1), jnp.float32),
        ),
        in_specs=[vspec(), vspec()],
        out_specs=(vspec(), vspec(), sspec()),
        name="pickup",
    )(recv_slot[None], invmem(arrived.reshape(total, 2 * chunk)))
    return (density.T, energy.T, electrons[0, 0])


def solution(mesh):
    placed = (
        P("pole", "grid", None),
        P("pole", "grid", None, None, None),
        P("pole", "grid", None, None),
        P("grid", None, None),
        P("pole"),
        P("pole"),
        P("grid", None),
        P("grid"),
        P("grid", None),
        P("grid"),
        P("grid"),
    )
    return jax.shard_map(
        body,
        mesh=mesh,
        in_specs=placed,
        out_specs=(P("grid", "pole"), P("grid", "pole"), P()),
        check_vma=False,
    )
```

```python
import functools

import jax
import jax.numpy as jnp
from jax import lax
from jax.experimental import pallas as pl
from jax.experimental.pallas import tpu as pltpu
from jax.sharding import PartitionSpec as P

VMEM = pltpu.VMEM
SMEM = pltpu.SMEM
LANES = 128
SUB = 8
TINY = 1e-30
FINE = 64.0
STEPS = 32760.0


def invmem(x):
    return pltpu.with_memory_space_constraint(x, VMEM)


def vspec():
    return pl.BlockSpec(memory_space=VMEM)


def hspec():
    return pl.BlockSpec(memory_space=pltpu.HBM)


def sspec():
    return pl.BlockSpec(memory_space=SMEM)


def pack_kernel(table_hbm, rows_ref, out_ref, table_ref, sems):
    stretches, shares, rows, width = rows_ref.shape
    copies = [
        pltpu.make_async_copy(
            rows_ref.at[c], out_ref.at[:, :, c * width : (c + 1) * width], sems.at[c]
        )
        for c in range(stretches)
    ]
    for copy in copies:
        copy.start()
    pltpu.sync_copy(table_hbm, table_ref)
    lane = lax.broadcasted_iota(jnp.int32, (rows, LANES), 1)
    table = jnp.zeros((rows, LANES), jnp.float32)
    for m in range(table_ref.shape[1]):
        table = jnp.where(lane == m, table_ref[0, m].astype(jnp.float32), table)
    table = table.astype(jnp.bfloat16)
    for s in range(shares):
        out_ref[s, :, stretches * width :] = table
    for copy in copies:
        copy.wait()


def select_kernel(width, blk_count, stretches, held_ref, out_ref, sem):
    dests, picked, _ = out_ref.shape
    tail = held_ref.shape[2] - LANES
    per_blk = picked // blk_count // SUB
    lane = lax.broadcasted_iota(jnp.int32, (1, LANES), 1)
    tables = []
    for s in range(dests):
        entry = held_ref[s, :, tail:].astype(jnp.float32)[:1]
        tables.append(
            [jnp.sum(jnp.where(lane == m, entry, 0.0)).astype(jnp.int32) for m in range(blk_count)]
        )
    long = tail // stretches
    for s, table in enumerate(tables):
        for m in range(blk_count):
            for k in range(per_blk):
                stretch = table[m] * per_blk + k
                device = stretch // stretches
                start = (stretch - device * stretches) * long
                back = device // 2
                place = jnp.where(device == 2 * back, back, dests - 1 - back)
                at = (m * per_blk + k) * SUB
                for n in range(blk_count):
                    col_at = pl.multiple_of(start + table[n] * width, LANES)
                    pltpu.make_async_copy(
                        held_ref.at[place, :, pl.ds(col_at, width)],
                        out_ref.at[s, at : at + SUB, n * width : (n + 1) * width],
                        sem,
                    ).start()
    pltpu.make_async_copy(out_ref, out_ref, sem).wait()


def columns_kernel(
    shares,
    chunk,
    counts_ref,
    hpattern_ref,
    weight_ref,
    energy_ref,
    rows_ref,
    factor_ref,
    diag_ref,
    inter_ref,
    out_ref,
    off_ref,
):
    blk_count, width, _ = factor_ref.shape
    parts = [
        factor_ref[m] * (m < counts_ref[0]).astype(jnp.float32).astype(jnp.bfloat16)
        for m in range(blk_count)
    ]
    lower = jnp.concatenate(parts, axis=0)
    product = jnp.dot(rows_ref[...], lower, preferred_element_type=jnp.float32)
    per_blk = width // shares
    for m in range(blk_count):
        scale = hpattern_ref[0, m].astype(jnp.float32)
        for j in range(shares):
            for c in range(per_blk // SUB):
                at = (j * blk_count + m) * per_blk + c * SUB
                piece = -product[at : at + SUB]
                row = m * width + (c * shares + j) * SUB
                off_ref[row : row + SUB, :] = piece
                place = width + row
                out_ref[place // chunk, place % chunk : place % chunk + SUB, :] = piece * scale
    off = off_ref[...]
    high = off.astype(jnp.bfloat16)
    rest = off - high.astype(jnp.float32)
    mid = rest.astype(jnp.bfloat16)
    low = (rest - mid.astype(jnp.float32)).astype(jnp.bfloat16)
    contract = functools.partial(
        lax.dot_general,
        dimension_numbers=(((0,), (0,)), ((), ())),
        preferred_element_type=jnp.float32,
    )
    product_sum = contract(lower, low) + contract(lower, mid) + contract(lower, high)
    diag_block = diag_ref[...].astype(jnp.float32) - product_sum
    at = 0
    while at < width:
        size = min(chunk - at % chunk, width - at)
        out_ref[at // chunk, at % chunk : at % chunk + size, :] = diag_block[at : at + size]
        at += size
    count = weight_ref[0] * jnp.sum(diag_block * inter_ref[...].astype(jnp.float32))
    row_id = lax.broadcasted_iota(jnp.int32, (SUB, width), 0)
    extra = jnp.where(row_id == 0, weight_ref[0], jnp.where(row_id == 1, energy_ref[0], count))
    for q in range(out_ref.shape[0]):
        out_ref[q, chunk : chunk + SUB, :] = extra


def place_kernel(slot_cap, dests, slot_ref, stack_ref, out_ref):
    poles, rows, width = stack_ref.shape
    chunk = rows - SUB
    dens = jnp.zeros((chunk, width), jnp.float32)
    energy = jnp.zeros((chunk, width), jnp.float32)
    count = jnp.zeros((1, width), jnp.float32)
    for p in range(poles):
        term = stack_ref[p, :chunk, :]
        dens = dens + stack_ref[p, chunk : chunk + 1, :] * term
        energy = energy + stack_ref[p, chunk + 1 : chunk + 2, :] * term
        count = count + stack_ref[p, chunk + 2 : chunk + 3, :]
    both = jnp.concatenate([dens, energy], axis=0).astype(jnp.bfloat16)
    total, lanes = out_ref.shape
    slots = total // dests
    one_hot = (lax.broadcasted_iota(jnp.int32, (total, width), 0) == slot_ref[...]).astype(
        jnp.bfloat16
    )
    placed = lax.dot_general(
        one_hot, both, (((1,), (1,)), ((), ())), preferred_element_type=jnp.float32
    )
    own = count[:, 0:1]
    high = own.astype(jnp.bfloat16).astype(jnp.float32)
    rest = own - high
    mid = rest.astype(jnp.bfloat16).astype(jnp.float32)
    lane = lax.broadcasted_iota(jnp.int32, (1, lanes), 1)
    pieces = jnp.where(lane == 0, high, jnp.where(lane == 1, mid, rest - mid))
    pieces = jnp.where(lane < 3, pieces, 0.0)
    row = lax.broadcasted_iota(jnp.int32, (total, 1), 0)
    marked = functools.reduce(
        jnp.logical_or, [row == g * slots + slot_cap for g in range(dests)]
    )
    out_ref[...] = jnp.where(marked, pieces, placed).astype(jnp.bfloat16)


def pickup_kernel(slot_cap, dests, slot_ref, recv_ref, dens_ref, energy_ref, count_ref):
    total, lanes = recv_ref.shape
    slots = total // dests
    chunk = lanes // 2
    width = slot_ref.shape[1]
    recv = recv_ref[...]
    one_hot = (lax.broadcasted_iota(jnp.int32, (total, width), 0) == slot_ref[...]).astype(
        jnp.bfloat16
    )
    out = lax.dot_general(
        recv, one_hot, (((0,), (0,)), ((), ())), preferred_element_type=jnp.float32
    ).astype(jnp.bfloat16)
    dens_ref[...] = out[:chunk]
    energy_ref[...] = out[chunk:]
    row = lax.broadcasted_iota(jnp.int32, (total, 1), 0)
    marked = functools.reduce(
        jnp.logical_or, [row == g * slots + slot_cap for g in range(dests)]
    )
    pieces = jnp.where(marked, recv[:, :LANES].astype(jnp.float32), 0.0)
    count_ref[0, 0] = jnp.sum(pieces)


def order_kernel(
    counts_ref,
    hpattern_ref,
    weight_ref,
    energy_ref,
    odd_ref,
    send_ref,
    recv_ref,
    factor_ref,
    diag_ref,
    inter_ref,
    lower_ref,
    turned_ref,
    diag_out,
    inter_out,
    info_ref,
    slots_ref,
):
    blk_count, width, _ = factor_ref.shape
    one_hot = (lax.broadcasted_iota(jnp.int32, (width, width), 0) == send_ref[...]).astype(
        jnp.bfloat16
    )

    def turn(matrix):
        return lax.dot_general(
            one_hot, matrix, (((1,), (1,)), ((), ())), preferred_element_type=jnp.float32
        ).astype(jnp.bfloat16)

    for m in range(blk_count):
        live = (m < counts_ref[0]).astype(jnp.float32).astype(jnp.bfloat16)
        block = factor_ref[m] * live
        lower_ref[m * width : (m + 1) * width, :] = block
        turned_ref[:, m * width : (m + 1) * width] = turn(block)
    diag_out[...] = turn(diag_ref[...])
    inter_out[...] = turn(inter_ref[...])

    rows, lanes = info_ref.shape
    row_id = lax.broadcasted_iota(jnp.int32, (rows, lanes), 0)
    block = lax.broadcasted_iota(jnp.int32, (rows, lanes), 1) // width
    info = jnp.ones((rows, lanes), jnp.float32)
    for m in range(blk_count):
        info = jnp.where(block == m + 1, hpattern_ref[0, m].astype(jnp.float32), info)
    info = jnp.where(row_id == 1, weight_ref[0], info)
    for at, scalar in ((2, weight_ref[0]), (4, energy_ref[0])):
        grown = jnp.full((rows, lanes), scalar) * 2.0**13
        grown_high = jnp.floor(grown)
        info = jnp.where(row_id == at, grown_high, info)
        info = jnp.where(row_id == at + 1, (grown - grown_high) * 2.0**15, info)
    info_ref[...] = info
    row_id = lax.broadcasted_iota(jnp.int32, (SUB, width), 0)
    slots_ref[...] = jnp.where(row_id == 0, recv_ref[...], odd_ref[0])


def halved_sum(values):
    while values.shape[0] > SUB:
        half = values.shape[0] // 2
        values = values[:half] + values[half:]
    while values.shape[1] > LANES:
        half = values.shape[1] // 2
        values = values[:, :half] + values[:, half:]
    return jnp.sum(values)


def whole(value):
    return value.astype(jnp.int32).astype(jnp.int16)


def fold_half(tile, right):
    rows = tile.shape[0] // 2
    lane = lax.broadcasted_iota(jnp.int32, (rows, LANES), 1)
    top, bottom = tile[:rows], tile[rows:]
    if right:
        return jnp.where(lane < LANES // 2, pltpu.roll(top, LANES // 2, 1), bottom)
    return jnp.where(lane < LANES // 2, top, pltpu.roll(bottom, LANES // 2, 1))


def encode_kernel(
    shares,
    chunk,
    rows_ref,
    lower_ref,
    turned_ref,
    diag_ref,
    inter_ref,
    info_ref,
    out_ref,
    sorted_ref,
):
    depth, width = lower_ref.shape
    blk_count = depth // width
    per_blk = width // shares
    for m in range(blk_count):
        for j in range(shares):
            at = (j * blk_count + m) * per_blk
            piece = rows_ref[at : at + per_blk, :].astype(jnp.float32)
            for c in range(per_blk // SUB):
                row = m * width + (c * shares + j) * SUB
                sorted_ref[row : row + SUB, :] = piece[c * SUB : (c + 1) * SUB]
    off = -lax.dot_general(
        turned_ref[...],
        sorted_ref[...].astype(jnp.bfloat16),
        (((1,), (1,)), ((), ())),
        preferred_element_type=jnp.float32,
    )
    high = off.astype(jnp.bfloat16)
    rest = off - high.astype(jnp.float32)
    mid = rest.astype(jnp.bfloat16)
    low = (rest - mid.astype(jnp.float32)).astype(jnp.bfloat16)
    lower = lower_ref[...]
    diag = diag_ref[...].astype(jnp.float32) - (
        jnp.dot(low, lower, preferred_element_type=jnp.float32)
        + jnp.dot(mid, lower, preferred_element_type=jnp.float32)
        + jnp.dot(high, lower, preferred_element_type=jnp.float32)
    )
    count = halved_sum(diag * inter_ref[...].astype(jnp.float32))
    values = jnp.concatenate([diag, off * info_ref[:1, width:]], axis=1)
    largest = jnp.max(jnp.abs(values), axis=0, keepdims=True)
    level = jnp.ceil(jnp.log2(jnp.maximum(largest, TINY)) * FINE)
    codes = jnp.floor(values * (jnp.exp2(level * (-1.0 / FINE)) * STEPS) + 0.5)

    row_id = lax.broadcasted_iota(jnp.int32, (SUB, LANES), 0)
    lane_id = lax.broadcasted_iota(jnp.int32, (SUB, LANES), 1)
    full_count = info_ref[1:2, :LANES] * jnp.full((SUB, LANES), count)
    power = jnp.ceil(jnp.log2(jnp.maximum(jnp.abs(full_count), TINY)))
    scaled = full_count * jnp.exp2(-power) * 2.0**14
    scaled_high = jnp.floor(scaled)
    extra = jnp.where(
        lane_id == 0,
        power,
        jnp.where(lane_id == 1, scaled_high, jnp.floor((scaled - scaled_high) * 2.0**15)),
    )
    extra = jnp.where(row_id < 6, info_ref[:, :LANES], extra)

    dests, _, _ = out_ref.shape
    pole_count = values.shape[1] // chunk
    owners = dests // pole_count
    cap = width // owners
    half = cap // 2
    for q in range(pole_count):
        right = q % 2 == 1
        full_at = (q * chunk + LANES - 1) // LANES * LANES
        half_at = full_at - LANES if right else full_at + LANES
        level_half = level[:, half_at : half_at + LANES]
        lane = lax.broadcasted_iota(jnp.int32, (1, LANES), 1)
        other = pltpu.roll(jnp.broadcast_to(level_half, (SUB, LANES)), LANES // 2, 1)[:1]
        level_half = jnp.where((lane < LANES // 2) == (not right), level_half, other)
        tail = jnp.where(
            row_id == 0,
            level[:, full_at : full_at + LANES],
            jnp.where(row_id == 1, level_half, extra),
        )
        tail = whole(tail)
        for g in range(owners):
            rows = slice(g * cap, (g + 1) * cap)
            d = q * owners + g
            out_ref[d, :cap, :] = whole(codes[rows, full_at : full_at + LANES])
            out_ref[d, cap : cap + half, :] = whole(
                fold_half(codes[rows, half_at : half_at + LANES], right)
            )
            out_ref[d, cap + half :, :] = tail


def decode_kernel(
    owners, cap, slots_ref, recv_ref, dens_ref, energy_ref, count_ref, full_ref, half_ref
):
    dests, rows, _ = recv_ref.shape
    poles = dests // owners
    half = cap // 2
    width = slots_ref.shape[1]
    count = jnp.zeros((1, 1), jnp.float32)
    lost = jnp.zeros((1, 1), jnp.float32)
    for g in range(owners):
        sums = [0.0, 0.0, 0.0, 0.0]
        for p in range(poles):
            piece = recv_ref[p * owners + g].astype(jnp.int32).astype(jnp.float32)
            extra = piece[cap + half :]
            scale = jnp.exp2(extra[:2] * (1.0 / FINE)) * (1.0 / STEPS)
            weight = extra[2:3] * 2.0**-13 + extra[3:4] * 2.0**-28
            energy = extra[4:5] * 2.0**-13 + extra[5:6] * 2.0**-28
            full = piece[:cap] * scale[:1]
            rest = piece[cap : cap + half] * scale[1:2]
            for at, term in enumerate(
                (weight * full, energy * full, weight * rest, energy * rest)
            ):
                sums[at] = sums[at] + term
            own = extra[6:7]
            own = (own[:, 1:2] * 2.0**-14 + own[:, 2:3] * 2.0**-29) * jnp.exp2(own[:, 0:1])
            grown = count + own
            part = grown - count
            lost = lost + ((count - (grown - part)) + (own - part))
            count = grown
        full_ref[g * cap : (g + 1) * cap, :LANES] = sums[0].astype(jnp.bfloat16)
        full_ref[g * cap : (g + 1) * cap, LANES:] = sums[1].astype(jnp.bfloat16)
        half_ref[g * half : (g + 1) * half, :LANES] = sums[2].astype(jnp.bfloat16)
        half_ref[g * half : (g + 1) * half, LANES:] = sums[3].astype(jnp.bfloat16)
    count_ref[0, 0] = jnp.sum(count + lost)

    slot = slots_ref[:1, :]
    pick = (lax.broadcasted_iota(jnp.int32, (owners * cap, width), 0) == slot).astype(jnp.bfloat16)
    row = lax.broadcasted_iota(jnp.int32, (owners * half, width), 0)
    owner = slot // cap
    within = slot - owner * cap
    place = owner * half + within
    left = (row == jnp.where(within < half, place, -1)).astype(jnp.bfloat16)
    right = (row == jnp.where(within >= half, place - half, -1)).astype(jnp.bfloat16)

    def take(held, chosen):
        return lax.dot_general(
            held, chosen, (((0,), (0,)), ((), ())), preferred_element_type=jnp.float32
        )

    full = take(full_ref[...], pick)
    by_left = take(half_ref[...], left)
    by_right = take(half_ref[...], right)
    mid = LANES // 2
    odd = jnp.broadcast_to(slots_ref[1:2, :], (LANES + mid, width)) == 1
    for at, ref in ((0, dens_ref), (LANES, energy_ref)):
        wide = full[at : at + LANES]
        slim = by_left[at : at + mid] + by_right[at + mid : at + LANES]
        ref[...] = jnp.where(
            odd, jnp.concatenate([slim, wide], axis=0), jnp.concatenate([wide, slim], axis=0)
        ).astype(jnp.bfloat16)


def ring_order(count):
    return list(range(0, count, 2)) + list(range(1, count, 2))[::-1]


def ranks(own, order):
    same = own[:, None] == own[None, :]
    earlier = order[None, :] < order[:, None]
    return jnp.sum((same & earlier).astype(jnp.int32), axis=1)


def body(
    anc_inv,
    factor_cols,
    diag_inv,
    intersection,
    pole_w,
    pole_z,
    ancestors,
    counts,
    hpattern,
    siesta_of,
    supernode_of,
):
    width = diag_inv.shape[-1]
    local_rows, anc_rows = anc_inv.shape[1:]
    blk_count = ancestors.shape[1]
    grid_count = lax.axis_size("grid")
    pole_count = lax.axis_size("pole")
    chunk = (blk_count + 1) * width // pole_count
    slot_cap = (width + grid_count - 1) // grid_count
    direct = (
        slot_cap * grid_count == width and slot_cap % 32 == 0 and chunk == LANES * 3 // 2
    )
    slots = slot_cap + (0 if direct else SUB if slot_cap % SUB == 0 else 1)

    dest_owner = siesta_of // width
    send_slot = dest_owner * slots + ranks(dest_owner, jnp.arange(width))
    source_dev = supernode_of // width
    recv_slot = source_dev * slots + ranks(source_dev, supernode_of)

    spread = grid_count * SUB
    if local_rows % spread == 0 and width % spread == 0:
        shares, ring = grid_count, ring_order(grid_count)
        stretches = local_rows // spread
        sent = pl.pallas_call(
            pack_kernel,
            out_shape=VMEM((grid_count, SUB, stretches * anc_rows + LANES), jnp.bfloat16),
            in_specs=[hspec(), hspec()],
            scratch_shapes=[
                SMEM(ancestors.shape, jnp.int32),
                pltpu.SemaphoreType.DMA((stretches,)),
            ],
            name="pack",
        )(ancestors, anc_inv[0].reshape(stretches, grid_count, SUB, anc_rows))
        held = lax.all_to_all(
            sent, "grid", split_axis=0, concat_axis=0, axis_index_groups=[ring], tiled=True
        )
        rows = width // grid_count
        chosen = pl.pallas_call(
            functools.partial(select_kernel, width, blk_count, stretches),
            out_shape=jax.ShapeDtypeStruct(
                (grid_count, blk_count * rows, blk_count * width), jnp.bfloat16
            ),
            in_specs=[vspec()],
            out_specs=hspec(),
            scratch_shapes=[pltpu.SemaphoreType.DMA(())],
            name="select",
        )(invmem(held))
        sub_block = lax.all_to_all(
            chosen, "grid", split_axis=0, concat_axis=0, axis_index_groups=[ring], tiled=True
        )
    else:
        shares = 1
        gathered = lax.all_gather(anc_inv[0], "grid", axis=0, tiled=True)
        blocks = gathered.reshape(anc_rows // width, width, anc_rows // width, width)
        sub_block = jnp.take(jnp.take(blocks, ancestors[0], axis=0), ancestors[0], axis=2)
    sub_block = sub_block.reshape(blk_count * width, blk_count * width)

    if direct:
        odd = (lax.axis_index("pole") & 1).astype(jnp.int32)[None]
        lower, turned, diag, inter, info, pickup_slots = pl.pallas_call(
            order_kernel,
            out_shape=(
                VMEM((blk_count * width, width), jnp.bfloat16),
                VMEM((width, blk_count * width), jnp.bfloat16),
                VMEM((width, width), jnp.bfloat16),
                VMEM((width, width), jnp.bfloat16),
                VMEM((SUB, (blk_count + 1) * width), jnp.float32),
                VMEM((SUB, width), jnp.int32),
            ),
            in_specs=[sspec()] * 5 + [vspec()] * 5,
            name="order",
        )(
            counts,
            hpattern,
            pole_w,
            pole_z,
            odd,
            send_slot[None],
            recv_slot[None],
            factor_cols[0, 0],
            diag_inv[0, 0],
            intersection[0],
        )
        rows = slot_cap * 3 // 2 + SUB
        coded = pl.pallas_call(
            functools.partial(encode_kernel, shares, chunk),
            out_shape=VMEM((pole_count * grid_count, rows, LANES), jnp.int16),
            in_specs=[vspec()] * 6,
            scratch_shapes=[VMEM((blk_count * width, blk_count * width), jnp.float32)],
            name="encode",
        )(*map(invmem, (sub_block, lower, turned, diag, inter, info)))
        arrived = lax.all_to_all(
            coded, ("pole", "grid"), split_axis=0, concat_axis=0, tiled=True
        )
        half = jax.ShapeDtypeStruct((chunk, width), jnp.bfloat16)
        density, energy, electrons = pl.pallas_call(
            functools.partial(decode_kernel, grid_count, slot_cap),
            out_shape=(half, half, jax.ShapeDtypeStruct((1, 1), jnp.float32)),
            in_specs=[vspec(), vspec()],
            out_specs=(vspec(), vspec(), sspec()),
            scratch_shapes=[
                VMEM((width, 2 * LANES), jnp.bfloat16),
                VMEM((width // 2, 2 * LANES), jnp.bfloat16),
            ],
            name="decode",
        )(invmem(pickup_slots), invmem(arrived))
        return (density.T, energy.T, electrons[0, 0])

    stack = pl.pallas_call(
        functools.partial(columns_kernel, shares, chunk),
        out_shape=jax.ShapeDtypeStruct((pole_count, chunk + SUB, width), jnp.float32),
        in_specs=[sspec()] * 4 + [vspec()] * 4,
        out_specs=vspec(),
        scratch_shapes=[VMEM((blk_count * width, width), jnp.float32)],
        name="columns",
    )(
        counts,
        hpattern,
        pole_w,
        pole_z,
        invmem(sub_block),
        factor_cols[0, 0],
        diag_inv[0, 0],
        intersection[0],
    )
    stack = lax.all_to_all(stack, "pole", split_axis=0, concat_axis=0, tiled=True)

    total = grid_count * slots
    placed = pl.pallas_call(
        functools.partial(place_kernel, slot_cap, grid_count),
        out_shape=jax.ShapeDtypeStruct((total, 2 * chunk), jnp.bfloat16),
        in_specs=[vspec(), vspec()],
        out_specs=vspec(),
        name="place",
    )(send_slot[None], invmem(stack))
    arrived = lax.all_to_all(
        placed.reshape(grid_count, slots, 2 * chunk),
        "grid",
        split_axis=0,
        concat_axis=0,
        tiled=True,
    )
    density, energy, electrons = pl.pallas_call(
        functools.partial(pickup_kernel, slot_cap, grid_count),
        out_shape=(
            jax.ShapeDtypeStruct((chunk, width), jnp.bfloat16),
            jax.ShapeDtypeStruct((chunk, width), jnp.bfloat16),
            jax.ShapeDtypeStruct((1, 1), jnp.float32),
        ),
        in_specs=[vspec(), vspec()],
        out_specs=(vspec(), vspec(), sspec()),
        name="pickup",
    )(recv_slot[None], invmem(arrived.reshape(total, 2 * chunk)))
    return (density.T, energy.T, electrons[0, 0])


def solution(mesh):
    placed = (
        P("pole", "grid", None),
        P("pole", "grid", None, None, None),
        P("pole", "grid", None, None),
        P("grid", None, None),
        P("pole"),
        P("pole"),
        P("grid", None),
        P("grid"),
        P("grid", None),
        P("grid"),
        P("grid"),
    )
    return jax.shard_map(
        body,
        mesh=mesh,
        in_specs=placed,
        out_specs=(P("grid", "pole"), P("grid", "pole"), P()),
        check_vma=False,
    )
```

```python
import functools

import jax
import jax.numpy as jnp
from jax import lax
from jax.experimental import pallas as pl
from jax.experimental.pallas import tpu as pltpu
from jax.sharding import PartitionSpec as P

VMEM = pltpu.VMEM
SMEM = pltpu.SMEM
LANES = 128
SUB = 8
TINY = 1e-30
FINE = 64.0
STEPS = 32760.0


def invmem(x):
    return pltpu.with_memory_space_constraint(x, VMEM)


def vspec():
    return pl.BlockSpec(memory_space=VMEM)


def hspec():
    return pl.BlockSpec(memory_space=pltpu.HBM)


def sspec():
    return pl.BlockSpec(memory_space=SMEM)


def pack_kernel(table_hbm, rows_ref, out_ref, table_ref, sems):
    stretches, shares, rows, width = rows_ref.shape
    copies = [
        pltpu.make_async_copy(
            rows_ref.at[c], out_ref.at[:, :, c * width : (c + 1) * width], sems.at[c]
        )
        for c in range(stretches)
    ]
    for copy in copies:
        copy.start()
    pltpu.sync_copy(table_hbm, table_ref)
    lane = lax.broadcasted_iota(jnp.int32, (rows, LANES), 1)
    table = jnp.zeros((rows, LANES), jnp.float32)
    for m in range(table_ref.shape[1]):
        table = jnp.where(lane == m, table_ref[0, m].astype(jnp.float32), table)
    table = table.astype(jnp.bfloat16)
    for s in range(shares):
        out_ref[s, :, stretches * width :] = table
    for copy in copies:
        copy.wait()


def select_kernel(width, blk_count, stretches, held_ref, out_ref, sem):
    dests, picked, _ = out_ref.shape
    tail = held_ref.shape[2] - LANES
    per_blk = picked // blk_count // SUB
    lane = lax.broadcasted_iota(jnp.int32, (1, LANES), 1)
    tables = []
    for s in range(dests):
        entry = held_ref[s, :, tail:].astype(jnp.float32)[:1]
        tables.append(
            [jnp.sum(jnp.where(lane == m, entry, 0.0)).astype(jnp.int32) for m in range(blk_count)]
        )
    long = tail // stretches
    for s, table in enumerate(tables):
        for m in range(blk_count):
            for k in range(per_blk):
                stretch = table[m] * per_blk + k
                device = stretch // stretches
                start = (stretch - device * stretches) * long
                back = device // 2
                place = jnp.where(device == 2 * back, back, dests - 1 - back)
                at = (m * per_blk + k) * SUB
                for n in range(blk_count):
                    col_at = pl.multiple_of(start + table[n] * width, LANES)
                    pltpu.make_async_copy(
                        held_ref.at[place, :, pl.ds(col_at, width)],
                        out_ref.at[s, at : at + SUB, n * width : (n + 1) * width],
                        sem,
                    ).start()
    pltpu.make_async_copy(out_ref, out_ref, sem).wait()


def columns_kernel(
    shares,
    chunk,
    counts_ref,
    hpattern_ref,
    weight_ref,
    energy_ref,
    rows_ref,
    factor_ref,
    diag_ref,
    inter_ref,
    out_ref,
    off_ref,
):
    blk_count, width, _ = factor_ref.shape
    parts = [
        factor_ref[m] * (m < counts_ref[0]).astype(jnp.float32).astype(jnp.bfloat16)
        for m in range(blk_count)
    ]
    lower = jnp.concatenate(parts, axis=0)
    product = jnp.dot(rows_ref[...], lower, preferred_element_type=jnp.float32)
    per_blk = width // shares
    for m in range(blk_count):
        scale = hpattern_ref[0, m].astype(jnp.float32)
        for j in range(shares):
            for c in range(per_blk // SUB):
                at = (j * blk_count + m) * per_blk + c * SUB
                piece = -product[at : at + SUB]
                row = m * width + (c * shares + j) * SUB
                off_ref[row : row + SUB, :] = piece
                place = width + row
                out_ref[place // chunk, place % chunk : place % chunk + SUB, :] = piece * scale
    off = off_ref[...]
    high = off.astype(jnp.bfloat16)
    rest = off - high.astype(jnp.float32)
    mid = rest.astype(jnp.bfloat16)
    low = (rest - mid.astype(jnp.float32)).astype(jnp.bfloat16)
    contract = functools.partial(
        lax.dot_general,
        dimension_numbers=(((0,), (0,)), ((), ())),
        preferred_element_type=jnp.float32,
    )
    product_sum = contract(lower, low) + contract(lower, mid) + contract(lower, high)
    diag_block = diag_ref[...].astype(jnp.float32) - product_sum
    at = 0
    while at < width:
        size = min(chunk - at % chunk, width - at)
        out_ref[at // chunk, at % chunk : at % chunk + size, :] = diag_block[at : at + size]
        at += size
    count = weight_ref[0] * jnp.sum(diag_block * inter_ref[...].astype(jnp.float32))
    row_id = lax.broadcasted_iota(jnp.int32, (SUB, width), 0)
    extra = jnp.where(row_id == 0, weight_ref[0], jnp.where(row_id == 1, energy_ref[0], count))
    for q in range(out_ref.shape[0]):
        out_ref[q, chunk : chunk + SUB, :] = extra


def place_kernel(slot_cap, dests, slot_ref, stack_ref, out_ref):
    poles, rows, width = stack_ref.shape
    chunk = rows - SUB
    dens = jnp.zeros((chunk, width), jnp.float32)
    energy = jnp.zeros((chunk, width), jnp.float32)
    count = jnp.zeros((1, width), jnp.float32)
    for p in range(poles):
        term = stack_ref[p, :chunk, :]
        dens = dens + stack_ref[p, chunk : chunk + 1, :] * term
        energy = energy + stack_ref[p, chunk + 1 : chunk + 2, :] * term
        count = count + stack_ref[p, chunk + 2 : chunk + 3, :]
    both = jnp.concatenate([dens, energy], axis=0).astype(jnp.bfloat16)
    total, lanes = out_ref.shape
    slots = total // dests
    one_hot = (lax.broadcasted_iota(jnp.int32, (total, width), 0) == slot_ref[...]).astype(
        jnp.bfloat16
    )
    placed = lax.dot_general(
        one_hot, both, (((1,), (1,)), ((), ())), preferred_element_type=jnp.float32
    )
    own = count[:, 0:1]
    high = own.astype(jnp.bfloat16).astype(jnp.float32)
    rest = own - high
    mid = rest.astype(jnp.bfloat16).astype(jnp.float32)
    lane = lax.broadcasted_iota(jnp.int32, (1, lanes), 1)
    pieces = jnp.where(lane == 0, high, jnp.where(lane == 1, mid, rest - mid))
    pieces = jnp.where(lane < 3, pieces, 0.0)
    row = lax.broadcasted_iota(jnp.int32, (total, 1), 0)
    marked = functools.reduce(
        jnp.logical_or, [row == g * slots + slot_cap for g in range(dests)]
    )
    out_ref[...] = jnp.where(marked, pieces, placed).astype(jnp.bfloat16)


def pickup_kernel(slot_cap, dests, slot_ref, recv_ref, dens_ref, energy_ref, count_ref):
    total, lanes = recv_ref.shape
    slots = total // dests
    chunk = lanes // 2
    width = slot_ref.shape[1]
    recv = recv_ref[...]
    one_hot = (lax.broadcasted_iota(jnp.int32, (total, width), 0) == slot_ref[...]).astype(
        jnp.bfloat16
    )
    out = lax.dot_general(
        recv, one_hot, (((0,), (0,)), ((), ())), preferred_element_type=jnp.float32
    ).astype(jnp.bfloat16)
    dens_ref[...] = out[:chunk]
    energy_ref[...] = out[chunk:]
    row = lax.broadcasted_iota(jnp.int32, (total, 1), 0)
    marked = functools.reduce(
        jnp.logical_or, [row == g * slots + slot_cap for g in range(dests)]
    )
    pieces = jnp.where(marked, recv[:, :LANES].astype(jnp.float32), 0.0)
    count_ref[0, 0] = jnp.sum(pieces)


def order_kernel(
    counts_ref,
    hpattern_ref,
    weight_ref,
    energy_ref,
    odd_ref,
    send_ref,
    recv_ref,
    factor_ref,
    diag_ref,
    inter_ref,
    lower_ref,
    turned_ref,
    diag_out,
    inter_out,
    info_ref,
    slots_ref,
):
    blk_count, width, _ = factor_ref.shape
    one_hot = (lax.broadcasted_iota(jnp.int32, (width, width), 0) == send_ref[...]).astype(
        jnp.bfloat16
    )

    def turn(matrix):
        return lax.dot_general(
            one_hot, matrix, (((1,), (1,)), ((), ())), preferred_element_type=jnp.float32
        ).astype(jnp.bfloat16)

    for m in range(blk_count):
        live = (m < counts_ref[0]).astype(jnp.float32).astype(jnp.bfloat16)
        block = factor_ref[m] * live
        lower_ref[m * width : (m + 1) * width, :] = block
        turned_ref[:, m * width : (m + 1) * width] = turn(block)
    diag_out[...] = turn(diag_ref[...])
    inter_out[...] = turn(inter_ref[...])

    rows, lanes = info_ref.shape
    row_id = lax.broadcasted_iota(jnp.int32, (rows, lanes), 0)
    block = lax.broadcasted_iota(jnp.int32, (rows, lanes), 1) // width
    info = jnp.ones((rows, lanes), jnp.float32)
    for m in range(blk_count):
        info = jnp.where(block == m + 1, hpattern_ref[0, m].astype(jnp.float32), info)
    info = jnp.where(row_id == 1, weight_ref[0], info)
    for at, scalar in ((2, weight_ref[0]), (4, energy_ref[0])):
        grown = jnp.full((rows, lanes), scalar) * 2.0**13
        grown_high = jnp.floor(grown)
        info = jnp.where(row_id == at, grown_high, info)
        info = jnp.where(row_id == at + 1, (grown - grown_high) * 2.0**15, info)
    info_ref[...] = info
    row_id = lax.broadcasted_iota(jnp.int32, (SUB, width), 0)
    slots_ref[...] = jnp.where(row_id == 0, recv_ref[...], odd_ref[0])


def halved_sum(values):
    while values.shape[0] > SUB:
        half = values.shape[0] // 2
        values = values[:half] + values[half:]
    while values.shape[1] > LANES:
        half = values.shape[1] // 2
        values = values[:, :half] + values[:, half:]
    return jnp.sum(values)


def whole(value):
    return value.astype(jnp.int32).astype(jnp.int16)


def fold_half(tile, right):
    rows = tile.shape[0] // 2
    lane = lax.broadcasted_iota(jnp.int32, (rows, LANES), 1)
    top, bottom = tile[:rows], tile[rows:]
    if right:
        return jnp.where(lane < LANES // 2, pltpu.roll(top, LANES // 2, 1), bottom)
    return jnp.where(lane < LANES // 2, top, pltpu.roll(bottom, LANES // 2, 1))


def encode_kernel(
    shares,
    chunk,
    places,
    rows_ref,
    lower_ref,
    turned_ref,
    diag_ref,
    inter_ref,
    info_ref,
    out_ref,
    sorted_ref,
):
    depth, width = lower_ref.shape
    blk_count = depth // width
    per_blk = width // shares
    for m in range(blk_count):
        for j in range(shares):
            at = (j * blk_count + m) * per_blk
            piece = rows_ref[at : at + per_blk, :].astype(jnp.float32)
            for c in range(per_blk // SUB):
                row = m * width + (c * shares + j) * SUB
                sorted_ref[row : row + SUB, :] = piece[c * SUB : (c + 1) * SUB]
    off = -lax.dot_general(
        turned_ref[...],
        sorted_ref[...].astype(jnp.bfloat16),
        (((1,), (1,)), ((), ())),
        preferred_element_type=jnp.float32,
    )
    high = off.astype(jnp.bfloat16)
    rest = off - high.astype(jnp.float32)
    mid = rest.astype(jnp.bfloat16)
    low = (rest - mid.astype(jnp.float32)).astype(jnp.bfloat16)
    lower = lower_ref[...]
    diag = diag_ref[...].astype(jnp.float32) - (
        jnp.dot(low, lower, preferred_element_type=jnp.float32)
        + jnp.dot(mid, lower, preferred_element_type=jnp.float32)
        + jnp.dot(high, lower, preferred_element_type=jnp.float32)
    )
    count = halved_sum(diag * inter_ref[...].astype(jnp.float32))
    values = jnp.concatenate([diag, off * info_ref[:1, width:]], axis=1)
    largest = jnp.max(jnp.abs(values), axis=0, keepdims=True)
    level = jnp.ceil(jnp.log2(jnp.maximum(largest, TINY)) * FINE)
    codes = jnp.floor(values * (jnp.exp2(level * (-1.0 / FINE)) * STEPS) + 0.5)

    row_id = lax.broadcasted_iota(jnp.int32, (SUB, LANES), 0)
    lane_id = lax.broadcasted_iota(jnp.int32, (SUB, LANES), 1)
    full_count = info_ref[1:2, :LANES] * jnp.full((SUB, LANES), count)
    power = jnp.ceil(jnp.log2(jnp.maximum(jnp.abs(full_count), TINY)))
    scaled = full_count * jnp.exp2(-power) * 2.0**14
    scaled_high = jnp.floor(scaled)
    extra = jnp.where(
        lane_id == 0,
        power,
        jnp.where(lane_id == 1, scaled_high, jnp.floor((scaled - scaled_high) * 2.0**15)),
    )
    extra = jnp.where(row_id < 6, info_ref[:, :LANES], extra)

    dests, _, _ = out_ref.shape
    pole_count = values.shape[1] // chunk
    owners = dests // pole_count
    cap = width // owners
    half = cap // 2
    for q in range(pole_count):
        right = q % 2 == 1
        full_at = (q * chunk + LANES - 1) // LANES * LANES
        half_at = full_at - LANES if right else full_at + LANES
        level_half = level[:, half_at : half_at + LANES]
        lane = lax.broadcasted_iota(jnp.int32, (1, LANES), 1)
        other = pltpu.roll(jnp.broadcast_to(level_half, (SUB, LANES)), LANES // 2, 1)[:1]
        level_half = jnp.where((lane < LANES // 2) == (not right), level_half, other)
        tail = jnp.where(
            row_id == 0,
            level[:, full_at : full_at + LANES],
            jnp.where(row_id == 1, level_half, extra),
        )
        tail = whole(tail)
        for g in range(owners):
            rows = slice(g * cap, (g + 1) * cap)
            d = places[q * owners + g]
            out_ref[d, :cap, :] = whole(codes[rows, full_at : full_at + LANES])
            out_ref[d, cap : cap + half, :] = whole(
                fold_half(codes[rows, half_at : half_at + LANES], right)
            )
            out_ref[d, cap + half :, :] = tail


def decode_kernel(
    owners, cap, places, slots_ref, recv_ref, dens_ref, energy_ref, count_ref, full_ref, half_ref
):
    dests, rows, _ = recv_ref.shape
    poles = dests // owners
    half = cap // 2
    width = slots_ref.shape[1]
    count = jnp.zeros((1, 1), jnp.float32)
    lost = jnp.zeros((1, 1), jnp.float32)
    for g in range(owners):
        sums = [0.0, 0.0, 0.0, 0.0]
        for p in range(poles):
            piece = recv_ref[places[p * owners + g]].astype(jnp.int32).astype(jnp.float32)
            extra = piece[cap + half :]
            scale = jnp.exp2(extra[:2] * (1.0 / FINE)) * (1.0 / STEPS)
            weight = extra[2:3] * 2.0**-13 + extra[3:4] * 2.0**-28
            energy = extra[4:5] * 2.0**-13 + extra[5:6] * 2.0**-28
            full = piece[:cap] * scale[:1]
            rest = piece[cap : cap + half] * scale[1:2]
            for at, term in enumerate(
                (weight * full, energy * full, weight * rest, energy * rest)
            ):
                sums[at] = sums[at] + term
            own = extra[6:7]
            own = (own[:, 1:2] * 2.0**-14 + own[:, 2:3] * 2.0**-29) * jnp.exp2(own[:, 0:1])
            grown = count + own
            part = grown - count
            lost = lost + ((count - (grown - part)) + (own - part))
            count = grown
        full_ref[g * cap : (g + 1) * cap, :LANES] = sums[0].astype(jnp.bfloat16)
        full_ref[g * cap : (g + 1) * cap, LANES:] = sums[1].astype(jnp.bfloat16)
        half_ref[g * half : (g + 1) * half, :LANES] = sums[2].astype(jnp.bfloat16)
        half_ref[g * half : (g + 1) * half, LANES:] = sums[3].astype(jnp.bfloat16)
    count_ref[0, 0] = jnp.sum(count + lost)

    slot = slots_ref[:1, :]
    pick = (lax.broadcasted_iota(jnp.int32, (owners * cap, width), 0) == slot).astype(jnp.bfloat16)
    row = lax.broadcasted_iota(jnp.int32, (owners * half, width), 0)
    owner = slot // cap
    within = slot - owner * cap
    place = owner * half + within
    left = (row == jnp.where(within < half, place, -1)).astype(jnp.bfloat16)
    right = (row == jnp.where(within >= half, place - half, -1)).astype(jnp.bfloat16)

    def take(held, chosen):
        return lax.dot_general(
            held, chosen, (((0,), (0,)), ((), ())), preferred_element_type=jnp.float32
        )

    full = take(full_ref[...], pick)
    by_left = take(half_ref[...], left)
    by_right = take(half_ref[...], right)
    mid = LANES // 2
    odd = jnp.broadcast_to(slots_ref[1:2, :], (LANES + mid, width)) == 1
    for at, ref in ((0, dens_ref), (LANES, energy_ref)):
        wide = full[at : at + LANES]
        slim = by_left[at : at + mid] + by_right[at + mid : at + LANES]
        ref[...] = jnp.where(
            odd, jnp.concatenate([slim, wide], axis=0), jnp.concatenate([wide, slim], axis=0)
        ).astype(jnp.bfloat16)


def ring_order(count):
    return list(range(0, count, 2)) + list(range(1, count, 2))[::-1]


def ranks(own, order):
    same = own[:, None] == own[None, :]
    earlier = order[None, :] < order[:, None]
    return jnp.sum((same & earlier).astype(jnp.int32), axis=1)


def body(
    anc_inv,
    factor_cols,
    diag_inv,
    intersection,
    pole_w,
    pole_z,
    ancestors,
    counts,
    hpattern,
    siesta_of,
    supernode_of,
):
    width = diag_inv.shape[-1]
    local_rows, anc_rows = anc_inv.shape[1:]
    blk_count = ancestors.shape[1]
    grid_count = lax.axis_size("grid")
    pole_count = lax.axis_size("pole")
    chunk = (blk_count + 1) * width // pole_count
    slot_cap = (width + grid_count - 1) // grid_count
    direct = (
        slot_cap * grid_count == width and slot_cap % 32 == 0 and chunk == LANES * 3 // 2
    )
    slots = slot_cap + (0 if direct else SUB if slot_cap % SUB == 0 else 1)

    dest_owner = siesta_of // width
    send_slot = dest_owner * slots + ranks(dest_owner, jnp.arange(width))
    source_dev = supernode_of // width
    recv_slot = source_dev * slots + ranks(source_dev, supernode_of)

    spread = grid_count * SUB
    if local_rows % spread == 0 and width % spread == 0:
        shares, ring = grid_count, ring_order(grid_count)
        stretches = local_rows // spread
        sent = pl.pallas_call(
            pack_kernel,
            out_shape=VMEM((grid_count, SUB, stretches * anc_rows + LANES), jnp.bfloat16),
            in_specs=[hspec(), hspec()],
            scratch_shapes=[
                SMEM(ancestors.shape, jnp.int32),
                pltpu.SemaphoreType.DMA((stretches,)),
            ],
            name="pack",
        )(ancestors, anc_inv[0].reshape(stretches, grid_count, SUB, anc_rows))
        held = lax.all_to_all(
            sent, "grid", split_axis=0, concat_axis=0, axis_index_groups=[ring], tiled=True
        )
        rows = width // grid_count
        chosen = pl.pallas_call(
            functools.partial(select_kernel, width, blk_count, stretches),
            out_shape=jax.ShapeDtypeStruct(
                (grid_count, blk_count * rows, blk_count * width), jnp.bfloat16
            ),
            in_specs=[vspec()],
            out_specs=hspec(),
            scratch_shapes=[pltpu.SemaphoreType.DMA(())],
            name="select",
        )(invmem(held))
        sub_block = lax.all_to_all(
            chosen, "grid", split_axis=0, concat_axis=0, axis_index_groups=[ring], tiled=True
        )
    else:
        shares = 1
        gathered = lax.all_gather(anc_inv[0], "grid", axis=0, tiled=True)
        blocks = gathered.reshape(anc_rows // width, width, anc_rows // width, width)
        sub_block = jnp.take(jnp.take(blocks, ancestors[0], axis=0), ancestors[0], axis=2)
    sub_block = sub_block.reshape(blk_count * width, blk_count * width)

    if direct:
        odd = (lax.axis_index("pole") & 1).astype(jnp.int32)[None]
        lower, turned, diag, inter, info, pickup_slots = pl.pallas_call(
            order_kernel,
            out_shape=(
                VMEM((blk_count * width, width), jnp.bfloat16),
                VMEM((width, blk_count * width), jnp.bfloat16),
                VMEM((width, width), jnp.bfloat16),
                VMEM((width, width), jnp.bfloat16),
                VMEM((SUB, (blk_count + 1) * width), jnp.float32),
                VMEM((SUB, width), jnp.int32),
            ),
            in_specs=[sspec()] * 5 + [vspec()] * 5,
            name="order",
        )(
            counts,
            hpattern,
            pole_w,
            pole_z,
            odd,
            send_slot[None],
            recv_slot[None],
            factor_cols[0, 0],
            diag_inv[0, 0],
            intersection[0],
        )
        everyone = [
            p * grid_count + g for g in ring_order(grid_count) for p in ring_order(pole_count)
        ]
        places = {device: at for at, device in enumerate(everyone)}
        rows = slot_cap * 3 // 2 + SUB
        coded = pl.pallas_call(
            functools.partial(encode_kernel, shares, chunk, places),
            out_shape=VMEM((pole_count * grid_count, rows, LANES), jnp.int16),
            in_specs=[vspec()] * 6,
            scratch_shapes=[VMEM((blk_count * width, blk_count * width), jnp.float32)],
            name="encode",
        )(*map(invmem, (sub_block, lower, turned, diag, inter, info)))
        arrived = lax.all_to_all(
            coded,
            ("pole", "grid"),
            split_axis=0,
            concat_axis=0,
            axis_index_groups=[everyone],
            tiled=True,
        )
        half = jax.ShapeDtypeStruct((chunk, width), jnp.bfloat16)
        density, energy, electrons = pl.pallas_call(
            functools.partial(decode_kernel, grid_count, slot_cap, places),
            out_shape=(half, half, jax.ShapeDtypeStruct((1, 1), jnp.float32)),
            in_specs=[vspec(), vspec()],
            out_specs=(vspec(), vspec(), sspec()),
            scratch_shapes=[
                VMEM((width, 2 * LANES), jnp.bfloat16),
                VMEM((width // 2, 2 * LANES), jnp.bfloat16),
            ],
            name="decode",
        )(invmem(pickup_slots), invmem(arrived))
        return (density.T, energy.T, electrons[0, 0])

    stack = pl.pallas_call(
        functools.partial(columns_kernel, shares, chunk),
        out_shape=jax.ShapeDtypeStruct((pole_count, chunk + SUB, width), jnp.float32),
        in_specs=[sspec()] * 4 + [vspec()] * 4,
        out_specs=vspec(),
        scratch_shapes=[VMEM((blk_count * width, width), jnp.float32)],
        name="columns",
    )(
        counts,
        hpattern,
        pole_w,
        pole_z,
        invmem(sub_block),
        factor_cols[0, 0],
        diag_inv[0, 0],
        intersection[0],
    )
    stack = lax.all_to_all(stack, "pole", split_axis=0, concat_axis=0, tiled=True)

    total = grid_count * slots
    placed = pl.pallas_call(
        functools.partial(place_kernel, slot_cap, grid_count),
        out_shape=jax.ShapeDtypeStruct((total, 2 * chunk), jnp.bfloat16),
        in_specs=[vspec(), vspec()],
        out_specs=vspec(),
        name="place",
    )(send_slot[None], invmem(stack))
    arrived = lax.all_to_all(
        placed.reshape(grid_count, slots, 2 * chunk),
        "grid",
        split_axis=0,
        concat_axis=0,
        tiled=True,
    )
    density, energy, electrons = pl.pallas_call(
        functools.partial(pickup_kernel, slot_cap, grid_count),
        out_shape=(
            jax.ShapeDtypeStruct((chunk, width), jnp.bfloat16),
            jax.ShapeDtypeStruct((chunk, width), jnp.bfloat16),
            jax.ShapeDtypeStruct((1, 1), jnp.float32),
        ),
        in_specs=[vspec(), vspec()],
        out_specs=(vspec(), vspec(), sspec()),
        name="pickup",
    )(recv_slot[None], invmem(arrived.reshape(total, 2 * chunk)))
    return (density.T, energy.T, electrons[0, 0])


def solution(mesh):
    placed = (
        P("pole", "grid", None),
        P("pole", "grid", None, None, None),
        P("pole", "grid", None, None),
        P("grid", None, None),
        P("pole"),
        P("pole"),
        P("grid", None),
        P("grid"),
        P("grid", None),
        P("grid"),
        P("grid"),
    )
    return jax.shard_map(
        body,
        mesh=mesh,
        in_specs=placed,
        out_specs=(P("grid", "pole"), P("grid", "pole"), P()),
        check_vma=False,
    )
```

```python
import functools

import jax
import jax.numpy as jnp
from jax import lax
from jax.experimental import pallas as pl
from jax.experimental.pallas import tpu as pltpu
from jax.sharding import PartitionSpec as P

VMEM = pltpu.VMEM
SMEM = pltpu.SMEM
LANES = 128
SUB = 8
TINY = 1e-30
FINE = 64.0
STEPS = 32760.0


def invmem(x):
    return pltpu.with_memory_space_constraint(x, VMEM)


def vspec():
    return pl.BlockSpec(memory_space=VMEM)


def hspec():
    return pl.BlockSpec(memory_space=pltpu.HBM)


def sspec():
    return pl.BlockSpec(memory_space=SMEM)


def pack_kernel(table_hbm, rows_ref, out_ref, table_ref, sems):
    stretches, shares, rows, width = rows_ref.shape
    copies = [
        pltpu.make_async_copy(
            rows_ref.at[c], out_ref.at[:, :, c * width : (c + 1) * width], sems.at[c]
        )
        for c in range(stretches)
    ]
    for copy in copies:
        copy.start()
    pltpu.sync_copy(table_hbm, table_ref)
    lane = lax.broadcasted_iota(jnp.int32, (rows, LANES), 1)
    table = jnp.zeros((rows, LANES), jnp.float32)
    for m in range(table_ref.shape[1]):
        table = jnp.where(lane == m, table_ref[0, m].astype(jnp.float32), table)
    table = table.astype(jnp.bfloat16)
    for s in range(shares):
        out_ref[s, :, stretches * width :] = table
    for copy in copies:
        copy.wait()


def select_kernel(width, blk_count, stretches, held_ref, out_ref, sem):
    dests, picked, _ = out_ref.shape
    tail = held_ref.shape[2] - LANES
    per_blk = picked // blk_count // SUB
    tables = []
    for s in range(dests):
        entry = held_ref[s, :, tail:].astype(jnp.float32)
        tables.append([entry[0, m].astype(jnp.int32) for m in range(blk_count)])
    long = tail // stretches
    for s, table in enumerate(tables):
        for m in range(blk_count):
            for k in range(per_blk):
                stretch = table[m] * per_blk + k
                device = stretch // stretches
                start = (stretch - device * stretches) * long
                back = device // 2
                place = jnp.where(device == 2 * back, back, dests - 1 - back)
                at = (m * per_blk + k) * SUB
                for n in range(blk_count):
                    col_at = pl.multiple_of(start + table[n] * width, LANES)
                    pltpu.make_async_copy(
                        held_ref.at[place, :, pl.ds(col_at, width)],
                        out_ref.at[s, at : at + SUB, n * width : (n + 1) * width],
                        sem,
                    ).start()
    pltpu.make_async_copy(out_ref, out_ref, sem).wait()


def columns_kernel(
    shares,
    chunk,
    counts_ref,
    hpattern_ref,
    weight_ref,
    energy_ref,
    rows_ref,
    factor_ref,
    diag_ref,
    inter_ref,
    out_ref,
    off_ref,
):
    blk_count, width, _ = factor_ref.shape
    parts = [
        factor_ref[m] * (m < counts_ref[0]).astype(jnp.float32).astype(jnp.bfloat16)
        for m in range(blk_count)
    ]
    lower = jnp.concatenate(parts, axis=0)
    product = jnp.dot(rows_ref[...], lower, preferred_element_type=jnp.float32)
    per_blk = width // shares
    for m in range(blk_count):
        scale = hpattern_ref[0, m].astype(jnp.float32)
        for j in range(shares):
            for c in range(per_blk // SUB):
                at = (j * blk_count + m) * per_blk + c * SUB
                piece = -product[at : at + SUB]
                row = m * width + (c * shares + j) * SUB
                off_ref[row : row + SUB, :] = piece
                place = width + row
                out_ref[place // chunk, place % chunk : place % chunk + SUB, :] = piece * scale
    off = off_ref[...]
    high = off.astype(jnp.bfloat16)
    rest = off - high.astype(jnp.float32)
    mid = rest.astype(jnp.bfloat16)
    low = (rest - mid.astype(jnp.float32)).astype(jnp.bfloat16)
    contract = functools.partial(
        lax.dot_general,
        dimension_numbers=(((0,), (0,)), ((), ())),
        preferred_element_type=jnp.float32,
    )
    product_sum = contract(lower, low) + contract(lower, mid) + contract(lower, high)
    diag_block = diag_ref[...].astype(jnp.float32) - product_sum
    at = 0
    while at < width:
        size = min(chunk - at % chunk, width - at)
        out_ref[at // chunk, at % chunk : at % chunk + size, :] = diag_block[at : at + size]
        at += size
    count = weight_ref[0] * jnp.sum(diag_block * inter_ref[...].astype(jnp.float32))
    row_id = lax.broadcasted_iota(jnp.int32, (SUB, width), 0)
    extra = jnp.where(row_id == 0, weight_ref[0], jnp.where(row_id == 1, energy_ref[0], count))
    for q in range(out_ref.shape[0]):
        out_ref[q, chunk : chunk + SUB, :] = extra


def place_kernel(slot_cap, dests, slot_ref, stack_ref, out_ref):
    poles, rows, width = stack_ref.shape
    chunk = rows - SUB
    dens = jnp.zeros((chunk, width), jnp.float32)
    energy = jnp.zeros((chunk, width), jnp.float32)
    count = jnp.zeros((1, width), jnp.float32)
    for p in range(poles):
        term = stack_ref[p, :chunk, :]
        dens = dens + stack_ref[p, chunk : chunk + 1, :] * term
        energy = energy + stack_ref[p, chunk + 1 : chunk + 2, :] * term
        count = count + stack_ref[p, chunk + 2 : chunk + 3, :]
    both = jnp.concatenate([dens, energy], axis=0).astype(jnp.bfloat16)
    total, lanes = out_ref.shape
    slots = total // dests
    one_hot = (lax.broadcasted_iota(jnp.int32, (total, width), 0) == slot_ref[...]).astype(
        jnp.bfloat16
    )
    placed = lax.dot_general(
        one_hot, both, (((1,), (1,)), ((), ())), preferred_element_type=jnp.float32
    )
    own = count[:, 0:1]
    high = own.astype(jnp.bfloat16).astype(jnp.float32)
    rest = own - high
    mid = rest.astype(jnp.bfloat16).astype(jnp.float32)
    lane = lax.broadcasted_iota(jnp.int32, (1, lanes), 1)
    pieces = jnp.where(lane == 0, high, jnp.where(lane == 1, mid, rest - mid))
    pieces = jnp.where(lane < 3, pieces, 0.0)
    row = lax.broadcasted_iota(jnp.int32, (total, 1), 0)
    marked = functools.reduce(
        jnp.logical_or, [row == g * slots + slot_cap for g in range(dests)]
    )
    out_ref[...] = jnp.where(marked, pieces, placed).astype(jnp.bfloat16)


def pickup_kernel(slot_cap, dests, slot_ref, recv_ref, dens_ref, energy_ref, count_ref):
    total, lanes = recv_ref.shape
    slots = total // dests
    chunk = lanes // 2
    width = slot_ref.shape[1]
    recv = recv_ref[...]
    one_hot = (lax.broadcasted_iota(jnp.int32, (total, width), 0) == slot_ref[...]).astype(
        jnp.bfloat16
    )
    out = lax.dot_general(
        recv, one_hot, (((0,), (0,)), ((), ())), preferred_element_type=jnp.float32
    ).astype(jnp.bfloat16)
    dens_ref[...] = out[:chunk]
    energy_ref[...] = out[chunk:]
    row = lax.broadcasted_iota(jnp.int32, (total, 1), 0)
    marked = functools.reduce(
        jnp.logical_or, [row == g * slots + slot_cap for g in range(dests)]
    )
    pieces = jnp.where(marked, recv[:, :LANES].astype(jnp.float32), 0.0)
    count_ref[0, 0] = jnp.sum(pieces)


def order_kernel(
    counts_ref,
    hpattern_ref,
    weight_ref,
    energy_ref,
    odd_ref,
    send_ref,
    recv_ref,
    factor_ref,
    diag_ref,
    inter_ref,
    lower_ref,
    turned_ref,
    diag_out,
    inter_out,
    info_ref,
    slots_ref,
):
    blk_count, width, _ = factor_ref.shape
    one_hot = (lax.broadcasted_iota(jnp.int32, (width, width), 0) == send_ref[...]).astype(
        jnp.bfloat16
    )

    def turn(matrix):
        return lax.dot_general(
            one_hot, matrix, (((1,), (1,)), ((), ())), preferred_element_type=jnp.float32
        ).astype(jnp.bfloat16)

    for m in range(blk_count):
        live = (m < counts_ref[0]).astype(jnp.float32).astype(jnp.bfloat16)
        block = factor_ref[m] * live
        lower_ref[m * width : (m + 1) * width, :] = block
        turned_ref[:, m * width : (m + 1) * width] = turn(block)
    diag_out[...] = turn(diag_ref[...])
    inter_out[...] = turn(inter_ref[...])

    rows, lanes = info_ref.shape
    row_id = lax.broadcasted_iota(jnp.int32, (rows, lanes), 0)
    block = lax.broadcasted_iota(jnp.int32, (rows, lanes), 1) // width
    info = jnp.ones((rows, lanes), jnp.float32)
    for m in range(blk_count):
        info = jnp.where(block == m + 1, hpattern_ref[0, m].astype(jnp.float32), info)
    info = jnp.where(row_id == 1, weight_ref[0], info)
    for at, scalar in ((2, weight_ref[0]), (4, energy_ref[0])):
        grown = jnp.full((rows, lanes), scalar) * 2.0**13
        grown_high = jnp.floor(grown)
        info = jnp.where(row_id == at, grown_high, info)
        info = jnp.where(row_id == at + 1, (grown - grown_high) * 2.0**15, info)
    info_ref[...] = info
    row_id = lax.broadcasted_iota(jnp.int32, (SUB, width), 0)
    slots_ref[...] = jnp.where(row_id == 0, recv_ref[...], odd_ref[0])


def halved_sum(values):
    while values.shape[0] > SUB:
        half = values.shape[0] // 2
        values = values[:half] + values[half:]
    while values.shape[1] > LANES:
        half = values.shape[1] // 2
        values = values[:, :half] + values[:, half:]
    return jnp.sum(values)


def whole(value):
    return value.astype(jnp.int32).astype(jnp.int16)


def fold_half(tile, right):
    rows = tile.shape[0] // 2
    lane = lax.broadcasted_iota(jnp.int32, (rows, LANES), 1)
    top, bottom = tile[:rows], tile[rows:]
    if right:
        return jnp.where(lane < LANES // 2, pltpu.roll(top, LANES // 2, 1), bottom)
    return jnp.where(lane < LANES // 2, top, pltpu.roll(bottom, LANES // 2, 1))


def encode_kernel(
    shares,
    chunk,
    places,
    rows_ref,
    lower_ref,
    turned_ref,
    diag_ref,
    inter_ref,
    info_ref,
    out_ref,
    sorted_ref,
):
    depth, width = lower_ref.shape
    blk_count = depth // width
    per_blk = width // shares
    for m in range(blk_count):
        for j in range(shares):
            at = (j * blk_count + m) * per_blk
            piece = rows_ref[at : at + per_blk, :].astype(jnp.float32)
            for c in range(per_blk // SUB):
                row = m * width + (c * shares + j) * SUB
                sorted_ref[row : row + SUB, :] = piece[c * SUB : (c + 1) * SUB]
    off = -lax.dot_general(
        turned_ref[...],
        sorted_ref[...].astype(jnp.bfloat16),
        (((1,), (1,)), ((), ())),
        preferred_element_type=jnp.float32,
    )
    high = off.astype(jnp.bfloat16)
    rest = off - high.astype(jnp.float32)
    mid = rest.astype(jnp.bfloat16)
    low = (rest - mid.astype(jnp.float32)).astype(jnp.bfloat16)
    lower = lower_ref[...]
    diag = diag_ref[...].astype(jnp.float32) - (
        jnp.dot(low, lower, preferred_element_type=jnp.float32)
        + jnp.dot(mid, lower, preferred_element_type=jnp.float32)
        + jnp.dot(high, lower, preferred_element_type=jnp.float32)
    )
    count = halved_sum(diag * inter_ref[...].astype(jnp.float32))
    values = jnp.concatenate([diag, off * info_ref[:1, width:]], axis=1)
    largest = jnp.max(jnp.abs(values), axis=0, keepdims=True)
    level = jnp.ceil(jnp.log2(jnp.maximum(largest, TINY)) * FINE)
    codes = jnp.floor(values * (jnp.exp2(level * (-1.0 / FINE)) * STEPS) + 0.5)

    row_id = lax.broadcasted_iota(jnp.int32, (SUB, LANES), 0)
    lane_id = lax.broadcasted_iota(jnp.int32, (SUB, LANES), 1)
    full_count = info_ref[1:2, :LANES] * jnp.full((SUB, LANES), count)
    power = jnp.ceil(jnp.log2(jnp.maximum(jnp.abs(full_count), TINY)))
    scaled = full_count * jnp.exp2(-power) * 2.0**14
    scaled_high = jnp.floor(scaled)
    extra = jnp.where(
        lane_id == 0,
        power,
        jnp.where(lane_id == 1, scaled_high, jnp.floor((scaled - scaled_high) * 2.0**15)),
    )
    extra = jnp.where(row_id < 6, info_ref[:, :LANES], extra)

    dests, _, _ = out_ref.shape
    pole_count = values.shape[1] // chunk
    owners = dests // pole_count
    cap = width // owners
    half = cap // 2
    for q in range(pole_count):
        right = q % 2 == 1
        full_at = (q * chunk + LANES - 1) // LANES * LANES
        half_at = full_at - LANES if right else full_at + LANES
        level_half = level[:, half_at : half_at + LANES]
        lane = lax.broadcasted_iota(jnp.int32, (1, LANES), 1)
        other = pltpu.roll(jnp.broadcast_to(level_half, (SUB, LANES)), LANES // 2, 1)[:1]
        level_half = jnp.where((lane < LANES // 2) == (not right), level_half, other)
        tail = jnp.where(
            row_id == 0,
            level[:, full_at : full_at + LANES],
            jnp.where(row_id == 1, level_half, extra),
        )
        tail = whole(tail)
        for g in range(owners):
            rows = slice(g * cap, (g + 1) * cap)
            d = places[q * owners + g]
            out_ref[d, :cap, :] = whole(codes[rows, full_at : full_at + LANES])
            out_ref[d, cap : cap + half, :] = whole(
                fold_half(codes[rows, half_at : half_at + LANES], right)
            )
            out_ref[d, cap + half :, :] = tail


def decode_kernel(
    owners, cap, places, slots_ref, recv_ref, dens_ref, energy_ref, count_ref, full_ref, half_ref
):
    dests, rows, _ = recv_ref.shape
    poles = dests // owners
    half = cap // 2
    width = slots_ref.shape[1]
    count = jnp.zeros((1, 1), jnp.float32)
    lost = jnp.zeros((1, 1), jnp.float32)
    for g in range(owners):
        sums = [0.0, 0.0, 0.0, 0.0]
        for p in range(poles):
            piece = recv_ref[places[p * owners + g]].astype(jnp.int32).astype(jnp.float32)
            extra = piece[cap + half :]
            scale = jnp.exp2(extra[:2] * (1.0 / FINE)) * (1.0 / STEPS)
            weight = extra[2:3] * 2.0**-13 + extra[3:4] * 2.0**-28
            energy = extra[4:5] * 2.0**-13 + extra[5:6] * 2.0**-28
            full = piece[:cap] * scale[:1]
            rest = piece[cap : cap + half] * scale[1:2]
            for at, term in enumerate(
                (weight * full, energy * full, weight * rest, energy * rest)
            ):
                sums[at] = sums[at] + term
            own = extra[6:7]
            own = (own[:, 1:2] * 2.0**-14 + own[:, 2:3] * 2.0**-29) * jnp.exp2(own[:, 0:1])
            grown = count + own
            part = grown - count
            lost = lost + ((count - (grown - part)) + (own - part))
            count = grown
        full_ref[g * cap : (g + 1) * cap, :LANES] = sums[0].astype(jnp.bfloat16)
        full_ref[g * cap : (g + 1) * cap, LANES:] = sums[1].astype(jnp.bfloat16)
        half_ref[g * half : (g + 1) * half, :LANES] = sums[2].astype(jnp.bfloat16)
        half_ref[g * half : (g + 1) * half, LANES:] = sums[3].astype(jnp.bfloat16)
    count_ref[0, 0] = jnp.sum(count + lost)

    slot = slots_ref[:1, :]
    pick = (lax.broadcasted_iota(jnp.int32, (owners * cap, width), 0) == slot).astype(jnp.bfloat16)
    row = lax.broadcasted_iota(jnp.int32, (owners * half, width), 0)
    owner = slot // cap
    within = slot - owner * cap
    place = owner * half + within
    left = (row == jnp.where(within < half, place, -1)).astype(jnp.bfloat16)
    right = (row == jnp.where(within >= half, place - half, -1)).astype(jnp.bfloat16)

    def take(held, chosen):
        return lax.dot_general(
            held, chosen, (((0,), (0,)), ((), ())), preferred_element_type=jnp.float32
        )

    full = take(full_ref[...], pick)
    by_left = take(half_ref[...], left)
    by_right = take(half_ref[...], right)
    mid = LANES // 2
    odd = jnp.broadcast_to(slots_ref[1:2, :], (LANES + mid, width)) == 1
    for at, ref in ((0, dens_ref), (LANES, energy_ref)):
        wide = full[at : at + LANES]
        slim = by_left[at : at + mid] + by_right[at + mid : at + LANES]
        ref[...] = jnp.where(
            odd, jnp.concatenate([slim, wide], axis=0), jnp.concatenate([wide, slim], axis=0)
        ).astype(jnp.bfloat16)


def ring_order(count):
    return list(range(0, count, 2)) + list(range(1, count, 2))[::-1]


def ranks(own, order):
    same = own[:, None] == own[None, :]
    earlier = order[None, :] < order[:, None]
    return jnp.sum((same & earlier).astype(jnp.int32), axis=1)


def body(
    anc_inv,
    factor_cols,
    diag_inv,
    intersection,
    pole_w,
    pole_z,
    ancestors,
    counts,
    hpattern,
    siesta_of,
    supernode_of,
):
    width = diag_inv.shape[-1]
    local_rows, anc_rows = anc_inv.shape[1:]
    blk_count = ancestors.shape[1]
    grid_count = lax.axis_size("grid")
    pole_count = lax.axis_size("pole")
    chunk = (blk_count + 1) * width // pole_count
    slot_cap = (width + grid_count - 1) // grid_count
    direct = (
        slot_cap * grid_count == width and slot_cap % 32 == 0 and chunk == LANES * 3 // 2
    )
    slots = slot_cap + (0 if direct else SUB if slot_cap % SUB == 0 else 1)

    dest_owner = siesta_of // width
    send_slot = dest_owner * slots + ranks(dest_owner, jnp.arange(width))
    source_dev = supernode_of // width
    recv_slot = source_dev * slots + ranks(source_dev, supernode_of)

    spread = grid_count * SUB
    if local_rows % spread == 0 and width % spread == 0:
        shares, ring = grid_count, ring_order(grid_count)
        stretches = local_rows // spread
        sent = pl.pallas_call(
            pack_kernel,
            out_shape=VMEM((grid_count, SUB, stretches * anc_rows + LANES), jnp.bfloat16),
            in_specs=[hspec(), hspec()],
            scratch_shapes=[
                SMEM(ancestors.shape, jnp.int32),
                pltpu.SemaphoreType.DMA((stretches,)),
            ],
            name="pack",
        )(ancestors, anc_inv[0].reshape(stretches, grid_count, SUB, anc_rows))
        held = lax.all_to_all(
            sent, "grid", split_axis=0, concat_axis=0, axis_index_groups=[ring], tiled=True
        )
        rows = width // grid_count
        chosen = pl.pallas_call(
            functools.partial(select_kernel, width, blk_count, stretches),
            out_shape=jax.ShapeDtypeStruct(
                (grid_count, blk_count * rows, blk_count * width), jnp.bfloat16
            ),
            in_specs=[vspec()],
            out_specs=hspec(),
            scratch_shapes=[pltpu.SemaphoreType.DMA(())],
            name="select",
        )(invmem(held))
        sub_block = lax.all_to_all(
            chosen, "grid", split_axis=0, concat_axis=0, axis_index_groups=[ring], tiled=True
        )
    else:
        shares = 1
        gathered = lax.all_gather(anc_inv[0], "grid", axis=0, tiled=True)
        blocks = gathered.reshape(anc_rows // width, width, anc_rows // width, width)
        sub_block = jnp.take(jnp.take(blocks, ancestors[0], axis=0), ancestors[0], axis=2)
    sub_block = sub_block.reshape(blk_count * width, blk_count * width)

    if direct:
        odd = (lax.axis_index("pole") & 1).astype(jnp.int32)[None]
        lower, turned, diag, inter, info, pickup_slots = pl.pallas_call(
            order_kernel,
            out_shape=(
                VMEM((blk_count * width, width), jnp.bfloat16),
                VMEM((width, blk_count * width), jnp.bfloat16),
                VMEM((width, width), jnp.bfloat16),
                VMEM((width, width), jnp.bfloat16),
                VMEM((SUB, (blk_count + 1) * width), jnp.float32),
                VMEM((SUB, width), jnp.int32),
            ),
            in_specs=[sspec()] * 5 + [vspec()] * 5,
            name="order",
        )(
            counts,
            hpattern,
            pole_w,
            pole_z,
            odd,
            send_slot[None],
            recv_slot[None],
            factor_cols[0, 0],
            diag_inv[0, 0],
            intersection[0],
        )
        everyone = [
            p * grid_count + g for g in ring_order(grid_count) for p in ring_order(pole_count)
        ]
        places = {device: at for at, device in enumerate(everyone)}
        rows = slot_cap * 3 // 2 + SUB
        coded = pl.pallas_call(
            functools.partial(encode_kernel, shares, chunk, places),
            out_shape=VMEM((pole_count * grid_count, rows, LANES), jnp.int16),
            in_specs=[vspec()] * 6,
            scratch_shapes=[VMEM((blk_count * width, blk_count * width), jnp.float32)],
            name="encode",
        )(*map(invmem, (sub_block, lower, turned, diag, inter, info)))
        arrived = lax.all_to_all(
            coded,
            ("pole", "grid"),
            split_axis=0,
            concat_axis=0,
            axis_index_groups=[everyone],
            tiled=True,
        )
        half = jax.ShapeDtypeStruct((chunk, width), jnp.bfloat16)
        density, energy, electrons = pl.pallas_call(
            functools.partial(decode_kernel, grid_count, slot_cap, places),
            out_shape=(half, half, jax.ShapeDtypeStruct((1, 1), jnp.float32)),
            in_specs=[vspec(), vspec()],
            out_specs=(vspec(), vspec(), sspec()),
            scratch_shapes=[
                VMEM((width, 2 * LANES), jnp.bfloat16),
                VMEM((width // 2, 2 * LANES), jnp.bfloat16),
            ],
            name="decode",
        )(invmem(pickup_slots), invmem(arrived))
        return (density.T, energy.T, electrons[0, 0])

    stack = pl.pallas_call(
        functools.partial(columns_kernel, shares, chunk),
        out_shape=jax.ShapeDtypeStruct((pole_count, chunk + SUB, width), jnp.float32),
        in_specs=[sspec()] * 4 + [vspec()] * 4,
        out_specs=vspec(),
        scratch_shapes=[VMEM((blk_count * width, width), jnp.float32)],
        name="columns",
    )(
        counts,
        hpattern,
        pole_w,
        pole_z,
        invmem(sub_block),
        factor_cols[0, 0],
        diag_inv[0, 0],
        intersection[0],
    )
    stack = lax.all_to_all(stack, "pole", split_axis=0, concat_axis=0, tiled=True)

    total = grid_count * slots
    placed = pl.pallas_call(
        functools.partial(place_kernel, slot_cap, grid_count),
        out_shape=jax.ShapeDtypeStruct((total, 2 * chunk), jnp.bfloat16),
        in_specs=[vspec(), vspec()],
        out_specs=vspec(),
        name="place",
    )(send_slot[None], invmem(stack))
    arrived = lax.all_to_all(
        placed.reshape(grid_count, slots, 2 * chunk),
        "grid",
        split_axis=0,
        concat_axis=0,
        tiled=True,
    )
    density, energy, electrons = pl.pallas_call(
        functools.partial(pickup_kernel, slot_cap, grid_count),
        out_shape=(
            jax.ShapeDtypeStruct((chunk, width), jnp.bfloat16),
            jax.ShapeDtypeStruct((chunk, width), jnp.bfloat16),
            jax.ShapeDtypeStruct((1, 1), jnp.float32),
        ),
        in_specs=[vspec(), vspec()],
        out_specs=(vspec(), vspec(), sspec()),
        name="pickup",
    )(recv_slot[None], invmem(arrived.reshape(total, 2 * chunk)))
    return (density.T, energy.T, electrons[0, 0])


def solution(mesh):
    placed = (
        P("pole", "grid", None),
        P("pole", "grid", None, None, None),
        P("pole", "grid", None, None),
        P("grid", None, None),
        P("pole"),
        P("pole"),
        P("grid", None),
        P("grid"),
        P("grid", None),
        P("grid"),
        P("grid"),
    )
    return jax.shard_map(
        body,
        mesh=mesh,
        in_specs=placed,
        out_specs=(P("grid", "pole"), P("grid", "pole"), P()),
        check_vma=False,
    )
```

```python
import functools

import jax
import jax.numpy as jnp
from jax import lax
from jax.experimental import pallas as pl
from jax.experimental.pallas import tpu as pltpu
from jax.sharding import PartitionSpec as P

VMEM = pltpu.VMEM
SMEM = pltpu.SMEM
LANES = 128
SUB = 8
TINY = 1e-30
FINE = 64.0
STEPS = 32760.0


def invmem(x):
    return pltpu.with_memory_space_constraint(x, VMEM)


def vspec():
    return pl.BlockSpec(memory_space=VMEM)


def hspec():
    return pl.BlockSpec(memory_space=pltpu.HBM)


def sspec():
    return pl.BlockSpec(memory_space=SMEM)


def pack_kernel(table_hbm, rows_ref, out_ref, table_ref, sems):
    stretches, shares, rows, width = rows_ref.shape
    copies = [
        pltpu.make_async_copy(
            rows_ref.at[c], out_ref.at[:, :, c * width : (c + 1) * width], sems.at[c]
        )
        for c in range(stretches)
    ]
    entries = pltpu.make_async_copy(table_hbm, table_ref, sems.at[stretches])
    entries.start()
    for copy in copies:
        copy.start()
    entries.wait()
    lane = lax.broadcasted_iota(jnp.int32, (rows, LANES), 1)
    table = jnp.zeros((rows, LANES), jnp.float32)
    for m in range(table_ref.shape[1]):
        table = jnp.where(lane == m, table_ref[0, m].astype(jnp.float32), table)
    table = table.astype(jnp.bfloat16)
    for s in range(shares):
        out_ref[s, :, stretches * width :] = table
    for copy in copies:
        copy.wait()


def select_kernel(width, blk_count, stretches, held_ref, out_ref, sem):
    dests, picked, _ = out_ref.shape
    tail = held_ref.shape[2] - LANES
    per_blk = picked // blk_count // SUB
    tables = []
    for s in range(dests):
        entry = held_ref[s, :, tail:].astype(jnp.float32)
        tables.append([entry[0, m].astype(jnp.int32) for m in range(blk_count)])
    long = tail // stretches
    for s, table in enumerate(tables):
        for m in range(blk_count):
            for k in range(per_blk):
                stretch = table[m] * per_blk + k
                device = stretch // stretches
                start = (stretch - device * stretches) * long
                back = device // 2
                place = jnp.where(device == 2 * back, back, dests - 1 - back)
                at = (m * per_blk + k) * SUB
                for n in range(blk_count):
                    col_at = pl.multiple_of(start + table[n] * width, LANES)
                    pltpu.make_async_copy(
                        held_ref.at[place, :, pl.ds(col_at, width)],
                        out_ref.at[s, at : at + SUB, n * width : (n + 1) * width],
                        sem,
                    ).start()
    pltpu.make_async_copy(out_ref, out_ref, sem).wait()


def columns_kernel(
    shares,
    chunk,
    counts_ref,
    hpattern_ref,
    weight_ref,
    energy_ref,
    rows_ref,
    factor_ref,
    diag_ref,
    inter_ref,
    out_ref,
    off_ref,
):
    blk_count, width, _ = factor_ref.shape
    parts = [
        factor_ref[m] * (m < counts_ref[0]).astype(jnp.float32).astype(jnp.bfloat16)
        for m in range(blk_count)
    ]
    lower = jnp.concatenate(parts, axis=0)
    product = jnp.dot(rows_ref[...], lower, preferred_element_type=jnp.float32)
    per_blk = width // shares
    for m in range(blk_count):
        scale = hpattern_ref[0, m].astype(jnp.float32)
        for j in range(shares):
            for c in range(per_blk // SUB):
                at = (j * blk_count + m) * per_blk + c * SUB
                piece = -product[at : at + SUB]
                row = m * width + (c * shares + j) * SUB
                off_ref[row : row + SUB, :] = piece
                place = width + row
                out_ref[place // chunk, place % chunk : place % chunk + SUB, :] = piece * scale
    off = off_ref[...]
    high = off.astype(jnp.bfloat16)
    rest = off - high.astype(jnp.float32)
    mid = rest.astype(jnp.bfloat16)
    low = (rest - mid.astype(jnp.float32)).astype(jnp.bfloat16)
    contract = functools.partial(
        lax.dot_general,
        dimension_numbers=(((0,), (0,)), ((), ())),
        preferred_element_type=jnp.float32,
    )
    product_sum = contract(lower, low) + contract(lower, mid) + contract(lower, high)
    diag_block = diag_ref[...].astype(jnp.float32) - product_sum
    at = 0
    while at < width:
        size = min(chunk - at % chunk, width - at)
        out_ref[at // chunk, at % chunk : at % chunk + size, :] = diag_block[at : at + size]
        at += size
    count = weight_ref[0] * jnp.sum(diag_block * inter_ref[...].astype(jnp.float32))
    row_id = lax.broadcasted_iota(jnp.int32, (SUB, width), 0)
    extra = jnp.where(row_id == 0, weight_ref[0], jnp.where(row_id == 1, energy_ref[0], count))
    for q in range(out_ref.shape[0]):
        out_ref[q, chunk : chunk + SUB, :] = extra


def place_kernel(slot_cap, dests, slot_ref, stack_ref, out_ref):
    poles, rows, width = stack_ref.shape
    chunk = rows - SUB
    dens = jnp.zeros((chunk, width), jnp.float32)
    energy = jnp.zeros((chunk, width), jnp.float32)
    count = jnp.zeros((1, width), jnp.float32)
    for p in range(poles):
        term = stack_ref[p, :chunk, :]
        dens = dens + stack_ref[p, chunk : chunk + 1, :] * term
        energy = energy + stack_ref[p, chunk + 1 : chunk + 2, :] * term
        count = count + stack_ref[p, chunk + 2 : chunk + 3, :]
    both = jnp.concatenate([dens, energy], axis=0).astype(jnp.bfloat16)
    total, lanes = out_ref.shape
    slots = total // dests
    one_hot = (lax.broadcasted_iota(jnp.int32, (total, width), 0) == slot_ref[...]).astype(
        jnp.bfloat16
    )
    placed = lax.dot_general(
        one_hot, both, (((1,), (1,)), ((), ())), preferred_element_type=jnp.float32
    )
    own = count[:, 0:1]
    high = own.astype(jnp.bfloat16).astype(jnp.float32)
    rest = own - high
    mid = rest.astype(jnp.bfloat16).astype(jnp.float32)
    lane = lax.broadcasted_iota(jnp.int32, (1, lanes), 1)
    pieces = jnp.where(lane == 0, high, jnp.where(lane == 1, mid, rest - mid))
    pieces = jnp.where(lane < 3, pieces, 0.0)
    row = lax.broadcasted_iota(jnp.int32, (total, 1), 0)
    marked = functools.reduce(
        jnp.logical_or, [row == g * slots + slot_cap for g in range(dests)]
    )
    out_ref[...] = jnp.where(marked, pieces, placed).astype(jnp.bfloat16)


def pickup_kernel(slot_cap, dests, slot_ref, recv_ref, dens_ref, energy_ref, count_ref):
    total, lanes = recv_ref.shape
    slots = total // dests
    chunk = lanes // 2
    width = slot_ref.shape[1]
    recv = recv_ref[...]
    one_hot = (lax.broadcasted_iota(jnp.int32, (total, width), 0) == slot_ref[...]).astype(
        jnp.bfloat16
    )
    out = lax.dot_general(
        recv, one_hot, (((0,), (0,)), ((), ())), preferred_element_type=jnp.float32
    ).astype(jnp.bfloat16)
    dens_ref[...] = out[:chunk]
    energy_ref[...] = out[chunk:]
    row = lax.broadcasted_iota(jnp.int32, (total, 1), 0)
    marked = functools.reduce(
        jnp.logical_or, [row == g * slots + slot_cap for g in range(dests)]
    )
    pieces = jnp.where(marked, recv[:, :LANES].astype(jnp.float32), 0.0)
    count_ref[0, 0] = jnp.sum(pieces)


def order_kernel(
    counts_ref,
    hpattern_ref,
    weight_ref,
    energy_ref,
    odd_ref,
    send_ref,
    recv_ref,
    factor_ref,
    diag_ref,
    inter_ref,
    lower_ref,
    turned_ref,
    diag_out,
    inter_out,
    info_ref,
    slots_ref,
):
    blk_count, width, _ = factor_ref.shape
    one_hot = (lax.broadcasted_iota(jnp.int32, (width, width), 0) == send_ref[...]).astype(
        jnp.bfloat16
    )

    def turn(matrix):
        return lax.dot_general(
            one_hot, matrix, (((1,), (1,)), ((), ())), preferred_element_type=jnp.float32
        ).astype(jnp.bfloat16)

    for m in range(blk_count):
        live = (m < counts_ref[0]).astype(jnp.float32).astype(jnp.bfloat16)
        block = factor_ref[m] * live
        lower_ref[m * width : (m + 1) * width, :] = block
        turned_ref[:, m * width : (m + 1) * width] = turn(block)
    diag_out[...] = turn(diag_ref[...])
    inter_out[...] = turn(inter_ref[...])

    rows, lanes = info_ref.shape
    row_id = lax.broadcasted_iota(jnp.int32, (rows, lanes), 0)
    block = lax.broadcasted_iota(jnp.int32, (rows, lanes), 1) // width
    info = jnp.ones((rows, lanes), jnp.float32)
    for m in range(blk_count):
        info = jnp.where(block == m + 1, hpattern_ref[0, m].astype(jnp.float32), info)
    info = jnp.where(row_id == 1, weight_ref[0], info)
    for at, scalar in ((2, weight_ref[0]), (4, energy_ref[0])):
        grown = jnp.full((rows, lanes), scalar) * 2.0**13
        grown_high = jnp.floor(grown)
        info = jnp.where(row_id == at, grown_high, info)
        info = jnp.where(row_id == at + 1, (grown - grown_high) * 2.0**15, info)
    info_ref[...] = info
    row_id = lax.broadcasted_iota(jnp.int32, (SUB, width), 0)
    slots_ref[...] = jnp.where(row_id == 0, recv_ref[...], odd_ref[0])


def halved_sum(values):
    while values.shape[0] > SUB:
        half = values.shape[0] // 2
        values = values[:half] + values[half:]
    while values.shape[1] > LANES:
        half = values.shape[1] // 2
        values = values[:, :half] + values[:, half:]
    return jnp.sum(values)


def whole(value):
    return value.astype(jnp.int32).astype(jnp.int16)


def fold_half(tile, right):
    rows = tile.shape[0] // 2
    lane = lax.broadcasted_iota(jnp.int32, (rows, LANES), 1)
    top, bottom = tile[:rows], tile[rows:]
    if right:
        return jnp.where(lane < LANES // 2, pltpu.roll(top, LANES // 2, 1), bottom)
    return jnp.where(lane < LANES // 2, top, pltpu.roll(bottom, LANES // 2, 1))


def encode_kernel(
    shares,
    chunk,
    places,
    rows_ref,
    lower_ref,
    turned_ref,
    diag_ref,
    inter_ref,
    info_ref,
    out_ref,
    sorted_ref,
):
    depth, width = lower_ref.shape
    blk_count = depth // width
    per_blk = width // shares
    for m in range(blk_count):
        for j in range(shares):
            at = (j * blk_count + m) * per_blk
            piece = rows_ref[at : at + per_blk, :].astype(jnp.float32)
            for c in range(per_blk // SUB):
                row = m * width + (c * shares + j) * SUB
                sorted_ref[row : row + SUB, :] = piece[c * SUB : (c + 1) * SUB]
    off = -lax.dot_general(
        turned_ref[...],
        sorted_ref[...].astype(jnp.bfloat16),
        (((1,), (1,)), ((), ())),
        preferred_element_type=jnp.float32,
    )
    high = off.astype(jnp.bfloat16)
    rest = off - high.astype(jnp.float32)
    mid = rest.astype(jnp.bfloat16)
    low = (rest - mid.astype(jnp.float32)).astype(jnp.bfloat16)
    lower = lower_ref[...]
    diag = diag_ref[...].astype(jnp.float32) - (
        jnp.dot(low, lower, preferred_element_type=jnp.float32)
        + jnp.dot(mid, lower, preferred_element_type=jnp.float32)
        + jnp.dot(high, lower, preferred_element_type=jnp.float32)
    )
    count = halved_sum(diag * inter_ref[...].astype(jnp.float32))
    values = jnp.concatenate([diag, off * info_ref[:1, width:]], axis=1)
    largest = jnp.max(jnp.abs(values), axis=0, keepdims=True)
    level = jnp.ceil(jnp.log2(jnp.maximum(largest, TINY)) * FINE)
    codes = jnp.floor(values * (jnp.exp2(level * (-1.0 / FINE)) * STEPS) + 0.5)

    row_id = lax.broadcasted_iota(jnp.int32, (SUB, LANES), 0)
    lane_id = lax.broadcasted_iota(jnp.int32, (SUB, LANES), 1)
    full_count = info_ref[1:2, :LANES] * jnp.full((SUB, LANES), count)
    power = jnp.ceil(jnp.log2(jnp.maximum(jnp.abs(full_count), TINY)))
    scaled = full_count * jnp.exp2(-power) * 2.0**14
    scaled_high = jnp.floor(scaled)
    extra = jnp.where(
        lane_id == 0,
        power,
        jnp.where(lane_id == 1, scaled_high, jnp.floor((scaled - scaled_high) * 2.0**15)),
    )
    extra = jnp.where(row_id < 6, info_ref[:, :LANES], extra)

    dests, _, _ = out_ref.shape
    pole_count = values.shape[1] // chunk
    owners = dests // pole_count
    cap = width // owners
    half = cap // 2
    for q in range(pole_count):
        right = q % 2 == 1
        full_at = (q * chunk + LANES - 1) // LANES * LANES
        half_at = full_at - LANES if right else full_at + LANES
        level_half = level[:, half_at : half_at + LANES]
        lane = lax.broadcasted_iota(jnp.int32, (1, LANES), 1)
        other = pltpu.roll(jnp.broadcast_to(level_half, (SUB, LANES)), LANES // 2, 1)[:1]
        level_half = jnp.where((lane < LANES // 2) == (not right), level_half, other)
        tail = jnp.where(
            row_id == 0,
            level[:, full_at : full_at + LANES],
            jnp.where(row_id == 1, level_half, extra),
        )
        tail = whole(tail)
        for g in range(owners):
            rows = slice(g * cap, (g + 1) * cap)
            d = places[q * owners + g]
            out_ref[d, :cap, :] = whole(codes[rows, full_at : full_at + LANES])
            out_ref[d, cap : cap + half, :] = whole(
                fold_half(codes[rows, half_at : half_at + LANES], right)
            )
            out_ref[d, cap + half :, :] = tail


def decode_kernel(
    owners, cap, places, slots_ref, recv_ref, dens_ref, energy_ref, count_ref, full_ref, half_ref
):
    dests, rows, _ = recv_ref.shape
    poles = dests // owners
    half = cap // 2
    width = slots_ref.shape[1]
    count = jnp.zeros((1, 1), jnp.float32)
    lost = jnp.zeros((1, 1), jnp.float32)
    for g in range(owners):
        sums = [0.0, 0.0, 0.0, 0.0]
        for p in range(poles):
            piece = recv_ref[places[p * owners + g]].astype(jnp.int32).astype(jnp.float32)
            extra = piece[cap + half :]
            scale = jnp.exp2(extra[:2] * (1.0 / FINE)) * (1.0 / STEPS)
            weight = extra[2:3] * 2.0**-13 + extra[3:4] * 2.0**-28
            energy = extra[4:5] * 2.0**-13 + extra[5:6] * 2.0**-28
            full = piece[:cap] * scale[:1]
            rest = piece[cap : cap + half] * scale[1:2]
            for at, term in enumerate(
                (weight * full, energy * full, weight * rest, energy * rest)
            ):
                sums[at] = sums[at] + term
            own = extra[6:7]
            own = (own[:, 1:2] * 2.0**-14 + own[:, 2:3] * 2.0**-29) * jnp.exp2(own[:, 0:1])
            grown = count + own
            part = grown - count
            lost = lost + ((count - (grown - part)) + (own - part))
            count = grown
        full_ref[g * cap : (g + 1) * cap, :LANES] = sums[0].astype(jnp.bfloat16)
        full_ref[g * cap : (g + 1) * cap, LANES:] = sums[1].astype(jnp.bfloat16)
        half_ref[g * half : (g + 1) * half, :LANES] = sums[2].astype(jnp.bfloat16)
        half_ref[g * half : (g + 1) * half, LANES:] = sums[3].astype(jnp.bfloat16)
    count_ref[0, 0] = jnp.sum(count + lost)

    slot = slots_ref[:1, :]
    pick = (lax.broadcasted_iota(jnp.int32, (owners * cap, width), 0) == slot).astype(jnp.bfloat16)
    row = lax.broadcasted_iota(jnp.int32, (owners * half, width), 0)
    owner = slot // cap
    within = slot - owner * cap
    place = owner * half + within
    left = (row == jnp.where(within < half, place, -1)).astype(jnp.bfloat16)
    right = (row == jnp.where(within >= half, place - half, -1)).astype(jnp.bfloat16)

    def take(held, chosen):
        return lax.dot_general(
            held, chosen, (((0,), (0,)), ((), ())), preferred_element_type=jnp.float32
        )

    full = take(full_ref[...], pick)
    by_left = take(half_ref[...], left)
    by_right = take(half_ref[...], right)
    mid = LANES // 2
    odd = jnp.broadcast_to(slots_ref[1:2, :], (LANES + mid, width)) == 1
    for at, ref in ((0, dens_ref), (LANES, energy_ref)):
        wide = full[at : at + LANES]
        slim = by_left[at : at + mid] + by_right[at + mid : at + LANES]
        ref[...] = jnp.where(
            odd, jnp.concatenate([slim, wide], axis=0), jnp.concatenate([wide, slim], axis=0)
        ).astype(jnp.bfloat16)


def ring_order(count):
    return list(range(0, count, 2)) + list(range(1, count, 2))[::-1]


def ranks(own, order):
    same = own[:, None] == own[None, :]
    earlier = order[None, :] < order[:, None]
    return jnp.sum((same & earlier).astype(jnp.int32), axis=1)


def body(
    anc_inv,
    factor_cols,
    diag_inv,
    intersection,
    pole_w,
    pole_z,
    ancestors,
    counts,
    hpattern,
    siesta_of,
    supernode_of,
):
    width = diag_inv.shape[-1]
    local_rows, anc_rows = anc_inv.shape[1:]
    blk_count = ancestors.shape[1]
    grid_count = lax.axis_size("grid")
    pole_count = lax.axis_size("pole")
    chunk = (blk_count + 1) * width // pole_count
    slot_cap = (width + grid_count - 1) // grid_count
    direct = (
        slot_cap * grid_count == width and slot_cap % 32 == 0 and chunk == LANES * 3 // 2
    )
    slots = slot_cap + (0 if direct else SUB if slot_cap % SUB == 0 else 1)

    dest_owner = siesta_of // width
    send_slot = dest_owner * slots + ranks(dest_owner, jnp.arange(width))
    source_dev = supernode_of // width
    recv_slot = source_dev * slots + ranks(source_dev, supernode_of)

    spread = grid_count * SUB
    if local_rows % spread == 0 and width % spread == 0:
        shares, ring = grid_count, ring_order(grid_count)
        stretches = local_rows // spread
        sent = pl.pallas_call(
            pack_kernel,
            out_shape=VMEM((grid_count, SUB, stretches * anc_rows + LANES), jnp.bfloat16),
            in_specs=[hspec(), hspec()],
            scratch_shapes=[
                SMEM(ancestors.shape, jnp.int32),
                pltpu.SemaphoreType.DMA((stretches + 1,)),
            ],
            name="pack",
        )(ancestors, anc_inv[0].reshape(stretches, grid_count, SUB, anc_rows))
        held = lax.all_to_all(
            sent, "grid", split_axis=0, concat_axis=0, axis_index_groups=[ring], tiled=True
        )
        rows = width // grid_count
        chosen = pl.pallas_call(
            functools.partial(select_kernel, width, blk_count, stretches),
            out_shape=jax.ShapeDtypeStruct(
                (grid_count, blk_count * rows, blk_count * width), jnp.bfloat16
            ),
            in_specs=[vspec()],
            out_specs=hspec(),
            scratch_shapes=[pltpu.SemaphoreType.DMA(())],
            name="select",
        )(invmem(held))
        sub_block = lax.all_to_all(
            chosen, "grid", split_axis=0, concat_axis=0, axis_index_groups=[ring], tiled=True
        )
    else:
        shares = 1
        gathered = lax.all_gather(anc_inv[0], "grid", axis=0, tiled=True)
        blocks = gathered.reshape(anc_rows // width, width, anc_rows // width, width)
        sub_block = jnp.take(jnp.take(blocks, ancestors[0], axis=0), ancestors[0], axis=2)
    sub_block = sub_block.reshape(blk_count * width, blk_count * width)

    if direct:
        odd = (lax.axis_index("pole") & 1).astype(jnp.int32)[None]
        lower, turned, diag, inter, info, pickup_slots = pl.pallas_call(
            order_kernel,
            out_shape=(
                VMEM((blk_count * width, width), jnp.bfloat16),
                VMEM((width, blk_count * width), jnp.bfloat16),
                VMEM((width, width), jnp.bfloat16),
                VMEM((width, width), jnp.bfloat16),
                VMEM((SUB, (blk_count + 1) * width), jnp.float32),
                VMEM((SUB, width), jnp.int32),
            ),
            in_specs=[sspec()] * 5 + [vspec()] * 5,
            name="order",
        )(
            counts,
            hpattern,
            pole_w,
            pole_z,
            odd,
            send_slot[None],
            recv_slot[None],
            factor_cols[0, 0],
            diag_inv[0, 0],
            intersection[0],
        )
        everyone = [
            p * grid_count + g for g in ring_order(grid_count) for p in ring_order(pole_count)
        ]
        places = {device: at for at, device in enumerate(everyone)}
        rows = slot_cap * 3 // 2 + SUB
        coded = pl.pallas_call(
            functools.partial(encode_kernel, shares, chunk, places),
            out_shape=VMEM((pole_count * grid_count, rows, LANES), jnp.int16),
            in_specs=[vspec()] * 6,
            scratch_shapes=[VMEM((blk_count * width, blk_count * width), jnp.float32)],
            name="encode",
        )(*map(invmem, (sub_block, lower, turned, diag, inter, info)))
        arrived = lax.all_to_all(
            coded,
            ("pole", "grid"),
            split_axis=0,
            concat_axis=0,
            axis_index_groups=[everyone],
            tiled=True,
        )
        half = jax.ShapeDtypeStruct((chunk, width), jnp.bfloat16)
        density, energy, electrons = pl.pallas_call(
            functools.partial(decode_kernel, grid_count, slot_cap, places),
            out_shape=(half, half, jax.ShapeDtypeStruct((1, 1), jnp.float32)),
            in_specs=[vspec(), vspec()],
            out_specs=(vspec(), vspec(), sspec()),
            scratch_shapes=[
                VMEM((width, 2 * LANES), jnp.bfloat16),
                VMEM((width // 2, 2 * LANES), jnp.bfloat16),
            ],
            name="decode",
        )(invmem(pickup_slots), invmem(arrived))
        return (density.T, energy.T, electrons[0, 0])

    stack = pl.pallas_call(
        functools.partial(columns_kernel, shares, chunk),
        out_shape=jax.ShapeDtypeStruct((pole_count, chunk + SUB, width), jnp.float32),
        in_specs=[sspec()] * 4 + [vspec()] * 4,
        out_specs=vspec(),
        scratch_shapes=[VMEM((blk_count * width, width), jnp.float32)],
        name="columns",
    )(
        counts,
        hpattern,
        pole_w,
        pole_z,
        invmem(sub_block),
        factor_cols[0, 0],
        diag_inv[0, 0],
        intersection[0],
    )
    stack = lax.all_to_all(stack, "pole", split_axis=0, concat_axis=0, tiled=True)

    total = grid_count * slots
    placed = pl.pallas_call(
        functools.partial(place_kernel, slot_cap, grid_count),
        out_shape=jax.ShapeDtypeStruct((total, 2 * chunk), jnp.bfloat16),
        in_specs=[vspec(), vspec()],
        out_specs=vspec(),
        name="place",
    )(send_slot[None], invmem(stack))
    arrived = lax.all_to_all(
        placed.reshape(grid_count, slots, 2 * chunk),
        "grid",
        split_axis=0,
        concat_axis=0,
        tiled=True,
    )
    density, energy, electrons = pl.pallas_call(
        functools.partial(pickup_kernel, slot_cap, grid_count),
        out_shape=(
            jax.ShapeDtypeStruct((chunk, width), jnp.bfloat16),
            jax.ShapeDtypeStruct((chunk, width), jnp.bfloat16),
            jax.ShapeDtypeStruct((1, 1), jnp.float32),
        ),
        in_specs=[vspec(), vspec()],
        out_specs=(vspec(), vspec(), sspec()),
        name="pickup",
    )(recv_slot[None], invmem(arrived.reshape(total, 2 * chunk)))
    return (density.T, energy.T, electrons[0, 0])


def solution(mesh):
    placed = (
        P("pole", "grid", None),
        P("pole", "grid", None, None, None),
        P("pole", "grid", None, None),
        P("grid", None, None),
        P("pole"),
        P("pole"),
        P("grid", None),
        P("grid"),
        P("grid", None),
        P("grid"),
        P("grid"),
    )
    return jax.shard_map(
        body,
        mesh=mesh,
        in_specs=placed,
        out_specs=(P("grid", "pole"), P("grid", "pole"), P()),
        check_vma=False,
    )
```
